256 devices in a mesh: rows: 64 (over y, z, core), feat: 4 (over x).
Axes of the slice: x: 4, y: 4, z: 8, core: 2. Of those that a mesh axis runs over, the one named last changes fastest.
Arguments:
- cells: bfloat16 [8192, 80, 128], P('rows', 'feat'), may hold values from -19 to 19
- block_table: int32 [64], replicated, may hold values from 0 to 7, as said below
- row_live: int32 [8192], replicated, may hold values from 0 to 1, as said below
- row_train: int32 [8192], replicated, may hold values from 0 to 1, as said below
- feat_qkv: bfloat16 [128, 384], replicated, may hold values from -0.5 to 0.5
- feat_out: bfloat16 [128, 128], replicated, may hold values from -0.5 to 0.5
- item_qkv: bfloat16 [128, 384], replicated, may hold values from -0.5 to 0.5
- item_out: bfloat16 [128, 128], replicated, may hold values from -0.5 to 0.5
Outputs:
- layer_output: bfloat16 [8192, 80, 128], P(('rows', 'feat'))
The draws below stay inside these ranges and needn't reach their ends.
Inputs may be any that keep to these rules, and one draw needn't show every extreme that they name: `block_table`: every table number appears in some block. `row_live`: every training row is live. `row_train`: each aligned group of 32 rows holds 1 to 4 training rows; some group holds exactly 4.
All inputs are finite; a program needn't handle non-finite values.
Results may differ from the reference program's by a relative error of at most 0.014.
Values may be sent and summed in bfloat16 or wider, within the bound.
A program may use at most 64 MiB of HBM per device.

```python
import jax
import jax.numpy as jnp
from jax import lax

F = 80
E = 128
HEADS = 4
HEAD_DIM = 32
BLOCK = 128
KEEP = 4
TABLES = 8
GROUP = 32
BLOCKS = 64
ROWS = 8192


def draw_cells(key, part):
    first_key, second_key, third_key, fourth_key = jax.random.split(jax.random.fold_in(key, 5), 4)
    base_part = jnp.clip(jax.random.normal(first_key, (ROWS, F, E), jnp.float32), -4.0, 4.0)
    log_scale = jax.random.uniform(second_key, (F,), jnp.float32, jnp.log(0.5), jnp.log(4.0))
    offsets = jax.random.uniform(third_key, (F,), jnp.float32, -2.0, 2.0)
    block_shift = 0.5 * jnp.clip(jax.random.normal(fourth_key, (ROWS // BLOCK, F, 1), jnp.float32), -2.0, 2.0)
    block_shift = jnp.repeat(block_shift, BLOCK, axis=0)
    cells_value = base_part * jnp.exp(log_scale)[None, :, None] + offsets[None, :, None] + block_shift
    return cells_value.astype(jnp.bfloat16)


def draw_block_table(key, part):
    count_blocks = ROWS // BLOCK
    first_key, second_key, third_key = jax.random.split(jax.random.fold_in(key, 3), 3)
    extra_count = count_blocks - TABLES
    low_pick = jnp.minimum(jax.random.randint(first_key, (extra_count,), 0, TABLES), jax.random.randint(second_key, (extra_count,), 0, TABLES))
    tables_all = jnp.concatenate([jnp.arange(TABLES, dtype=jnp.int32), low_pick.astype(jnp.int32)])
    return jax.random.permutation(third_key, tables_all).astype(jnp.int32)


def train_pattern(key):
    count_key, order_key = jax.random.split(jax.random.fold_in(key, 17))
    group_count = ROWS // GROUP
    counts = jax.random.randint(count_key, (group_count,), 1, KEEP + 1).astype(jnp.int32).at[0].set(KEEP)
    scores = jax.random.randint(order_key, (group_count, GROUP), 0, 1 << 20).astype(jnp.int32) * GROUP + jnp.arange(GROUP, dtype=jnp.int32)[None, :]
    ranks = jnp.argsort(jnp.argsort(scores, axis=1, stable=True), axis=1, stable=True)
    return (ranks < counts[:, None]).astype(jnp.int32).reshape(ROWS)


def draw_row_train(key, part):
    return train_pattern(key)


def draw_row_live(key, part):
    train_rows = train_pattern(key)
    chance = jax.random.randint(jax.random.fold_in(key, 29), (ROWS,), 0, 8)
    return jnp.maximum(train_rows, (chance < 7).astype(jnp.int32))


def bell_draw(key, dims, scale, bound, held_as=jnp.bfloat16):
    drawn = jax.random.normal(key, dims, jnp.float32) * scale
    return jnp.minimum(jnp.maximum(drawn, -bound), bound).astype(held_as)


def setup_inputs(seed: int = 0) -> dict:
    key_list = jax.random.split(jax.random.key(seed), 9)
    return {
        "cells": draw_cells(jax.random.fold_in(key_list[8], 71), 0),
        "block_table": draw_block_table(jax.random.fold_in(key_list[8], 71), 0),
        "row_live": draw_row_live(jax.random.fold_in(key_list[8], 71), 0),
        "row_train": draw_row_train(jax.random.fold_in(key_list[8], 71), 0),
        "feat_qkv": bell_draw(key_list[4], (E, 3 * E), E ** -0.5, 0.5),
        "feat_out": bell_draw(key_list[5], (E, E), E ** -0.5, 0.5),
        "item_qkv": bell_draw(key_list[6], (E, 3 * E), E ** -0.5, 0.5),
        "item_out": bell_draw(key_list[7], (E, E), E ** -0.5, 0.5),
    }


EPSILON = 1e-05
MASKED = -1e+30

def compact_train(train_rows):
    positions = jnp.arange(train_rows.shape[-1], dtype=jnp.int32)
    ordinal = (jnp.cumsum(train_rows, axis=-1) - 1).astype(jnp.int32)
    slot_ids = jnp.arange(KEEP, dtype=jnp.int32)
    matched = (train_rows[..., None, :] == 1) & (ordinal[..., None, :] == slot_ids[:, None])
    return lax.optimization_barrier(jnp.sum(jnp.where(matched, positions, 0), axis=-1)).astype(jnp.int32)

def feature_block(normed_block, feat_qkv, feat_out):
    row_count, feat_count, width_all = normed_block.shape
    projected = jnp.dot(normed_block, feat_qkv, preferred_element_type=jnp.float32).astype(jnp.bfloat16)
    head_shape = (row_count, feat_count, HEADS, HEAD_DIM)
    queries = projected[..., :width_all].reshape(head_shape).astype(jnp.float32)
    key_part = projected[..., width_all:2 * width_all].reshape(head_shape).astype(jnp.float32)
    value_part = projected[..., 2 * width_all:].reshape(head_shape).astype(jnp.float32)
    scores = jnp.einsum('rqhd,rkhd->rhqk', queries, key_part) * HEAD_DIM ** (-0.5)
    shares = jax.nn.softmax(scores, axis=-1).astype(jnp.bfloat16)
    attended = jnp.einsum('rhqk,rkhd->rqhd', shares.astype(jnp.float32), value_part).astype(jnp.bfloat16)
    attended = attended.reshape(row_count, feat_count, width_all)
    update = jnp.dot(attended, feat_out, preferred_element_type=jnp.float32)
    return (normed_block.astype(jnp.float32) + update).astype(jnp.bfloat16)

def reference(cells, block_table, row_live, row_train, feat_qkv, feat_out, item_qkv, item_out):
    row_table = jnp.repeat(block_table, BLOCK).astype(jnp.int32)
    table_ids = jnp.arange(TABLES, dtype=jnp.int32)
    table_hot = ((row_table[:, None] == table_ids[None, :]) & (row_live[:, None] == 1)).astype(jnp.float32)
    values = cells.astype(jnp.float32)
    count_sum = lax.optimization_barrier(jnp.sum(table_hot, axis=0)) * E
    first_sum = jnp.dot(table_hot.T, lax.optimization_barrier(jnp.sum(values, axis=2)), precision=lax.Precision.HIGHEST)
    table_mean = first_sum / count_sum[:, None]
    centred = values - table_mean[row_table][:, :, None]
    second_sum = jnp.dot(table_hot.T, lax.optimization_barrier(jnp.sum(centred * centred, axis=2)), precision=lax.Precision.HIGHEST)
    table_spread = second_sum / count_sum[:, None]
    normed = (centred * lax.rsqrt(table_spread[row_table] + EPSILON)[:, :, None]).astype(jnp.bfloat16)
    blocked = normed.reshape(BLOCKS, BLOCK, F, E)
    mixed_cells = lax.map(lambda block_cells: feature_block(block_cells, feat_qkv, feat_out), blocked)
    mixed_cells = mixed_cells.reshape(ROWS, F, E)
    group_count = ROWS // GROUP
    train_groups = row_train.reshape(group_count, GROUP)
    places = compact_train(train_groups)
    slot_ids = jnp.arange(KEEP, dtype=jnp.int32)
    key_valid = (slot_ids[None, :] < lax.optimization_barrier(jnp.sum(train_groups, axis=1)).astype(jnp.int32)[:, None]).reshape(-1)
    key_rows = (jnp.arange(group_count, dtype=jnp.int32)[:, None] * GROUP + places).reshape(-1)
    key_table = row_table[key_rows]
    chosen = mixed_cells[key_rows]
    queries = jnp.dot(mixed_cells, item_qkv[:, :E], preferred_element_type=jnp.float32).astype(jnp.bfloat16)
    key_value = jnp.dot(chosen, item_qkv[:, E:], preferred_element_type=jnp.float32).astype(jnp.bfloat16)
    queries = queries.reshape(ROWS, F, HEADS, HEAD_DIM)
    key_part = key_value[..., :E].reshape(-1, F, HEADS, HEAD_DIM)
    value_part = key_value[..., E:].reshape(-1, F, HEADS, HEAD_DIM)
    allowed = (row_table[:, None] == key_table[None, :]) & key_valid[None, :]

    def one_feature(feature_parts):
        feature_query, feature_key, feature_value = feature_parts
        scores = jnp.einsum('qhd,khd->hqk', feature_query.astype(jnp.float32), feature_key.astype(jnp.float32))
        scores = jnp.where(allowed[None], scores * HEAD_DIM ** (-0.5), MASKED)
        shares = jax.nn.softmax(scores, axis=-1).astype(jnp.bfloat16)
        return jnp.einsum('hqk,khd->qhd', shares.astype(jnp.float32), feature_value.astype(jnp.float32)).astype(jnp.bfloat16)
    attended = lax.map(one_feature, (jnp.moveaxis(queries, 1, 0), jnp.moveaxis(key_part, 1, 0), jnp.moveaxis(value_part, 1, 0)))
    attended = jnp.moveaxis(attended, 0, 1).reshape(ROWS, F, E)
    update = jnp.dot(attended, item_out, preferred_element_type=jnp.float32)
    return (mixed_cells.astype(jnp.float32) + update).astype(jnp.bfloat16)
```

```python
import jax
import jax.numpy as jnp
from jax import lax
from jax.experimental import pallas as pl
from jax.experimental.pallas import tpu as pltpu
from jax.sharding import PartitionSpec as P

HEADS = 4
HEAD_DIM = 32
WIDTH = 128
KEEP = 4
XS, YS, ZS, CS = 4, 4, 8, 2
BLOCKS = YS * ZS * CS
BLOCK = 128
FEATS = 80
SHARD = 20
OWNED = 5
GROUP = 32
OWNERS = XS * YS
PLACES = ZS * CS
KEYS = YS * XS * KEEP
TILE = 256
EPSILON = 1e-05
MASKED = -1e30
SCALE = HEAD_DIM**-0.5 * 1.4426950408889634
MESH = pl.DeviceIdType.MESH
F32 = jnp.float32
BF16 = jnp.bfloat16
VMEM = pl.BlockSpec(memory_space=pltpu.VMEM)
SMEM = pl.BlockSpec(memory_space=pltpu.SMEM)
ANY = pl.BlockSpec(memory_space=pl.ANY)


def iota(shape, dim):
    return lax.broadcasted_iota(jnp.int32, shape, dim)


def row_of(y, z, c):
    return y * (ZS * CS) + z * CS + c


def around(at, step, size):
    return lax.rem(at + step + size, size)


def remote(source, target, send, recv, row, feat):
    return pltpu.make_async_remote_copy(
        src_ref=source,
        dst_ref=target,
        send_sem=send,
        recv_sem=recv,
        device_id=(row, feat),
        device_id_type=MESH,
    )


def position():
    row = lax.axis_index("rows")
    x = lax.axis_index("feat")
    y = lax.div(row, ZS * CS)
    z = lax.rem(lax.div(row, CS), ZS)
    c = lax.rem(row, CS)
    return row, x, y, z, c


def mix_kernel(
    cells, table, live, train, wqkv, wout, q_out, kv_out,
    own, xbuf, st_src, sx, sy_src, sy, sz, nrm, qkv, att, mix, send,
    own_sem, xs, xr, ss, sr, ys, yr, zs, zr, qs, qr, rs, rr, ls, lr, ps, pr,
):
    row, x, y, z, c = position()
    owner = y * XS + x

    fetch = pltpu.make_async_copy(cells, own, own_sem.at[0])
    fetch.start()
    barrier = pltpu.get_barrier_semaphore()
    greet = []
    for dy in range(YS):
        for dx in range(XS):
            if dx or dy:
                greet.append((row_of(around(y, dy, YS), z, c), around(x, dx, XS)))
        greet.append((row_of(around(y, dy, YS), z, 1 - c), x))
    for dz in range(1, ZS):
        greet.append((row_of(y, around(z, dz, ZS), c), x))
    for peer in greet:
        pl.semaphore_signal(barrier, inc=1, device_id=peer, device_id_type=MESH)
    fetch.wait()

    base = row * BLOCK

    def add_first(r, carry):
        total, count = carry
        w = live[base + r]
        return total + w.astype(F32) * own[r].astype(F32), count + w

    total, count = lax.fori_loop(
        0, BLOCK, add_first, (jnp.zeros((SHARD, WIDTH), F32), jnp.int32(0)), unroll=8
    )
    first = jnp.sum(total, axis=1, keepdims=True)
    entries = jnp.full((SHARD, WIDTH), count.astype(F32) * WIDTH, F32)
    mean_here = jnp.broadcast_to(first, (SHARD, WIDTH)) / entries

    def add_second(r, total):
        off = own[r].astype(F32) - mean_here
        return total + live[base + r].astype(F32) * (off * off)

    second = jnp.sum(
        lax.fori_loop(0, BLOCK, add_second, jnp.zeros((SHARD, WIDTH), F32), unroll=8),
        axis=1,
        keepdims=True,
    )
    lane = iota((SHARD, WIDTH), 1)
    sub = iota((SHARD, WIDTH), 0)
    spot = lane == sub + GROUP * x

    def to_row(column):
        return jnp.sum(jnp.where(spot, column, 0.0), axis=0, keepdims=True)

    st_src[...] = jnp.concatenate(
        [to_row(first), to_row(second), to_row(entries), jnp.zeros((5, WIDTH), F32)], axis=0
    )
    pl.semaphore_wait(barrier, len(greet))

    stat_x = []
    for d in range(1, XS):
        copy = remote(st_src, sx.at[x], ss.at[d], sr.at[d], row, around(x, d, XS))
        copy.start()
        stat_x.append(copy)
    bulk = []
    for d in (1, 3, 2):
        to = around(x, d, XS)
        copy = remote(
            cells.at[pl.ds(to * GROUP, GROUP)], xbuf.at[x], xs.at[d], xr.at[d], row, to
        )
        copy.start()
        bulk.append((d, copy))
    keep = pltpu.make_async_copy(own.at[pl.ds(x * GROUP, GROUP)], xbuf.at[x], own_sem.at[1])
    keep.start()
    sx[x] = st_src[...]
    for d in range(1, XS):
        came = around(x, -d, XS)
        remote(st_src, sx.at[came], ss.at[d], sr.at[d], row, x).wait_recv()
    merged = sx[0] + sx[1] + sx[2] + sx[3]
    sy_src[...] = merged
    here = y * CS + c
    sy[here] = merged
    stat_y = []
    for dy in range(YS):
        for dc in range(CS):
            if dy or dc:
                k = dy * CS + dc
                to = row_of(around(y, dy, YS), z, around(c, dc, CS))
                copy = remote(sy_src, sy.at[here], ys.at[k], yr.at[k], to, x)
                copy.start()
                stat_y.append(copy)
    for dy in range(YS):
        for dc in range(CS):
            if dy or dc:
                k = dy * CS + dc
                came = around(y, -dy, YS) * CS + around(c, dc, CS)
                remote(sy_src, sy.at[came], ys.at[k], yr.at[k], row, x).wait_recv()
    stat_z = []
    for d in range(1, ZS):
        copy = remote(
            sy, sz.at[z], zs.at[d], zr.at[d], row_of(y, around(z, d, ZS), c), x
        )
        copy.start()
        stat_z.append(copy)
    sz[z] = sy[...]
    for d in range(1, ZS):
        came = around(z, -d, ZS)
        remote(sy, sz.at[came], zs.at[d], zr.at[d], row, x).wait_recv()

    mine = table[row]
    weights = []
    acc = jnp.zeros((8, WIDTH), F32)
    for zz in range(ZS):
        for yc in range(YS * CS):
            at = row_of(yc // CS, zz, yc % CS)
            w = jnp.where(table[at] == mine, 1.0, 0.0).astype(F32)
            weights.append(w)
            acc = acc + w * sz[zz, yc]
    entries_all = acc[2:3]
    mean_row = acc[0:1] / entries_all
    spread = jnp.zeros((1, WIDTH), F32)
    for zz in range(ZS):
        for yc in range(YS * CS):
            tile = sz[zz, yc]
            off = tile[0:1] / tile[2:3] - mean_row
            spread = spread + weights[zz * YS * CS + yc] * (tile[1:2] + tile[2:3] * (off * off))
    inv_row = lax.rsqrt(spread / entries_all + EPSILON)

    for _, copy in bulk:
        copy.wait_recv()
    keep.wait()
    for s in range(XS):
        pick = lane == sub + GROUP * s
        mean_col = jnp.broadcast_to(
            jnp.sum(jnp.where(pick, mean_row, 0.0), axis=1, keepdims=True), (SHARD, WIDTH)
        )
        inv_col = jnp.broadcast_to(
            jnp.sum(jnp.where(pick, inv_row, 0.0), axis=1, keepdims=True), (SHARD, WIDTH)
        )

        def norm(r, none, s=s, mean_col=mean_col, inv_col=inv_col):
            value = (xbuf[s, r].astype(F32) - mean_col) * inv_col
            nrm[r, SHARD * s : SHARD * (s + 1), :] = value.astype(BF16).astype(F32)
            return none

        lax.fori_loop(0, GROUP, norm, 0, unroll=4)

    def project(i, none):
        part = nrm[pl.ds(i * 4, 4)].reshape(4 * FEATS, WIDTH).astype(BF16)
        out = jnp.dot(part, wqkv[...], preferred_element_type=F32)
        qkv[pl.ds(i * 4, 4), :, 0:WIDTH] = (
            (out[:, :WIDTH] * SCALE).astype(BF16).reshape(4, FEATS, WIDTH)
        )
        qkv[pl.ds(i * 4, 4), :, WIDTH:] = (
            out[:, WIDTH:].astype(BF16).reshape(4, FEATS, 2 * WIDTH)
        )
        return none

    lax.fori_loop(0, GROUP // 4, project, 0)

    head = iota((FEATS, WIDTH), 1) // HEAD_DIM
    ones = jnp.ones((FEATS, WIDTH), BF16)

    def attend(r, none):
        query = qkv[r, :, 0:WIDTH]
        key = qkv[r, :, WIDTH : 2 * WIDTH]
        value = jnp.concatenate([qkv[r, :, 2 * WIDTH :], ones], axis=1)
        stacked = jnp.concatenate(
            [jnp.where(head == h, query, jnp.zeros_like(query)) for h in range(HEADS)], axis=0
        )
        scores = lax.dot_general(
            stacked, key, (((1,), (1,)), ((), ())), preferred_element_type=F32
        )
        top = jnp.max(scores, axis=1, keepdims=True)
        shares = jnp.exp2(scores - top).astype(BF16)
        out = jnp.dot(shares, value, preferred_element_type=F32)
        num = out[0:FEATS, :WIDTH]
        den = out[0:FEATS, WIDTH:]
        for h in range(1, HEADS):
            num = jnp.where(head == h, out[h * FEATS : (h + 1) * FEATS, :WIDTH], num)
            den = jnp.where(head == h, out[h * FEATS : (h + 1) * FEATS, WIDTH:], den)
        att[r] = (num / den).astype(BF16)
        return none

    lax.fori_loop(0, GROUP, attend, 0)

    def update(i, none):
        part = att[pl.ds(i * 4, 4)].reshape(4 * FEATS, WIDTH)
        out = jnp.dot(part, wout[...], preferred_element_type=F32)
        out = out + nrm[pl.ds(i * 4, 4)].reshape(4 * FEATS, WIDTH)
        mix[pl.ds(i * 4 * FEATS, 4 * FEATS), :] = out
        return none

    lax.fori_loop(0, GROUP // 4, update, 0)

    def turn(f, none):
        send[f] = mix[pl.ds(f, GROUP, stride=FEATS), :].astype(BF16)
        return none

    lax.fori_loop(0, FEATS, turn, 0, unroll=4)

    moved = []
    for dy in range(YS):
        for dx in range(XS):
            if dx or dy:
                k = dy * XS + dx
                ty, tx = around(y, dy, YS), around(x, dx, XS)
                copy = remote(
                    send.at[pl.ds((ty * XS + tx) * OWNED, OWNED)],
                    q_out.at[owner],
                    qs.at[k],
                    qr.at[k],
                    row_of(ty, z, c),
                    tx,
                )
                copy.start()
                moved.append(copy)
    q_out[owner] = send[pl.ds(owner * OWNED, OWNED)]
    lane = iota((BLOCK, BLOCK), 1)
    sub = iota((BLOCK, BLOCK), 0)
    lower = ((sub // GROUP == lane // GROUP) & (sub <= lane)).astype(F32).astype(BF16)
    place = iota((OWNERS, BLOCK), 0)
    along = iota((OWNERS, BLOCK), 1)
    picks = []
    for yy in range(YS):
        flags = jnp.broadcast_to(
            train[pl.ds(row_of(yy, z, c), 1), :].astype(F32), (OWNERS, BLOCK)
        )
        ordinal = jnp.dot(flags.astype(BF16), lower, preferred_element_type=F32)
        wanted = (place % KEEP + 1).astype(F32)
        hit = (flags > 0.5) & (ordinal == wanted) & (along // GROUP == place // KEEP)
        picks.append(hit.astype(F32).astype(BF16))
    for copy in moved:
        copy.wait_recv()

    spot_here = z * CS + c
    for yy in range(YS):
        for f in range(OWNED):
            rows = jnp.concatenate([q_out[yy * XS + xx, f] for xx in range(XS)], axis=0)
            kv_out[spot_here, f, yy * 16 : yy * 16 + 16, :] = jnp.dot(
                picks[yy], rows, preferred_element_type=F32
            ).astype(BF16)

    right, left = row_of(y, around(z, 1, ZS), c), row_of(y, around(z, -1, ZS), c)
    other = row_of(y, z, 1 - c)

    def slot(d):
        return around(z, d, ZS) * CS + c

    def over(d):
        k = d + 4
        copy = remote(kv_out.at[slot(d)], kv_out.at[slot(d)], ps.at[k], pr.at[k], other, x)
        copy.start()
        sent.append(copy)

    sent = []
    for k in range(4):
        copy = remote(kv_out.at[slot(-k)], kv_out.at[slot(-k)], rs.at[k], rr.at[k], right, x)
        copy.start()
        sent.append(copy)
        if k < 3:
            copy = remote(kv_out.at[slot(k)], kv_out.at[slot(k)], ls.at[k], lr.at[k], left, x)
            copy.start()
            sent.append(copy)
        if k == 0:
            over(0)
        came = kv_out.at[slot(-1 - k)]
        remote(came, came, rs.at[k], rr.at[k], right, x).wait_recv()
        over(-1 - k)
        if k < 3:
            came = kv_out.at[slot(1 + k)]
            remote(came, came, ls.at[k], lr.at[k], left, x).wait_recv()
            over(1 + k)
    for d in range(-4, 4):
        came = kv_out.at[around(z, d, ZS) * CS + 1 - c]
        remote(came, came, ps.at[d + 4], pr.at[d + 4], other, x).wait_recv()

    for copy in stat_x + [copy for _, copy in bulk] + stat_y + stat_z + moved + sent:
        copy.wait_send()


def item_kernel(q_in, kv_in, table, train, wqkv, wout, out, qp, kvp, kvc, bias):
    row, x, y, z, c = position()
    kvc[...] = jnp.zeros_like(kvc)

    def project_q(i, none):
        part = q_in[i].reshape(OWNED * GROUP, WIDTH)
        got = jnp.dot(part, wqkv[:, :WIDTH], preferred_element_type=F32)
        qp[i] = (got * SCALE).astype(BF16).reshape(OWNED, GROUP, WIDTH)
        return none

    lax.fori_loop(0, OWNERS, project_q, 0)

    def project_kv(i, none):
        part = kv_in[i].reshape(OWNED * KEYS, WIDTH)
        got = jnp.dot(part, wqkv[:, WIDTH:], preferred_element_type=F32)
        kvp[i] = got.astype(BF16).reshape(OWNED, KEYS, 2 * WIDTH)
        return none

    lax.fori_loop(0, PLACES, project_kv, 0)

    group = (iota((OWNERS, BLOCK), 1) // GROUP == iota((OWNERS, BLOCK), 0) // KEEP)
    counts = lax.dot_general(
        group.astype(F32).astype(BF16),
        train[...].astype(F32).astype(BF16),
        (((1,), (1,)), ((), ())),
        preferred_element_type=F32,
    )
    number = (iota((OWNERS, BLOCKS), 0) % KEEP).astype(F32)
    bias_all = jnp.where(number < counts, 0.0, MASKED)
    which = iota((OWNERS, BLOCKS), 1)
    head = iota((BLOCK, WIDTH), 1) // HEAD_DIM

    def one_block(yy, none):
        mine = table[row_of(yy, z, c)]

        def gather(j, n):
            hit = table[j] == mine

            @pl.when(hit)
            def _():
                at = pl.multiple_of(n * 16, 16)
                come = pl.multiple_of(lax.div(j, PLACES) * 16, 16)
                for f in range(OWNED):
                    kvc[f, pl.ds(at, 16), :] = kvp[lax.rem(j, PLACES), f, pl.ds(come, 16), :]
                column = jnp.sum(jnp.where(which == j, bias_all, 0.0), axis=1, keepdims=True)
                bias[pl.ds(at, 16), :] = jnp.broadcast_to(column, (16, WIDTH))

            return n + hit.astype(jnp.int32)

        n = lax.fori_loop(0, BLOCKS, gather, jnp.int32(0))
        tiles = lax.div(n + 15, 16)

        def tail(i, none):
            bias[pl.ds(pl.multiple_of(i * 16, 16), 16), :] = jnp.full((16, WIDTH), MASKED, F32)
            return none

        lax.fori_loop(n, tiles * 16, tail, 0)

        def one_feature(f, none):
            query = jnp.concatenate([qp[yy * XS + xx, f] for xx in range(XS)], axis=0)
            stacked = jnp.concatenate(
                [jnp.where(head == h, query, jnp.zeros_like(query)) for h in range(HEADS)],
                axis=0,
            )

            def one_tile(kt, carry):
                top, total, acc = carry
                at = pl.multiple_of(kt * TILE, TILE)
                key = kvc[f, pl.ds(at, TILE), 0:WIDTH]
                value = kvc[f, pl.ds(at, TILE), WIDTH:]
                scores = lax.dot_general(
                    key, stacked, (((1,), (1,)), ((), ())), preferred_element_type=F32
                )
                mask = bias[pl.ds(at, TILE), :]
                scores = scores + jnp.concatenate([mask] * HEADS, axis=1)
                new_top = jnp.maximum(top, jnp.max(scores, axis=0, keepdims=True))
                shares = jnp.exp2(scores - new_top)
                fade = jnp.exp2(top - new_top)
                total = total * fade + jnp.sum(shares, axis=0, keepdims=True)
                got = lax.dot_general(
                    value, shares.astype(BF16), (((0,), (0,)), ((), ())),
                    preferred_element_type=F32,
                )
                parts = []
                for h in range(HEADS):
                    rows = slice(h * HEAD_DIM, (h + 1) * HEAD_DIM)
                    cols = slice(h * BLOCK, (h + 1) * BLOCK)
                    parts.append(acc[rows] * fade[:, cols] + got[rows, cols])
                return new_top, total, jnp.concatenate(parts, axis=0)

            top, total, acc = lax.fori_loop(
                0,
                tiles,
                one_tile,
                (
                    jnp.full((1, HEADS * BLOCK), MASKED, F32),
                    jnp.zeros((1, HEADS * BLOCK), F32),
                    jnp.zeros((WIDTH, BLOCK), F32),
                ),
            )
            attended = jnp.concatenate(
                [
                    acc[h * HEAD_DIM : (h + 1) * HEAD_DIM] / total[:, h * BLOCK : (h + 1) * BLOCK]
                    for h in range(HEADS)
                ],
                axis=0,
            ).astype(BF16)
            got = lax.dot_general(
                attended, wout[...], (((0,), (0,)), ((), ())), preferred_element_type=F32
            )
            for xx in range(XS):
                mixed = q_in[yy * XS + xx, f].astype(F32)
                out[yy * XS + xx, f] = (mixed + got[xx * GROUP : (xx + 1) * GROUP]).astype(BF16)
            return none

        lax.fori_loop(0, OWNED, one_feature, 0)
        return none

    lax.fori_loop(0, YS, one_block, 0)


def back_kernel(done, out, send_sems, recv_sems):
    row, x, y, z, c = position()
    owner = y * XS + x
    barrier = pltpu.get_barrier_semaphore()
    for dy in range(YS):
        for dx in range(XS):
            if dx or dy:
                peer = (row_of(around(y, dy, YS), z, c), around(x, dx, XS))
                pl.semaphore_signal(barrier, inc=1, device_id=peer, device_id_type=MESH)
    pl.semaphore_wait(barrier, OWNERS - 1)
    sent = []
    for dy in range(YS):
        for dx in range(XS):
            if dx or dy:
                k = dy * XS + dx
                ty, tx = around(y, dy, YS), around(x, dx, XS)
                copy = remote(
                    done.at[ty * XS + tx],
                    out.at[owner],
                    send_sems.at[k],
                    recv_sems.at[k],
                    row_of(ty, z, c),
                    tx,
                )
                copy.start()
                sent.append(copy)
    out[owner] = done[owner]
    for copy in sent:
        copy.wait_recv()
    for copy in sent:
        copy.wait_send()


def turn_kernel(rows, out, wide):
    def widen(g, none):
        wide[pl.ds(pl.multiple_of(g * OWNED * GROUP, 32), OWNED * GROUP), :] = (
            rows[g].reshape(OWNED * GROUP, WIDTH).astype(F32)
        )
        return none

    lax.fori_loop(0, OWNERS, widen, 0)

    def turn(r, none):
        out[r] = wide[pl.ds(r, FEATS, stride=GROUP), :].astype(BF16)
        return none

    lax.fori_loop(0, GROUP, turn, 0, unroll=4)


def on_device(cells, block_table, row_live, row_train, feat_qkv, feat_out, item_qkv, item_out):
    train = row_train.reshape(BLOCKS, BLOCK)
    dma = pltpu.SemaphoreType.DMA
    moved = jax.ShapeDtypeStruct((OWNERS, OWNED, GROUP, WIDTH), BF16)
    query, key = pl.pallas_call(
        mix_kernel,
        name="mix",
        out_shape=(moved, jax.ShapeDtypeStruct((PLACES, OWNED, KEYS, WIDTH), BF16)),
        in_specs=[ANY, SMEM, SMEM, VMEM, VMEM, VMEM],
        out_specs=(VMEM, VMEM),
        scratch_shapes=[
            pltpu.VMEM((BLOCK, SHARD, WIDTH), BF16),
            pltpu.VMEM((XS, GROUP, SHARD, WIDTH), BF16),
            pltpu.VMEM((8, WIDTH), F32),
            pltpu.VMEM((XS, 8, WIDTH), F32),
            pltpu.VMEM((8, WIDTH), F32),
            pltpu.VMEM((YS * CS, 8, WIDTH), F32),
            pltpu.VMEM((ZS, YS * CS, 8, WIDTH), F32),
            pltpu.VMEM((GROUP, FEATS, WIDTH), F32),
            pltpu.VMEM((GROUP, FEATS, 3 * WIDTH), BF16),
            pltpu.VMEM((GROUP, FEATS, WIDTH), BF16),
            pltpu.VMEM((GROUP * FEATS, WIDTH), F32),
            pltpu.VMEM((FEATS, GROUP, WIDTH), BF16),
            dma((2,)),
            dma((XS,)), dma((XS,)), dma((XS,)), dma((XS,)),
            dma((8,)), dma((8,)), dma((8,)), dma((8,)),
            dma((OWNERS,)), dma((OWNERS,)),
            dma((4,)), dma((4,)), dma((4,)), dma((4,)), dma((8,)), dma((8,)),
        ],
        compiler_params=pltpu.CompilerParams(collective_id=0, has_side_effects=True),
    )(cells, block_table, row_live, train, feat_qkv, feat_out)
    done = pl.pallas_call(
        item_kernel,
        name="item",
        out_shape=moved,
        in_specs=[VMEM, VMEM, SMEM, VMEM, VMEM, VMEM],
        out_specs=VMEM,
        scratch_shapes=[
            pltpu.VMEM((OWNERS, OWNED, GROUP, WIDTH), BF16),
            pltpu.VMEM((PLACES, OWNED, KEYS, 2 * WIDTH), BF16),
            pltpu.VMEM((OWNED, PLACES * KEYS, 2 * WIDTH), BF16),
            pltpu.VMEM((PLACES * KEYS, WIDTH), F32),
        ],
    )(query, key, block_table, train, item_qkv, item_out)
    rows = pl.pallas_call(
        back_kernel,
        name="back",
        out_shape=moved,
        in_specs=[VMEM],
        out_specs=VMEM,
        scratch_shapes=[dma((OWNERS,)), dma((OWNERS,))],
        compiler_params=pltpu.CompilerParams(collective_id=1, has_side_effects=True),
    )(done)
    return pl.pallas_call(
        turn_kernel,
        name="turn",
        out_shape=jax.ShapeDtypeStruct((GROUP, FEATS, WIDTH), BF16),
        in_specs=[VMEM],
        out_specs=VMEM,
        scratch_shapes=[pltpu.VMEM((FEATS * GROUP, WIDTH), F32)],
    )(rows)


def solution(mesh):
    return jax.shard_map(
        on_device,
        mesh=mesh,
        in_specs=(P("rows", "feat", None), P(), P(), P(), P(), P(), P(), P()),
        out_specs=P(("rows", "feat"), None, None),
        check_vma=False,
    )
```

```python
import jax
import jax.numpy as jnp
from jax import lax
from jax.experimental import pallas as pl
from jax.experimental.pallas import tpu as pltpu
from jax.sharding import PartitionSpec as P

HEADS = 4
HEAD_DIM = 32
WIDTH = 128
KEEP = 4
XS, YS, ZS, CS = 4, 4, 8, 2
BLOCKS = YS * ZS * CS
BLOCK = 128
FEATS = 80
SHARD = 20
OWNED = 5
GROUP = 32
OWNERS = XS * YS
PLACES = ZS * CS
KEYS = YS * XS * KEEP
TILE = 256
EPSILON = 1e-05
MASKED = -1e30
SCALE = HEAD_DIM**-0.5 * 1.4426950408889634
MESH = pl.DeviceIdType.MESH
F32 = jnp.float32
BF16 = jnp.bfloat16
VMEM = pl.BlockSpec(memory_space=pltpu.VMEM)
SMEM = pl.BlockSpec(memory_space=pltpu.SMEM)
ANY = pl.BlockSpec(memory_space=pl.ANY)


def iota(shape, dim):
    return lax.broadcasted_iota(jnp.int32, shape, dim)


def row_of(y, z, c):
    return y * (ZS * CS) + z * CS + c


def around(at, step, size):
    return lax.rem(at + step + size, size)


def remote(source, target, send, recv, row, feat):
    return pltpu.make_async_remote_copy(
        src_ref=source,
        dst_ref=target,
        send_sem=send,
        recv_sem=recv,
        device_id=(row, feat),
        device_id_type=MESH,
    )


def position():
    row = lax.axis_index("rows")
    x = lax.axis_index("feat")
    y = lax.div(row, ZS * CS)
    z = lax.rem(lax.div(row, CS), ZS)
    c = lax.rem(row, CS)
    return row, x, y, z, c


def mix_kernel(
    cells, table, live, train, wqkv, wout, q_out, kv_out,
    own, xbuf, part, level, mean_of, inv_of, st_src, sx, sy_src, sy, sz, nrm, rows, qkv, att, mix, send,
    own_sem, xs, xr, ss, sr, ys, yr, zs, zr, qs, qr, rs, rr, ls, lr, ps, pr,
):
    row, x, y, z, c = position()
    owner = y * XS + x

    fetch = pltpu.make_async_copy(cells, own, own_sem.at[0])
    fetch.start()
    barrier = pltpu.get_barrier_semaphore()
    greet = []
    for dy in range(YS):
        for dx in range(XS):
            if dx or dy:
                greet.append((row_of(around(y, dy, YS), z, c), around(x, dx, XS)))
        greet.append((row_of(around(y, dy, YS), z, 1 - c), x))
    for dz in range(1, ZS):
        greet.append((row_of(y, around(z, dz, ZS), c), x))
    for peer in greet:
        pl.semaphore_signal(barrier, inc=1, device_id=peer, device_id_type=MESH)
    fetch.wait()

    square = iota((BLOCK, WIDTH), 0) == iota((BLOCK, WIDTH), 1)
    flags = live[pl.ds(row, 1), :].astype(F32)
    weight = jnp.broadcast_to(
        jnp.sum(jnp.where(square, flags, 0.0), axis=1, keepdims=True), (BLOCK, WIDTH)
    )
    entries = jnp.broadcast_to(jnp.sum(flags, axis=1, keepdims=True) * WIDTH, (SHARD, WIDTH))

    def add_first(f, none):
        part[pl.ds(f, 1), :] = jnp.sum(own[f].astype(F32) * weight, axis=0, keepdims=True)
        return none

    lax.fori_loop(0, SHARD, add_first, 0, unroll=4)
    first = jnp.sum(part[...], axis=1, keepdims=True)
    level[...] = jnp.broadcast_to(first, (SHARD, WIDTH)) / entries

    def add_second(f, none):
        off = own[f].astype(F32) - level[pl.ds(f, 1), :]
        part[pl.ds(f, 1), :] = jnp.sum(off * off * weight, axis=0, keepdims=True)
        return none

    lax.fori_loop(0, SHARD, add_second, 0, unroll=4)
    second = jnp.sum(part[...], axis=1, keepdims=True)
    lane = iota((SHARD, WIDTH), 1)
    sub = iota((SHARD, WIDTH), 0)
    spot = lane == sub + GROUP * x

    def to_row(column):
        return jnp.sum(jnp.where(spot, column, 0.0), axis=0, keepdims=True)

    st_src[...] = jnp.concatenate(
        [to_row(first), to_row(second), to_row(entries), jnp.zeros((5, WIDTH), F32)], axis=0
    )
    pl.semaphore_wait(barrier, len(greet))

    stat_x = []
    for d in range(1, XS):
        copy = remote(st_src, sx.at[x], ss.at[d], sr.at[d], row, around(x, d, XS))
        copy.start()
        stat_x.append(copy)
    bulk = []
    for d in (1, 3, 2):
        to = around(x, d, XS)
        copy = remote(
            cells.at[:, pl.ds(pl.multiple_of(to * GROUP, GROUP), GROUP)],
            xbuf.at[pl.ds(x * SHARD, SHARD)],
            xs.at[d],
            xr.at[d],
            row,
            to,
        )
        copy.start()
        bulk.append((d, copy))
    keep = pltpu.make_async_copy(
        own.at[:, pl.ds(pl.multiple_of(x * GROUP, GROUP), GROUP)],
        xbuf.at[pl.ds(x * SHARD, SHARD)],
        own_sem.at[1],
    )
    keep.start()
    sx[x] = st_src[...]
    for d in range(1, XS):
        came = around(x, -d, XS)
        remote(st_src, sx.at[came], ss.at[d], sr.at[d], row, x).wait_recv()
    merged = sx[0] + sx[1] + sx[2] + sx[3]
    sy_src[...] = merged
    here = y * CS + c
    sy[here] = merged
    stat_y = []
    for dy in range(YS):
        for dc in range(CS):
            if dy or dc:
                k = dy * CS + dc
                to = row_of(around(y, dy, YS), z, around(c, dc, CS))
                copy = remote(sy_src, sy.at[here], ys.at[k], yr.at[k], to, x)
                copy.start()
                stat_y.append(copy)
    for dy in range(YS):
        for dc in range(CS):
            if dy or dc:
                k = dy * CS + dc
                came = around(y, -dy, YS) * CS + around(c, dc, CS)
                remote(sy_src, sy.at[came], ys.at[k], yr.at[k], row, x).wait_recv()
    stat_z = []
    for d in range(1, ZS):
        copy = remote(
            sy, sz.at[z], zs.at[d], zr.at[d], row_of(y, around(z, d, ZS), c), x
        )
        copy.start()
        stat_z.append(copy)
    sz[z] = sy[...]
    for d in range(1, ZS):
        came = around(z, -d, ZS)
        remote(sy, sz.at[came], zs.at[d], zr.at[d], row, x).wait_recv()

    mine = table[row]
    weights = []
    acc = jnp.zeros((8, WIDTH), F32)
    for zz in range(ZS):
        for yc in range(YS * CS):
            at = row_of(yc // CS, zz, yc % CS)
            w = jnp.where(table[at] == mine, 1.0, 0.0).astype(F32)
            weights.append(w)
            acc = acc + w * sz[zz, yc]
    entries_all = acc[2:3]
    mean_row = acc[0:1] / entries_all
    spread = jnp.zeros((1, WIDTH), F32)
    for zz in range(ZS):
        for yc in range(YS * CS):
            tile = sz[zz, yc]
            off = tile[0:1] / tile[2:3] - mean_row
            spread = spread + weights[zz * YS * CS + yc] * (tile[1:2] + tile[2:3] * (off * off))
    inv_row = lax.rsqrt(spread / entries_all + EPSILON)

    for d, _ in bulk:
        came = xbuf.at[pl.ds(around(x, -d, XS) * SHARD, SHARD)]
        remote(came, came, xs.at[d], xr.at[d], row, x).wait_recv()
    keep.wait()
    for s in range(XS):
        pick = lane == sub + GROUP * s
        for ref, values in ((mean_of, mean_row), (inv_of, inv_row)):
            column = jnp.sum(jnp.where(pick, values, 0.0), axis=1, keepdims=True)
            ref[SHARD * s : SHARD * (s + 1), :] = jnp.broadcast_to(column, (SHARD, WIDTH))

    def norm(f, none):
        value = (xbuf[f].astype(F32) - mean_of[pl.ds(f, 1), :]) * inv_of[pl.ds(f, 1), :]
        nrm[pl.ds(pl.multiple_of(f * GROUP, GROUP), GROUP), :] = value.astype(BF16).astype(F32)
        return none

    lax.fori_loop(0, FEATS, norm, 0, unroll=4)

    def by_row(r, none):
        rows[r] = nrm[pl.ds(r, FEATS, stride=GROUP), :].astype(BF16)
        return none

    lax.fori_loop(0, GROUP, by_row, 0, unroll=4)

    def project(i, none):
        some = rows[pl.ds(i * 4, 4)].reshape(4 * FEATS, WIDTH)
        out = jnp.dot(some, wqkv[...], preferred_element_type=F32)
        qkv[pl.ds(i * 4, 4), :, 0:WIDTH] = (
            (out[:, :WIDTH] * SCALE).astype(BF16).reshape(4, FEATS, WIDTH)
        )
        qkv[pl.ds(i * 4, 4), :, WIDTH:] = (
            out[:, WIDTH:].astype(BF16).reshape(4, FEATS, 2 * WIDTH)
        )
        return none

    lax.fori_loop(0, GROUP // 4, project, 0)

    head = iota((FEATS, WIDTH), 1) // HEAD_DIM
    def attend(r, none):
        query = qkv[r, :, 0:WIDTH]
        key = qkv[r, :, WIDTH : 2 * WIDTH]
        value = qkv[r, :, 2 * WIDTH :]
        keys = jnp.concatenate(
            [jnp.where(head == h, key, jnp.zeros_like(key)) for h in range(HEADS)], axis=0
        )
        values = jnp.concatenate(
            [jnp.where(head == h, value, jnp.zeros_like(value)) for h in range(HEADS)], axis=0
        )
        scores = lax.dot_general(
            keys, query, (((1,), (1,)), ((), ())), preferred_element_type=F32
        )
        shares = []
        for h in range(HEADS):
            some = scores[h * FEATS : (h + 1) * FEATS]
            some = jnp.exp2(some - jnp.max(some, axis=0, keepdims=True))
            shares.append((some * (1.0 / jnp.sum(some, axis=0, keepdims=True))).astype(BF16))
        att[r] = lax.dot_general(
            jnp.concatenate(shares, axis=0),
            values,
            (((0,), (0,)), ((), ())),
            preferred_element_type=F32,
        ).astype(BF16)
        return none

    lax.fori_loop(0, GROUP, attend, 0, unroll=16)

    def update(i, none):
        some = att[pl.ds(i * 4, 4)].reshape(4 * FEATS, WIDTH)
        out = jnp.dot(some, wout[...], preferred_element_type=F32)
        out = out + rows[pl.ds(i * 4, 4)].reshape(4 * FEATS, WIDTH).astype(F32)
        mix[pl.ds(i * 4 * FEATS, 4 * FEATS), :] = out
        return none

    lax.fori_loop(0, GROUP // 4, update, 0)

    def turn(f, none):
        send[f] = mix[pl.ds(f, GROUP, stride=FEATS), :].astype(BF16)
        return none

    lax.fori_loop(0, FEATS, turn, 0, unroll=4)

    moved = []
    for dy in range(YS):
        for dx in range(XS):
            if dx or dy:
                k = dy * XS + dx
                ty, tx = around(y, dy, YS), around(x, dx, XS)
                copy = remote(
                    send.at[pl.ds((ty * XS + tx) * OWNED, OWNED)],
                    q_out.at[owner],
                    qs.at[k],
                    qr.at[k],
                    row_of(ty, z, c),
                    tx,
                )
                copy.start()
                moved.append(copy)
    q_out[owner] = send[pl.ds(owner * OWNED, OWNED)]
    lane = iota((BLOCK, BLOCK), 1)
    sub = iota((BLOCK, BLOCK), 0)
    lower = ((sub // GROUP == lane // GROUP) & (sub <= lane)).astype(F32).astype(BF16)
    place = iota((OWNERS, BLOCK), 0)
    along = iota((OWNERS, BLOCK), 1)
    picks = []
    for yy in range(YS):
        flags = jnp.broadcast_to(
            train[pl.ds(row_of(yy, z, c), 1), :].astype(F32), (OWNERS, BLOCK)
        )
        ordinal = jnp.dot(flags.astype(BF16), lower, preferred_element_type=F32)
        wanted = (place % KEEP + 1).astype(F32)
        hit = (flags > 0.5) & (ordinal == wanted) & (along // GROUP == place // KEEP)
        picks.append(hit.astype(F32).astype(BF16))
    for copy in moved:
        copy.wait_recv()

    spot_here = z * CS + c
    for yy in range(YS):
        for f in range(OWNED):
            found = jnp.concatenate([q_out[yy * XS + xx, f] for xx in range(XS)], axis=0)
            kv_out[spot_here, f, yy * 16 : yy * 16 + 16, :] = jnp.dot(
                picks[yy], found, preferred_element_type=F32
            ).astype(BF16)

    right, left = row_of(y, around(z, 1, ZS), c), row_of(y, around(z, -1, ZS), c)
    other = row_of(y, z, 1 - c)

    def slot(d):
        return around(z, d, ZS) * CS + c

    def over(d):
        k = d + 4
        copy = remote(kv_out.at[slot(d)], kv_out.at[slot(d)], ps.at[k], pr.at[k], other, x)
        copy.start()
        sent.append(copy)

    sent = []
    for k in range(4):
        copy = remote(kv_out.at[slot(-k)], kv_out.at[slot(-k)], rs.at[k], rr.at[k], right, x)
        copy.start()
        sent.append(copy)
        if k < 3:
            copy = remote(kv_out.at[slot(k)], kv_out.at[slot(k)], ls.at[k], lr.at[k], left, x)
            copy.start()
            sent.append(copy)
        if k == 0:
            over(0)
        came = kv_out.at[slot(-1 - k)]
        remote(came, came, rs.at[k], rr.at[k], right, x).wait_recv()
        over(-1 - k)
        if k < 3:
            came = kv_out.at[slot(1 + k)]
            remote(came, came, ls.at[k], lr.at[k], left, x).wait_recv()
            over(1 + k)
    for d in range(-4, 4):
        came = kv_out.at[around(z, d, ZS) * CS + 1 - c]
        remote(came, came, ps.at[d + 4], pr.at[d + 4], other, x).wait_recv()

    for copy in stat_x + [copy for _, copy in bulk] + stat_y + stat_z + moved + sent:
        copy.wait_send()


def item_kernel(q_in, kv_in, table, train, wqkv, wout, out, qp, kvp, kvc, bias):
    row, x, y, z, c = position()
    kvc[...] = jnp.zeros_like(kvc)

    def project_q(i, none):
        part = q_in[i].reshape(OWNED * GROUP, WIDTH)
        got = jnp.dot(part, wqkv[:, :WIDTH], preferred_element_type=F32)
        qp[i] = (got * SCALE).astype(BF16).reshape(OWNED, GROUP, WIDTH)
        return none

    lax.fori_loop(0, OWNERS, project_q, 0)

    def project_kv(i, none):
        part = kv_in[i].reshape(OWNED * KEYS, WIDTH)
        got = jnp.dot(part, wqkv[:, WIDTH:], preferred_element_type=F32)
        kvp[i] = got.astype(BF16).reshape(OWNED, KEYS, 2 * WIDTH)
        return none

    lax.fori_loop(0, PLACES, project_kv, 0)

    group = (iota((OWNERS, BLOCK), 1) // GROUP == iota((OWNERS, BLOCK), 0) // KEEP)
    counts = lax.dot_general(
        group.astype(F32).astype(BF16),
        train[...].astype(F32).astype(BF16),
        (((1,), (1,)), ((), ())),
        preferred_element_type=F32,
    )
    number = (iota((OWNERS, BLOCKS), 0) % KEEP).astype(F32)
    bias_all = jnp.where(number < counts, 0.0, MASKED)
    which = iota((OWNERS, BLOCKS), 1)
    head = iota((BLOCK, WIDTH), 1) // HEAD_DIM

    def one_block(yy, none):
        mine = table[row_of(yy, z, c)]

        def gather(j, n):
            hit = table[j] == mine

            @pl.when(hit)
            def _():
                at = pl.multiple_of(n * 16, 16)
                come = pl.multiple_of(lax.div(j, PLACES) * 16, 16)
                for f in range(OWNED):
                    kvc[f, pl.ds(at, 16), :] = kvp[lax.rem(j, PLACES), f, pl.ds(come, 16), :]
                column = jnp.sum(jnp.where(which == j, bias_all, 0.0), axis=1, keepdims=True)
                bias[pl.ds(at, 16), :] = jnp.broadcast_to(column, (16, WIDTH))

            return n + hit.astype(jnp.int32)

        n = lax.fori_loop(0, BLOCKS, gather, jnp.int32(0))
        tiles = lax.div(n + 15, 16)

        def tail(i, none):
            bias[pl.ds(pl.multiple_of(i * 16, 16), 16), :] = jnp.full((16, WIDTH), MASKED, F32)
            return none

        lax.fori_loop(n, tiles * 16, tail, 0)

        def one_feature(f, none):
            query = jnp.concatenate([qp[yy * XS + xx, f] for xx in range(XS)], axis=0)
            stacked = jnp.concatenate(
                [jnp.where(head == h, query, jnp.zeros_like(query)) for h in range(HEADS)],
                axis=0,
            )

            def one_tile(kt, carry):
                top, total, acc = carry
                at = pl.multiple_of(kt * TILE, TILE)
                key = kvc[f, pl.ds(at, TILE), 0:WIDTH]
                value = kvc[f, pl.ds(at, TILE), WIDTH:]
                scores = lax.dot_general(
                    key, stacked, (((1,), (1,)), ((), ())), preferred_element_type=F32
                )
                mask = bias[pl.ds(at, TILE), :]
                scores = scores + jnp.concatenate([mask] * HEADS, axis=1)
                new_top = jnp.maximum(top, jnp.max(scores, axis=0, keepdims=True))
                shares = jnp.exp2(scores - new_top)
                fade = jnp.exp2(top - new_top)
                total = total * fade + jnp.sum(shares, axis=0, keepdims=True)
                got = lax.dot_general(
                    value, shares.astype(BF16), (((0,), (0,)), ((), ())),
                    preferred_element_type=F32,
                )
                parts = []
                for h in range(HEADS):
                    rows = slice(h * HEAD_DIM, (h + 1) * HEAD_DIM)
                    cols = slice(h * BLOCK, (h + 1) * BLOCK)
                    parts.append(acc[rows] * fade[:, cols] + got[rows, cols])
                return new_top, total, jnp.concatenate(parts, axis=0)

            top, total, acc = lax.fori_loop(
                0,
                tiles,
                one_tile,
                (
                    jnp.full((1, HEADS * BLOCK), MASKED, F32),
                    jnp.zeros((1, HEADS * BLOCK), F32),
                    jnp.zeros((WIDTH, BLOCK), F32),
                ),
            )
            attended = jnp.concatenate(
                [
                    acc[h * HEAD_DIM : (h + 1) * HEAD_DIM] / total[:, h * BLOCK : (h + 1) * BLOCK]
                    for h in range(HEADS)
                ],
                axis=0,
            ).astype(BF16)
            got = lax.dot_general(
                attended, wout[...], (((0,), (0,)), ((), ())), preferred_element_type=F32
            )
            for xx in range(XS):
                mixed = q_in[yy * XS + xx, f].astype(F32)
                out[yy * XS + xx, f] = (mixed + got[xx * GROUP : (xx + 1) * GROUP]).astype(BF16)
            return none

        lax.fori_loop(0, OWNED, one_feature, 0)
        return none

    lax.fori_loop(0, YS, one_block, 0)


def back_kernel(done, out, send_sems, recv_sems):
    row, x, y, z, c = position()
    owner = y * XS + x
    barrier = pltpu.get_barrier_semaphore()
    for dy in range(YS):
        for dx in range(XS):
            if dx or dy:
                peer = (row_of(around(y, dy, YS), z, c), around(x, dx, XS))
                pl.semaphore_signal(barrier, inc=1, device_id=peer, device_id_type=MESH)
    pl.semaphore_wait(barrier, OWNERS - 1)
    sent = []
    for dy in range(YS):
        for dx in range(XS):
            if dx or dy:
                k = dy * XS + dx
                ty, tx = around(y, dy, YS), around(x, dx, XS)
                copy = remote(
                    done.at[ty * XS + tx],
                    out.at[owner],
                    send_sems.at[k],
                    recv_sems.at[k],
                    row_of(ty, z, c),
                    tx,
                )
                copy.start()
                sent.append(copy)
    out[owner] = done[owner]
    for copy in sent:
        copy.wait_recv()
    for copy in sent:
        copy.wait_send()


def turn_kernel(rows, out, wide):
    def widen(g, none):
        wide[pl.ds(pl.multiple_of(g * OWNED * GROUP, 32), OWNED * GROUP), :] = (
            rows[g].reshape(OWNED * GROUP, WIDTH).astype(F32)
        )
        return none

    lax.fori_loop(0, OWNERS, widen, 0)

    def turn(r, none):
        out[r] = wide[pl.ds(r, FEATS, stride=GROUP), :].astype(BF16)
        return none

    lax.fori_loop(0, GROUP, turn, 0, unroll=4)


def on_device(cells, block_table, row_live, row_train, feat_qkv, feat_out, item_qkv, item_out):
    train = row_train.reshape(BLOCKS, BLOCK)
    live = row_live.reshape(BLOCKS, BLOCK)
    by_feature = jnp.transpose(cells, (1, 0, 2))
    dma = pltpu.SemaphoreType.DMA
    moved = jax.ShapeDtypeStruct((OWNERS, OWNED, GROUP, WIDTH), BF16)
    query, key = pl.pallas_call(
        mix_kernel,
        name="mix",
        out_shape=(moved, jax.ShapeDtypeStruct((PLACES, OWNED, KEYS, WIDTH), BF16)),
        in_specs=[ANY, SMEM, VMEM, VMEM, VMEM, VMEM],
        out_specs=(VMEM, VMEM),
        scratch_shapes=[
            pltpu.VMEM((SHARD, BLOCK, WIDTH), BF16),
            pltpu.VMEM((FEATS, GROUP, WIDTH), BF16),
            pltpu.VMEM((SHARD, WIDTH), F32),
            pltpu.VMEM((SHARD, WIDTH), F32),
            pltpu.VMEM((FEATS, WIDTH), F32),
            pltpu.VMEM((FEATS, WIDTH), F32),
            pltpu.VMEM((8, WIDTH), F32),
            pltpu.VMEM((XS, 8, WIDTH), F32),
            pltpu.VMEM((8, WIDTH), F32),
            pltpu.VMEM((YS * CS, 8, WIDTH), F32),
            pltpu.VMEM((ZS, YS * CS, 8, WIDTH), F32),
            pltpu.VMEM((GROUP * FEATS, WIDTH), F32),
            pltpu.VMEM((GROUP, FEATS, WIDTH), BF16),
            pltpu.VMEM((GROUP, FEATS, 3 * WIDTH), BF16),
            pltpu.VMEM((GROUP, FEATS, WIDTH), BF16),
            pltpu.VMEM((GROUP * FEATS, WIDTH), F32),
            pltpu.VMEM((FEATS, GROUP, WIDTH), BF16),
            dma((2,)),
            dma((XS,)), dma((XS,)), dma((XS,)), dma((XS,)),
            dma((8,)), dma((8,)), dma((8,)), dma((8,)),
            dma((OWNERS,)), dma((OWNERS,)),
            dma((4,)), dma((4,)), dma((4,)), dma((4,)), dma((8,)), dma((8,)),
        ],
        compiler_params=pltpu.CompilerParams(collective_id=0, has_side_effects=True),
    )(by_feature, block_table, live, train, feat_qkv, feat_out)
    done = pl.pallas_call(
        item_kernel,
        name="item",
        out_shape=moved,
        in_specs=[VMEM, VMEM, SMEM, VMEM, VMEM, VMEM],
        out_specs=VMEM,
        scratch_shapes=[
            pltpu.VMEM((OWNERS, OWNED, GROUP, WIDTH), BF16),
            pltpu.VMEM((PLACES, OWNED, KEYS, 2 * WIDTH), BF16),
            pltpu.VMEM((OWNED, PLACES * KEYS, 2 * WIDTH), BF16),
            pltpu.VMEM((PLACES * KEYS, WIDTH), F32),
        ],
    )(query, key, block_table, train, item_qkv, item_out)
    rows = pl.pallas_call(
        back_kernel,
        name="back",
        out_shape=moved,
        in_specs=[VMEM],
        out_specs=VMEM,
        scratch_shapes=[dma((OWNERS,)), dma((OWNERS,))],
        compiler_params=pltpu.CompilerParams(collective_id=1, has_side_effects=True),
    )(done)
    return pl.pallas_call(
        turn_kernel,
        name="turn",
        out_shape=jax.ShapeDtypeStruct((GROUP, FEATS, WIDTH), BF16),
        in_specs=[VMEM],
        out_specs=VMEM,
        scratch_shapes=[pltpu.VMEM((FEATS * GROUP, WIDTH), F32)],
    )(rows)


def solution(mesh):
    return jax.shard_map(
        on_device,
        mesh=mesh,
        in_specs=(P("rows", "feat", None), P(), P(), P(), P(), P(), P(), P()),
        out_specs=P(("rows", "feat"), None, None),
        check_vma=False,
    )
```

```python
import jax
import jax.numpy as jnp
from jax import lax
from jax.experimental import pallas as pl
from jax.experimental.pallas import tpu as pltpu
from jax.sharding import PartitionSpec as P

HEADS = 4
HEAD_DIM = 32
WIDTH = 128
KEEP = 4
XS, YS, ZS, CS = 4, 4, 8, 2
BLOCKS = YS * ZS * CS
BLOCK = 128
FEATS = 80
SHARD = 20
OWNED = 5
GROUP = 32
OWNERS = XS * YS
PLACES = ZS * CS
KEYS = YS * XS * KEEP
TILE = 256
EPSILON = 1e-05
MASKED = -1e30
SCALE = HEAD_DIM**-0.5 * 1.4426950408889634
MESH = pl.DeviceIdType.MESH
F32 = jnp.float32
BF16 = jnp.bfloat16
VMEM = pl.BlockSpec(memory_space=pltpu.VMEM)
SMEM = pl.BlockSpec(memory_space=pltpu.SMEM)
ANY = pl.BlockSpec(memory_space=pl.ANY)


def iota(shape, dim):
    return lax.broadcasted_iota(jnp.int32, shape, dim)


def row_of(y, z, c):
    return y * (ZS * CS) + z * CS + c


def around(at, step, size):
    return lax.rem(at + step + size, size)


def remote(source, target, send, recv, row, feat):
    return pltpu.make_async_remote_copy(
        src_ref=source,
        dst_ref=target,
        send_sem=send,
        recv_sem=recv,
        device_id=(row, feat),
        device_id_type=MESH,
    )


def position():
    row = lax.axis_index("rows")
    x = lax.axis_index("feat")
    y = lax.div(row, ZS * CS)
    z = lax.rem(lax.div(row, CS), ZS)
    c = lax.rem(row, CS)
    return row, x, y, z, c


def mix_kernel(
    cells, table, live, train, wqkv, wout, q_out, kv_out,
    own, xbuf, part, level, mean_of, inv_of, st_src, sx, sy_src, sy, sz_src, sz, counts, nrm, rows, qkv, att, mix, send,
    key_wide, key_send, key_in,
    own_sem, xs, xr, ss, sr, ys, yr, zs, zr, ks, kr, qs, qr, rs, rr, ls, lr, ps, pr,
):
    row, x, y, z, c = position()
    owner = y * XS + x

    fetch = pltpu.make_async_copy(cells, own, own_sem.at[0])
    fetch.start()
    barrier = pltpu.get_barrier_semaphore()
    greet = []
    for dy in range(YS):
        for dx in range(XS):
            if dx or dy:
                greet.append((row_of(around(y, dy, YS), z, c), around(x, dx, XS)))
        greet.append((row_of(around(y, dy, YS), z, 1 - c), x))
    for dz in range(1, ZS):
        greet.append((row_of(y, around(z, dz, ZS), c), x))
    for peer in greet:
        pl.semaphore_signal(barrier, inc=1, device_id=peer, device_id_type=MESH)
    fetch.wait()

    square = iota((BLOCK, WIDTH), 0) == iota((BLOCK, WIDTH), 1)
    flags = live[pl.ds(row, 1), :].astype(F32)
    weight = jnp.broadcast_to(
        jnp.sum(jnp.where(square, flags, 0.0), axis=1, keepdims=True), (BLOCK, WIDTH)
    )
    entries = jnp.broadcast_to(jnp.sum(flags, axis=1, keepdims=True) * WIDTH, (SHARD, WIDTH))

    def add_first(f, none):
        part[pl.ds(f, 1), :] = jnp.sum(own[f].astype(F32) * weight, axis=0, keepdims=True)
        return none

    lax.fori_loop(0, SHARD, add_first, 0, unroll=4)
    first = jnp.sum(part[...], axis=1, keepdims=True)
    level[...] = jnp.broadcast_to(first, (SHARD, WIDTH)) / entries

    def add_second(f, none):
        off = own[f].astype(F32) - level[pl.ds(f, 1), :]
        part[pl.ds(f, 1), :] = jnp.sum(off * off * weight, axis=0, keepdims=True)
        return none

    lax.fori_loop(0, SHARD, add_second, 0, unroll=4)
    second = jnp.sum(part[...], axis=1, keepdims=True)
    lane = iota((SHARD, WIDTH), 1)
    sub = iota((SHARD, WIDTH), 0)
    spot = lane == sub + GROUP * x

    def to_row(column):
        return jnp.sum(jnp.where(spot, column, 0.0), axis=0, keepdims=True)

    st_src[...] = jnp.concatenate(
        [to_row(first), to_row(second), jnp.zeros((6, WIDTH), F32)], axis=0
    )
    counts[...] = WIDTH * jnp.dot(
        live[...].astype(F32).astype(BF16),
        jnp.ones((BLOCK, WIDTH), BF16),
        preferred_element_type=F32,
    )
    key_wide[...] = jnp.zeros_like(key_wide)
    pl.semaphore_wait(barrier, len(greet))

    stat_x = []
    for d in range(1, XS):
        copy = remote(st_src, sx.at[x], ss.at[d], sr.at[d], row, around(x, d, XS))
        copy.start()
        stat_x.append(copy)
    bulk = []
    for d in (1, 3, 2):
        to = around(x, d, XS)
        copy = remote(
            cells.at[:, pl.ds(pl.multiple_of(to * GROUP, GROUP), GROUP)],
            xbuf.at[pl.ds(x * SHARD, SHARD)],
            xs.at[d],
            xr.at[d],
            row,
            to,
        )
        copy.start()
        bulk.append((d, copy))
    keep = pltpu.make_async_copy(
        own.at[:, pl.ds(pl.multiple_of(x * GROUP, GROUP), GROUP)],
        xbuf.at[pl.ds(x * SHARD, SHARD)],
        own_sem.at[1],
    )
    keep.start()
    sx[x] = st_src[...]
    for d in range(1, XS):
        came = around(x, -d, XS)
        remote(st_src, sx.at[came], ss.at[d], sr.at[d], row, x).wait_recv()
    merged = sx[0] + sx[1] + sx[2] + sx[3]
    sy_src[...] = merged
    here = y * CS + c
    sy[here] = merged
    stat_y = []
    for dy in range(YS):
        for dc in range(CS):
            if dy or dc:
                k = dy * CS + dc
                to = row_of(around(y, dy, YS), z, around(c, dc, CS))
                copy = remote(sy_src, sy.at[here], ys.at[k], yr.at[k], to, x)
                copy.start()
                stat_y.append(copy)
    for dy in range(YS):
        for dc in range(CS):
            if dy or dc:
                k = dy * CS + dc
                came = around(y, -dy, YS) * CS + around(c, dc, CS)
                remote(sy_src, sy.at[came], ys.at[k], yr.at[k], row, x).wait_recv()
    for k in range(2):
        tile = jnp.concatenate([sy[i, k : k + 1, :] for i in range(YS * CS)], axis=0)
        sz_src[k] = tile
        sz[z, k] = tile
    stat_z = []
    for d in range(1, ZS):
        copy = remote(
            sz_src, sz.at[z], zs.at[d], zr.at[d], row_of(y, around(z, d, ZS), c), x
        )
        copy.start()
        stat_z.append(copy)
    spots = [jnp.int32(0)] * KEEP
    seen = jnp.int32(0)
    for r in range(GROUP):
        flag = train[row * BLOCK + x * GROUP + r]
        for j in range(KEEP):
            spots[j] = jnp.where((flag == 1) & (seen == j), r, spots[j])
        seen = seen + flag
    mine = table[row]
    weights = [jnp.where(table[b] == mine, 1.0, 0.0).astype(F32) for b in range(BLOCKS)]
    entries_all = jnp.zeros((1, WIDTH), F32)
    for b in range(BLOCKS):
        entries_all = entries_all + weights[b] * counts[b : b + 1, :]
    for d in range(1, ZS):
        came = around(z, -d, ZS)
        remote(sz_src, sz.at[came], zs.at[d], zr.at[d], row, x).wait_recv()

    places = [
        (zz, i, row_of(i // CS, zz, i % CS)) for zz in range(ZS) for i in range(YS * CS)
    ]
    acc = jnp.zeros((1, WIDTH), F32)
    for zz, i, b in places:
        acc = acc + weights[b] * sz[zz, 0, i : i + 1, :]
    mean_row = acc / entries_all
    spread = jnp.zeros((1, WIDTH), F32)
    for zz, i, b in places:
        entries_b = counts[b : b + 1, :]
        off = sz[zz, 0, i : i + 1, :] / entries_b - mean_row
        spread = spread + weights[b] * (sz[zz, 1, i : i + 1, :] + entries_b * (off * off))
    inv_row = lax.rsqrt(spread / entries_all + EPSILON)

    for d, _ in bulk:
        came = xbuf.at[pl.ds(around(x, -d, XS) * SHARD, SHARD)]
        remote(came, came, xs.at[d], xr.at[d], row, x).wait_recv()
    keep.wait()
    for s in range(XS):
        pick = lane == sub + GROUP * s
        for ref, values in ((mean_of, mean_row), (inv_of, inv_row)):
            column = jnp.sum(jnp.where(pick, values, 0.0), axis=1, keepdims=True)
            ref[SHARD * s : SHARD * (s + 1), :] = jnp.broadcast_to(column, (SHARD, WIDTH))

    def norm(f, none):
        value = (xbuf[f].astype(F32) - mean_of[pl.ds(f, 1), :]) * inv_of[pl.ds(f, 1), :]
        nrm[pl.ds(pl.multiple_of(f * GROUP, GROUP), GROUP), :] = value.astype(BF16).astype(F32)
        return none

    lax.fori_loop(0, FEATS, norm, 0, unroll=4)

    def by_row(r, none):
        rows[r] = nrm[pl.ds(r, FEATS, stride=GROUP), :].astype(BF16)
        return none

    lax.fori_loop(0, GROUP, by_row, 0, unroll=4)

    def project(i, none):
        some = rows[pl.ds(i * 4, 4)].reshape(4 * FEATS, WIDTH)
        out = jnp.dot(some, wqkv[...], preferred_element_type=F32)
        qkv[pl.ds(i * 4, 4), :, 0:WIDTH] = (
            (out[:, :WIDTH] * SCALE).astype(BF16).reshape(4, FEATS, WIDTH)
        )
        qkv[pl.ds(i * 4, 4), :, WIDTH:] = (
            out[:, WIDTH:].astype(BF16).reshape(4, FEATS, 2 * WIDTH)
        )
        return none

    lax.fori_loop(0, GROUP // 4, project, 0)

    head = iota((FEATS, WIDTH), 1) // HEAD_DIM
    def attended(r):
        query = qkv[r, :, 0:WIDTH]
        key = qkv[r, :, WIDTH : 2 * WIDTH]
        value = qkv[r, :, 2 * WIDTH :]
        keys = jnp.concatenate(
            [jnp.where(head == h, key, jnp.zeros_like(key)) for h in range(HEADS)], axis=0
        )
        values = jnp.concatenate(
            [jnp.where(head == h, value, jnp.zeros_like(value)) for h in range(HEADS)], axis=0
        )
        scores = lax.dot_general(
            keys, query, (((1,), (1,)), ((), ())), preferred_element_type=F32
        )
        shares = []
        for h in range(HEADS):
            some = scores[h * FEATS : (h + 1) * FEATS]
            some = jnp.exp2(some - jnp.max(some, axis=0, keepdims=True))
            shares.append((some * (1.0 / jnp.sum(some, axis=0, keepdims=True))).astype(BF16))
        return lax.dot_general(
            jnp.concatenate(shares, axis=0),
            values,
            (((0,), (0,)), ((), ())),
            preferred_element_type=F32,
        ).astype(BF16)

    found = [attended(spot) for spot in spots]
    for j in range(KEEP):
        out = jnp.dot(found[j], wout[...], preferred_element_type=F32)
        out = out + rows[spots[j]].astype(F32)
        key_wide[pl.ds(KEEP * lax.rem(x, 2) + j, FEATS, stride=8), :] = out
    key_send[...] = key_wide[...].reshape(FEATS, 8, WIDTH).astype(BF16)
    peers = []
    for dy in range(YS):
        for dx in range(XS):
            if dx or dy:
                ty, tx = around(y, dy, YS), around(x, dx, XS)
                peers.append((dy * XS + dx, ty * XS + tx, row_of(ty, z, c), tx))
    sent = []
    key_moved = []
    for k, to, to_row, tx in peers:
        copy = remote(
            key_send.at[pl.ds(to * OWNED, OWNED)], key_in.at[owner], ks.at[k], kr.at[k], to_row, tx
        )
        copy.start()
        key_moved.append(copy)
    key_in[owner] = key_send[pl.ds(owner * OWNED, OWNED)]

    moved = []

    def half(part):
        first_row = part * (GROUP // 2)

        def attend(r, none):
            att[r] = attended(r)
            return none

        lax.fori_loop(first_row, first_row + GROUP // 2, attend, 0, unroll=16)

        def update(i, none):
            some = att[pl.ds(i * 4, 4)].reshape(4 * FEATS, WIDTH)
            out = jnp.dot(some, wout[...], preferred_element_type=F32)
            out = out + rows[pl.ds(i * 4, 4)].reshape(4 * FEATS, WIDTH).astype(F32)
            mix[pl.ds(i * 4 * FEATS, 4 * FEATS), :] = out
            return none

        lax.fori_loop(part * 4, part * 4 + 4, update, 0, unroll=2)

        def turn(f, none):
            send[f, first_row : first_row + GROUP // 2, :] = mix[
                pl.ds(first_row * FEATS + f, GROUP // 2, stride=FEATS), :
            ].astype(BF16)
            return none

        lax.fori_loop(0, FEATS, turn, 0, unroll=8)
        these = pl.ds(first_row, GROUP // 2)
        for k, to, to_row, tx in peers:
            copy = remote(
                send.at[pl.ds(to * OWNED, OWNED), these],
                q_out.at[owner, :, these],
                qs.at[part * OWNERS + k],
                qr.at[part * OWNERS + k],
                to_row,
                tx,
            )
            copy.start()
            moved.append(copy)
        q_out[owner, :, first_row : first_row + GROUP // 2, :] = send[
            pl.ds(owner * OWNED, OWNED), first_row : first_row + GROUP // 2, :
        ]

    half(0)

    for copy in key_moved:
        copy.wait_recv()
    spot_here = z * CS + c
    for yy in range(YS):
        for f in range(OWNED):
            low = key_in[yy * XS, f].astype(F32) + key_in[yy * XS + 1, f].astype(F32)
            high = key_in[yy * XS + 2, f].astype(F32) + key_in[yy * XS + 3, f].astype(F32)
            kv_out[spot_here, f, yy * 16 : yy * 16 + 16, :] = jnp.concatenate(
                [low, high], axis=0
            ).astype(BF16)

    right, left = row_of(y, around(z, 1, ZS), c), row_of(y, around(z, -1, ZS), c)
    other = row_of(y, z, 1 - c)

    def slot(d, f):
        return kv_out.at[around(z, d, ZS) * CS + c, f]

    def over(d, f):
        k = (d + 4) * OWNED + f
        copy = remote(slot(d, f), slot(d, f), ps.at[k], pr.at[k], other, x)
        copy.start()
        sent.append(copy)

    def go_right(k, f):
        k_f = k * OWNED + f
        copy = remote(slot(-k, f), slot(-k, f), rs.at[k_f], rr.at[k_f], right, x)
        copy.start()
        sent.append(copy)

    def go_left(k, f):
        k_f = k * OWNED + f
        copy = remote(slot(k, f), slot(k, f), ls.at[k_f], lr.at[k_f], left, x)
        copy.start()
        sent.append(copy)

    for f in range(OWNED):
        go_right(0, f)
        go_left(0, f)
    for f in range(OWNED):
        over(0, f)

    half(1)

    for k in range(4):
        for f in range(OWNED):
            k_f = k * OWNED + f
            came = slot(-1 - k, f)
            remote(came, came, rs.at[k_f], rr.at[k_f], right, x).wait_recv()
            if k < 3:
                go_right(k + 1, f)
            over(-1 - k, f)
            if k < 3:
                came = slot(1 + k, f)
                remote(came, came, ls.at[k_f], lr.at[k_f], left, x).wait_recv()
                if k < 2:
                    go_left(k + 1, f)
                over(1 + k, f)
    for copy in moved:
        copy.wait_recv()
    for d in range(-4, 4):
        for f in range(OWNED):
            came = kv_out.at[around(z, d, ZS) * CS + 1 - c, f]
            k = (d + 4) * OWNED + f
            remote(came, came, ps.at[k], pr.at[k], other, x).wait_recv()

    for copy in stat_x + [copy for _, copy in bulk] + stat_y + stat_z + key_moved + moved + sent:
        copy.wait_send()


def item_kernel(
    q_in, kv_in, table, train, wqkv, wout, out,
    qp, kvp, kvc, bias, stack, tops, totals, accs, every, chosen,
):
    row, x, y, z, c = position()
    kvc[...] = jnp.zeros_like(kvc)

    def project_q(i, none):
        part = q_in[i].reshape(OWNED * GROUP, WIDTH)
        got = jnp.dot(part, wqkv[:, :WIDTH], preferred_element_type=F32)
        qp[i] = (got * SCALE).astype(BF16).reshape(OWNED, GROUP, WIDTH)
        return none

    lax.fori_loop(0, OWNERS, project_q, 0, unroll=4)

    def project_kv(i, none):
        part = kv_in[i].reshape(OWNED * KEYS, WIDTH)
        got = jnp.dot(part, wqkv[:, WIDTH:], preferred_element_type=F32)
        kvp[i] = got.astype(BF16).reshape(OWNED, KEYS, 2 * WIDTH)
        return none

    lax.fori_loop(0, PLACES, project_kv, 0, unroll=4)

    group = (iota((OWNERS, BLOCK), 1) // GROUP == iota((OWNERS, BLOCK), 0) // KEEP)
    spread = train[...].astype(F32)[:, None, :] * group.astype(F32)[None]
    counts = jnp.dot(
        spread.reshape(BLOCKS * OWNERS, BLOCK).astype(BF16),
        jnp.ones((BLOCK, WIDTH), BF16),
        preferred_element_type=F32,
    )
    number = (iota((BLOCKS * OWNERS, WIDTH), 0) % KEEP).astype(F32)
    every[...] = jnp.where(number < counts, 0.0, MASKED)
    head = iota((BLOCK, WIDTH), 1) // HEAD_DIM

    def one_block(yy, none):
        mine = table[row_of(yy, z, c)]

        n = jnp.int32(0)
        for j in range(BLOCKS):
            chosen[n] = j
            n = n + jnp.where(table[j] == mine, 1, 0)

        def gather(i, none):
            j = chosen[i]
            at = pl.multiple_of(i * 16, 16)
            come = pl.multiple_of(lax.div(j, PLACES) * 16, 16)
            for f in range(OWNED):
                kvc[f, pl.ds(at, 16), :] = kvp[lax.rem(j, PLACES), f, pl.ds(come, 16), :]
            bias[pl.ds(at, 16), :] = every[pl.ds(pl.multiple_of(j * 16, 16), 16), :]
            return none

        lax.fori_loop(0, n, gather, 0)
        tiles = lax.div(n + 15, 16)

        def tail(i, none):
            bias[pl.ds(pl.multiple_of(i * 16, 16), 16), :] = jnp.full((16, WIDTH), MASKED, F32)
            return none

        lax.fori_loop(n, tiles * 16, tail, 0)

        for f in range(OWNED):
            query = jnp.concatenate([qp[yy * XS + xx, f] for xx in range(XS)], axis=0)
            stack[f] = jnp.concatenate(
                [jnp.where(head == h, query, jnp.zeros_like(query)) for h in range(HEADS)],
                axis=0,
            )
        def first_tile():
            mask = jnp.concatenate([bias[0:TILE, :]] * HEADS, axis=1)
            for f in range(OWNED):
                scores = lax.dot_general(
                    kvc[f, 0:TILE, 0:WIDTH],
                    stack[f],
                    (((1,), (1,)), ((), ())),
                    preferred_element_type=F32,
                )
                scores = scores + mask
                top = jnp.max(scores, axis=0, keepdims=True)
                shares = jnp.exp2(scores - top)
                tops[f] = top
                totals[f] = jnp.sum(shares, axis=0, keepdims=True)
                got = lax.dot_general(
                    kvc[f, 0:TILE, WIDTH:],
                    shares.astype(BF16),
                    (((0,), (0,)), ((), ())),
                    preferred_element_type=F32,
                )
                for h in range(HEADS):
                    rows = slice(h * HEAD_DIM, (h + 1) * HEAD_DIM)
                    cols = slice(h * BLOCK, (h + 1) * BLOCK)
                    accs[f, rows, :] = got[rows, cols]

        first_tile()
        def one_tile(kt, none):
            at = pl.multiple_of(kt * TILE, TILE)
            mask = bias[pl.ds(at, TILE), :]
            mask = jnp.concatenate([mask] * HEADS, axis=1)
            for f in range(OWNED):
                top = tops[f]
                scores = lax.dot_general(
                    kvc[f, pl.ds(at, TILE), 0:WIDTH],
                    stack[f],
                    (((1,), (1,)), ((), ())),
                    preferred_element_type=F32,
                )
                scores = scores + mask
                new_top = jnp.maximum(top, jnp.max(scores, axis=0, keepdims=True))
                shares = jnp.exp2(scores - new_top)
                fade = jnp.exp2(top - new_top)
                tops[f] = new_top
                totals[f] = totals[f] * fade + jnp.sum(shares, axis=0, keepdims=True)
                got = lax.dot_general(
                    kvc[f, pl.ds(at, TILE), WIDTH:],
                    shares.astype(BF16),
                    (((0,), (0,)), ((), ())),
                    preferred_element_type=F32,
                )
                for h in range(HEADS):
                    rows = slice(h * HEAD_DIM, (h + 1) * HEAD_DIM)
                    cols = slice(h * BLOCK, (h + 1) * BLOCK)
                    accs[f, rows, :] = accs[f, rows, :] * fade[:, cols] + got[rows, cols]
            return none

        lax.fori_loop(1, tiles, one_tile, 0)
        for f in range(OWNED):
            total = totals[f]
            attended = jnp.concatenate(
                [
                    accs[f, h * HEAD_DIM : (h + 1) * HEAD_DIM, :]
                    * (1.0 / total[:, h * BLOCK : (h + 1) * BLOCK])
                    for h in range(HEADS)
                ],
                axis=0,
            ).astype(BF16)
            got = lax.dot_general(
                attended, wout[...], (((0,), (0,)), ((), ())), preferred_element_type=F32
            )
            for xx in range(XS):
                mixed = q_in[yy * XS + xx, f].astype(F32)
                out[yy * XS + xx, f] = (mixed + got[xx * GROUP : (xx + 1) * GROUP]).astype(BF16)
        return none

    lax.fori_loop(0, YS, one_block, 0)


def back_kernel(done, out, send_sems, recv_sems):
    row, x, y, z, c = position()
    owner = y * XS + x
    barrier = pltpu.get_barrier_semaphore()
    for dy in range(YS):
        for dx in range(XS):
            if dx or dy:
                peer = (row_of(around(y, dy, YS), z, c), around(x, dx, XS))
                pl.semaphore_signal(barrier, inc=1, device_id=peer, device_id_type=MESH)
    pl.semaphore_wait(barrier, OWNERS - 1)
    sent = []
    for dy in range(YS):
        for dx in range(XS):
            if dx or dy:
                k = dy * XS + dx
                ty, tx = around(y, dy, YS), around(x, dx, XS)
                copy = remote(
                    done.at[ty * XS + tx],
                    out.at[owner],
                    send_sems.at[k],
                    recv_sems.at[k],
                    row_of(ty, z, c),
                    tx,
                )
                copy.start()
                sent.append(copy)
    out[owner] = done[owner]
    for copy in sent:
        copy.wait_recv()
    for copy in sent:
        copy.wait_send()


def turn_kernel(rows, out, wide):
    def widen(g, none):
        wide[pl.ds(pl.multiple_of(g * OWNED * GROUP, 32), OWNED * GROUP), :] = (
            rows[g].reshape(OWNED * GROUP, WIDTH).astype(F32)
        )
        return none

    lax.fori_loop(0, OWNERS, widen, 0)

    def turn(r, none):
        out[r] = wide[pl.ds(r, FEATS, stride=GROUP), :].astype(BF16)
        return none

    lax.fori_loop(0, GROUP, turn, 0, unroll=4)


def item_call(query, key, block_table, train, item_qkv, item_out):
    moved = jax.ShapeDtypeStruct((OWNERS, OWNED, GROUP, WIDTH), BF16)
    return pl.pallas_call(
        item_kernel,
        name="item",
        out_shape=moved,
        in_specs=[VMEM, VMEM, SMEM, VMEM, VMEM, VMEM],
        out_specs=VMEM,
        scratch_shapes=[
            pltpu.VMEM((OWNERS, OWNED, GROUP, WIDTH), BF16),
            pltpu.VMEM((PLACES, OWNED, KEYS, 2 * WIDTH), BF16),
            pltpu.VMEM((OWNED, PLACES * KEYS, 2 * WIDTH), BF16),
            pltpu.VMEM((PLACES * KEYS, WIDTH), F32),
            pltpu.VMEM((OWNED, HEADS * BLOCK, WIDTH), BF16),
            pltpu.VMEM((OWNED, 1, HEADS * BLOCK), F32),
            pltpu.VMEM((OWNED, 1, HEADS * BLOCK), F32),
            pltpu.VMEM((OWNED, WIDTH, BLOCK), F32),
            pltpu.VMEM((PLACES * KEYS, WIDTH), F32),
            pltpu.SMEM((BLOCKS + 8,), jnp.int32),
        ],
    )(query, key, block_table, train, item_qkv, item_out)


def on_device(cells, block_table, row_live, row_train, feat_qkv, feat_out, item_qkv, item_out):
    train = row_train.reshape(BLOCKS, BLOCK)
    live = row_live.reshape(BLOCKS, BLOCK)
    by_feature = jnp.transpose(cells, (1, 0, 2))
    dma = pltpu.SemaphoreType.DMA
    moved = jax.ShapeDtypeStruct((OWNERS, OWNED, GROUP, WIDTH), BF16)
    query, key = pl.pallas_call(
        mix_kernel,
        name="mix",
        out_shape=(moved, jax.ShapeDtypeStruct((PLACES, OWNED, KEYS, WIDTH), BF16)),
        in_specs=[ANY, SMEM, VMEM, SMEM, VMEM, VMEM],
        out_specs=(VMEM, VMEM),
        scratch_shapes=[
            pltpu.VMEM((SHARD, BLOCK, WIDTH), BF16),
            pltpu.VMEM((FEATS, GROUP, WIDTH), BF16),
            pltpu.VMEM((SHARD, WIDTH), F32),
            pltpu.VMEM((SHARD, WIDTH), F32),
            pltpu.VMEM((FEATS, WIDTH), F32),
            pltpu.VMEM((FEATS, WIDTH), F32),
            pltpu.VMEM((8, WIDTH), F32),
            pltpu.VMEM((XS, 8, WIDTH), F32),
            pltpu.VMEM((8, WIDTH), F32),
            pltpu.VMEM((YS * CS, 8, WIDTH), F32),
            pltpu.VMEM((2, YS * CS, WIDTH), F32),
            pltpu.VMEM((ZS, 2, YS * CS, WIDTH), F32),
            pltpu.VMEM((BLOCKS, WIDTH), F32),
            pltpu.VMEM((GROUP * FEATS, WIDTH), F32),
            pltpu.VMEM((GROUP, FEATS, WIDTH), BF16),
            pltpu.VMEM((GROUP, FEATS, 3 * WIDTH), BF16),
            pltpu.VMEM((GROUP, FEATS, WIDTH), BF16),
            pltpu.VMEM((GROUP * FEATS, WIDTH), F32),
            pltpu.VMEM((FEATS, GROUP, WIDTH), BF16),
            pltpu.VMEM((FEATS * 8, WIDTH), F32),
            pltpu.VMEM((FEATS, 8, WIDTH), BF16),
            pltpu.VMEM((OWNERS, OWNED, 8, WIDTH), BF16),
            dma((2,)),
            dma((XS,)), dma((XS,)), dma((XS,)), dma((XS,)),
            dma((8,)), dma((8,)), dma((8,)), dma((8,)),
            dma((OWNERS,)), dma((OWNERS,)), dma((2 * OWNERS,)), dma((2 * OWNERS,)),
            dma((4 * OWNED,)), dma((4 * OWNED,)), dma((3 * OWNED,)), dma((3 * OWNED,)),
            dma((8 * OWNED,)), dma((8 * OWNED,)),
        ],
        compiler_params=pltpu.CompilerParams(collective_id=0, has_side_effects=True),
    )(by_feature, block_table, live, row_train, feat_qkv, feat_out)
    done = item_call(query, key, block_table, train, item_qkv, item_out)
    rows = pl.pallas_call(
        back_kernel,
        name="back",
        out_shape=moved,
        in_specs=[VMEM],
        out_specs=VMEM,
        scratch_shapes=[dma((OWNERS,)), dma((OWNERS,))],
        compiler_params=pltpu.CompilerParams(collective_id=1, has_side_effects=True),
    )(done)
    return pl.pallas_call(
        turn_kernel,
        name="turn",
        out_shape=jax.ShapeDtypeStruct((GROUP, FEATS, WIDTH), BF16),
        in_specs=[VMEM],
        out_specs=VMEM,
        scratch_shapes=[pltpu.VMEM((FEATS * GROUP, WIDTH), F32)],
    )(rows)


def solution(mesh):
    return jax.shard_map(
        on_device,
        mesh=mesh,
        in_specs=(P("rows", "feat", None), P(), P(), P(), P(), P(), P(), P()),
        out_specs=P(("rows", "feat"), None, None),
        check_vma=False,
    )
```

```python
import jax
import jax.numpy as jnp
from jax import lax
from jax.experimental import pallas as pl
from jax.experimental.pallas import tpu as pltpu
from jax.sharding import PartitionSpec as P

HEADS = 4
HEAD_DIM = 32
WIDTH = 128
KEEP = 4
XS, YS, ZS, CS = 4, 4, 8, 2
BLOCKS = YS * ZS * CS
BLOCK = 128
FEATS = 80
SHARD = 20
OWNED = 5
GROUP = 32
OWNERS = XS * YS
PLACES = ZS * CS
KEYS = YS * XS * KEEP
TILE = 256
EPSILON = 1e-05
MASKED = -1e30
SCALE = HEAD_DIM**-0.5 * 1.4426950408889634
MESH = pl.DeviceIdType.MESH
MIX_VMEM = 20 << 20
ITEM_VMEM = 20 << 20
BACK_VMEM = 8 << 20
F32 = jnp.float32
BF16 = jnp.bfloat16
VMEM = pl.BlockSpec(memory_space=pltpu.VMEM)
SMEM = pl.BlockSpec(memory_space=pltpu.SMEM)
ANY = pl.BlockSpec(memory_space=pl.ANY)


def iota(shape, dim):
    return lax.broadcasted_iota(jnp.int32, shape, dim)


def row_of(y, z, c):
    return y * (ZS * CS) + z * CS + c


def around(at, step, size):
    return lax.rem(at + step + size, size)


def remote(source, target, send, recv, row, feat):
    return pltpu.make_async_remote_copy(
        src_ref=source,
        dst_ref=target,
        send_sem=send,
        recv_sem=recv,
        device_id=(row, feat),
        device_id_type=MESH,
    )


def position():
    row = lax.axis_index("rows")
    x = lax.axis_index("feat")
    y = lax.div(row, ZS * CS)
    z = lax.rem(lax.div(row, CS), ZS)
    c = lax.rem(row, CS)
    return row, x, y, z, c


def mix_kernel(
    cells, table, live, train, wqkv, wout, q_out, kv_out,
    own, xbuf, part, level, mean_of, inv_of, st_src, sx, sy_src, sy, sz_src, sz, counts, nrm, rows, qkv, att, mix, send,
    key_wide, key_send, key_in,
    own_sem, xs, xr, ss, sr, ys, yr, zs, zr, ks, kr, qs, qr, rs, rr, ls, lr, ps, pr,
):
    row, x, y, z, c = position()
    owner = y * XS + x

    fetch = pltpu.make_async_copy(cells, own, own_sem.at[0])
    fetch.start()
    barrier = pltpu.get_barrier_semaphore()
    greet = []
    for dy in range(YS):
        for dx in range(XS):
            if dx or dy:
                greet.append((row_of(around(y, dy, YS), z, c), around(x, dx, XS)))
        greet.append((row_of(around(y, dy, YS), z, 1 - c), x))
    for dz in range(1, ZS):
        greet.append((row_of(y, around(z, dz, ZS), c), x))
    for peer in greet:
        pl.semaphore_signal(barrier, inc=1, device_id=peer, device_id_type=MESH)
    fetch.wait()

    square = iota((BLOCK, WIDTH), 0) == iota((BLOCK, WIDTH), 1)
    flags = live[pl.ds(row, 1), :].astype(F32)
    weight = jnp.broadcast_to(
        jnp.sum(jnp.where(square, flags, 0.0), axis=1, keepdims=True), (BLOCK, WIDTH)
    )
    entries = jnp.broadcast_to(jnp.sum(flags, axis=1, keepdims=True) * WIDTH, (SHARD, WIDTH))

    def add_first(f, none):
        part[pl.ds(f, 1), :] = jnp.sum(own[f].astype(F32) * weight, axis=0, keepdims=True)
        return none

    lax.fori_loop(0, SHARD, add_first, 0, unroll=4)
    first = jnp.sum(part[...], axis=1, keepdims=True)
    level[...] = jnp.broadcast_to(first, (SHARD, WIDTH)) / entries

    def add_second(f, none):
        off = own[f].astype(F32) - level[pl.ds(f, 1), :]
        part[pl.ds(f, 1), :] = jnp.sum(off * off * weight, axis=0, keepdims=True)
        return none

    lax.fori_loop(0, SHARD, add_second, 0, unroll=4)
    second = jnp.sum(part[...], axis=1, keepdims=True)
    lane = iota((SHARD, WIDTH), 1)
    sub = iota((SHARD, WIDTH), 0)
    spot = lane == sub + GROUP * x

    def to_row(column):
        return jnp.sum(jnp.where(spot, column, 0.0), axis=0, keepdims=True)

    st_src[...] = jnp.concatenate(
        [to_row(first), to_row(second), jnp.zeros((6, WIDTH), F32)], axis=0
    )
    counts[...] = WIDTH * jnp.dot(
        live[...].astype(F32).astype(BF16),
        jnp.ones((BLOCK, WIDTH), BF16),
        preferred_element_type=F32,
    )
    key_wide[...] = jnp.zeros_like(key_wide)
    pl.semaphore_wait(barrier, len(greet))

    stat_x = []
    for d in range(1, XS):
        copy = remote(st_src, sx.at[x], ss.at[d], sr.at[d], row, around(x, d, XS))
        copy.start()
        stat_x.append(copy)
    bulk = []
    for d in (1, 3, 2):
        to = around(x, d, XS)
        copy = remote(
            cells.at[:, pl.ds(pl.multiple_of(to * GROUP, GROUP), GROUP)],
            xbuf.at[pl.ds(x * SHARD, SHARD)],
            xs.at[d],
            xr.at[d],
            row,
            to,
        )
        copy.start()
        bulk.append((d, copy))
    keep = pltpu.make_async_copy(
        own.at[:, pl.ds(pl.multiple_of(x * GROUP, GROUP), GROUP)],
        xbuf.at[pl.ds(x * SHARD, SHARD)],
        own_sem.at[1],
    )
    keep.start()
    sx[x] = st_src[...]
    for d in range(1, XS):
        came = around(x, -d, XS)
        remote(st_src, sx.at[came], ss.at[d], sr.at[d], row, x).wait_recv()
    merged = sx[0] + sx[1] + sx[2] + sx[3]
    sy_src[...] = merged
    here = y * CS + c
    sy[here] = merged
    stat_y = []
    for dy in range(YS):
        for dc in range(CS):
            if dy or dc:
                k = dy * CS + dc
                to = row_of(around(y, dy, YS), z, around(c, dc, CS))
                copy = remote(sy_src, sy.at[here], ys.at[k], yr.at[k], to, x)
                copy.start()
                stat_y.append(copy)
    for dy in range(YS):
        for dc in range(CS):
            if dy or dc:
                k = dy * CS + dc
                came = around(y, -dy, YS) * CS + around(c, dc, CS)
                remote(sy_src, sy.at[came], ys.at[k], yr.at[k], row, x).wait_recv()
    for k in range(2):
        tile = jnp.concatenate([sy[i, k : k + 1, :] for i in range(YS * CS)], axis=0)
        sz_src[k] = tile
        sz[z, k] = tile
    stat_z = []
    for d in range(1, ZS):
        copy = remote(
            sz_src, sz.at[z], zs.at[d], zr.at[d], row_of(y, around(z, d, ZS), c), x
        )
        copy.start()
        stat_z.append(copy)
    spots = [jnp.int32(0)] * KEEP
    seen = jnp.int32(0)
    for r in range(GROUP):
        flag = train[row * BLOCK + x * GROUP + r]
        for j in range(KEEP):
            spots[j] = jnp.where((flag == 1) & (seen == j), r, spots[j])
        seen = seen + flag
    mine = table[row]
    weights = [jnp.where(table[b] == mine, 1.0, 0.0).astype(F32) for b in range(BLOCKS)]
    entries_all = jnp.zeros((1, WIDTH), F32)
    for b in range(BLOCKS):
        entries_all = entries_all + weights[b] * counts[b : b + 1, :]
    for d in range(1, ZS):
        came = around(z, -d, ZS)
        remote(sz_src, sz.at[came], zs.at[d], zr.at[d], row, x).wait_recv()

    places = [
        (zz, i, row_of(i // CS, zz, i % CS)) for zz in range(ZS) for i in range(YS * CS)
    ]
    acc = jnp.zeros((1, WIDTH), F32)
    for zz, i, b in places:
        acc = acc + weights[b] * sz[zz, 0, i : i + 1, :]
    mean_row = acc / entries_all
    spread = jnp.zeros((1, WIDTH), F32)
    for zz, i, b in places:
        entries_b = counts[b : b + 1, :]
        off = sz[zz, 0, i : i + 1, :] / entries_b - mean_row
        spread = spread + weights[b] * (sz[zz, 1, i : i + 1, :] + entries_b * (off * off))
    inv_row = lax.rsqrt(spread / entries_all + EPSILON)

    for d, _ in bulk:
        came = xbuf.at[pl.ds(around(x, -d, XS) * SHARD, SHARD)]
        remote(came, came, xs.at[d], xr.at[d], row, x).wait_recv()
    keep.wait()
    for s in range(XS):
        pick = lane == sub + GROUP * s
        for ref, values in ((mean_of, mean_row), (inv_of, inv_row)):
            column = jnp.sum(jnp.where(pick, values, 0.0), axis=1, keepdims=True)
            ref[SHARD * s : SHARD * (s + 1), :] = jnp.broadcast_to(column, (SHARD, WIDTH))

    def norm(f, none):
        value = (xbuf[f].astype(F32) - mean_of[pl.ds(f, 1), :]) * inv_of[pl.ds(f, 1), :]
        nrm[pl.ds(pl.multiple_of(f * GROUP, GROUP), GROUP), :] = value.astype(BF16).astype(F32)
        return none

    lax.fori_loop(0, FEATS, norm, 0, unroll=4)

    def by_row(r, none):
        rows[r] = nrm[pl.ds(r, FEATS, stride=GROUP), :].astype(BF16)
        return none

    lax.fori_loop(0, GROUP, by_row, 0, unroll=4)

    def project(i, none):
        some = rows[pl.ds(i * 4, 4)].reshape(4 * FEATS, WIDTH)
        out = jnp.dot(some, wqkv[...], preferred_element_type=F32)
        qkv[pl.ds(i * 4, 4), :, 0:WIDTH] = (
            (out[:, :WIDTH] * SCALE).astype(BF16).reshape(4, FEATS, WIDTH)
        )
        qkv[pl.ds(i * 4, 4), :, WIDTH:] = (
            out[:, WIDTH:].astype(BF16).reshape(4, FEATS, 2 * WIDTH)
        )
        return none

    lax.fori_loop(0, GROUP // 4, project, 0)

    head = iota((FEATS, WIDTH), 1) // HEAD_DIM
    def attended(r):
        query = qkv[r, :, 0:WIDTH]
        key = qkv[r, :, WIDTH : 2 * WIDTH]
        value = qkv[r, :, 2 * WIDTH :]
        keys = jnp.concatenate(
            [jnp.where(head == h, key, jnp.zeros_like(key)) for h in range(HEADS)], axis=0
        )
        values = jnp.concatenate(
            [jnp.where(head == h, value, jnp.zeros_like(value)) for h in range(HEADS)], axis=0
        )
        scores = lax.dot_general(
            keys, query, (((1,), (1,)), ((), ())), preferred_element_type=F32
        )
        shares = []
        for h in range(HEADS):
            some = scores[h * FEATS : (h + 1) * FEATS]
            some = jnp.exp2(some - jnp.max(some, axis=0, keepdims=True))
            shares.append((some * (1.0 / jnp.sum(some, axis=0, keepdims=True))).astype(BF16))
        return lax.dot_general(
            jnp.concatenate(shares, axis=0),
            values,
            (((0,), (0,)), ((), ())),
            preferred_element_type=F32,
        ).astype(BF16)

    found = [attended(spot) for spot in spots]
    for j in range(KEEP):
        out = jnp.dot(found[j], wout[...], preferred_element_type=F32)
        out = out + rows[spots[j]].astype(F32)
        key_wide[pl.ds(KEEP * lax.rem(x, 2) + j, FEATS, stride=8), :] = out
    key_send[...] = key_wide[...].reshape(FEATS, 8, WIDTH).astype(BF16)
    peers = []
    for dy in range(YS):
        for dx in range(XS):
            if dx or dy:
                ty, tx = around(y, dy, YS), around(x, dx, XS)
                peers.append((dy * XS + dx, ty * XS + tx, row_of(ty, z, c), tx))
    sent = []
    key_moved = []
    for k, to, to_row, tx in peers:
        copy = remote(
            key_send.at[pl.ds(to * OWNED, OWNED)], key_in.at[owner], ks.at[k], kr.at[k], to_row, tx
        )
        copy.start()
        key_moved.append(copy)
    key_in[owner] = key_send[pl.ds(owner * OWNED, OWNED)]

    moved = []

    def half(part):
        first_row = part * (GROUP // 2)

        def attend(r, none):
            att[r] = attended(r)
            return none

        lax.fori_loop(first_row, first_row + GROUP // 2, attend, 0, unroll=16)

        def update(i, none):
            some = att[pl.ds(i * 4, 4)].reshape(4 * FEATS, WIDTH)
            out = jnp.dot(some, wout[...], preferred_element_type=F32)
            out = out + rows[pl.ds(i * 4, 4)].reshape(4 * FEATS, WIDTH).astype(F32)
            mix[pl.ds(i * 4 * FEATS, 4 * FEATS), :] = out
            return none

        lax.fori_loop(part * 4, part * 4 + 4, update, 0, unroll=2)

        def turn(f, none):
            send[f, first_row : first_row + GROUP // 2, :] = mix[
                pl.ds(first_row * FEATS + f, GROUP // 2, stride=FEATS), :
            ].astype(BF16)
            return none

        lax.fori_loop(0, FEATS, turn, 0, unroll=8)
        these = pl.ds(first_row, GROUP // 2)
        for k, to, to_row, tx in peers:
            copy = remote(
                send.at[pl.ds(to * OWNED, OWNED), these],
                q_out.at[owner, :, these],
                qs.at[part * OWNERS + k],
                qr.at[part * OWNERS + k],
                to_row,
                tx,
            )
            copy.start()
            moved.append(copy)
        q_out[owner, :, first_row : first_row + GROUP // 2, :] = send[
            pl.ds(owner * OWNED, OWNED), first_row : first_row + GROUP // 2, :
        ]

    half(0)

    for copy in key_moved:
        copy.wait_recv()
    spot_here = z * CS + c
    for yy in range(YS):
        for f in range(OWNED):
            low = key_in[yy * XS, f].astype(F32) + key_in[yy * XS + 1, f].astype(F32)
            high = key_in[yy * XS + 2, f].astype(F32) + key_in[yy * XS + 3, f].astype(F32)
            kv_out[spot_here, f, yy * 16 : yy * 16 + 16, :] = jnp.concatenate(
                [low, high], axis=0
            ).astype(BF16)

    right, left = row_of(y, around(z, 1, ZS), c), row_of(y, around(z, -1, ZS), c)
    other = row_of(y, z, 1 - c)

    def slot(d, f):
        return kv_out.at[around(z, d, ZS) * CS + c, f]

    def over(d, f):
        k = (d + 4) * OWNED + f
        copy = remote(slot(d, f), slot(d, f), ps.at[k], pr.at[k], other, x)
        copy.start()
        sent.append(copy)

    def go_right(k, f):
        k_f = k * OWNED + f
        copy = remote(slot(-k, f), slot(-k, f), rs.at[k_f], rr.at[k_f], right, x)
        copy.start()
        sent.append(copy)

    def go_left(k, f):
        k_f = k * OWNED + f
        copy = remote(slot(k, f), slot(k, f), ls.at[k_f], lr.at[k_f], left, x)
        copy.start()
        sent.append(copy)

    for f in range(OWNED):
        go_right(0, f)
        go_left(0, f)
    for f in range(OWNED):
        over(0, f)

    half(1)

    for k in range(4):
        for f in range(OWNED):
            k_f = k * OWNED + f
            came = slot(-1 - k, f)
            remote(came, came, rs.at[k_f], rr.at[k_f], right, x).wait_recv()
            if k < 3:
                go_right(k + 1, f)
            over(-1 - k, f)
            if k < 3:
                came = slot(1 + k, f)
                remote(came, came, ls.at[k_f], lr.at[k_f], left, x).wait_recv()
                if k < 2:
                    go_left(k + 1, f)
                over(1 + k, f)
    for copy in moved:
        copy.wait_recv()
    for d in range(-4, 4):
        for f in range(OWNED):
            came = kv_out.at[around(z, d, ZS) * CS + 1 - c, f]
            k = (d + 4) * OWNED + f
            remote(came, came, ps.at[k], pr.at[k], other, x).wait_recv()

    for copy in stat_x + [copy for _, copy in bulk] + stat_y + stat_z + key_moved + moved + sent:
        copy.wait_send()


def item_kernel(
    q_in, kv_in, table, train, wqkv, wout, out,
    qp, kvp, kvc, bias, stack, tops, totals, accs, every, chosen,
):
    row, x, y, z, c = position()
    kvc[...] = jnp.zeros_like(kvc)

    def project_q(i, none):
        part = q_in[i].reshape(OWNED * GROUP, WIDTH)
        got = jnp.dot(part, wqkv[:, :WIDTH], preferred_element_type=F32)
        qp[i] = (got * SCALE).astype(BF16).reshape(OWNED, GROUP, WIDTH)
        return none

    lax.fori_loop(0, OWNERS, project_q, 0, unroll=4)

    def project_kv(i, none):
        part = kv_in[i].reshape(OWNED * KEYS, WIDTH)
        got = jnp.dot(part, wqkv[:, WIDTH:], preferred_element_type=F32)
        kvp[i] = got.astype(BF16).reshape(OWNED, KEYS, 2 * WIDTH)
        return none

    lax.fori_loop(0, PLACES, project_kv, 0, unroll=4)

    group = (iota((OWNERS, BLOCK), 1) // GROUP == iota((OWNERS, BLOCK), 0) // KEEP)
    spread = train[...].astype(F32)[:, None, :] * group.astype(F32)[None]
    counts = jnp.dot(
        spread.reshape(BLOCKS * OWNERS, BLOCK).astype(BF16),
        jnp.ones((BLOCK, WIDTH), BF16),
        preferred_element_type=F32,
    )
    number = (iota((BLOCKS * OWNERS, WIDTH), 0) % KEEP).astype(F32)
    every[...] = jnp.where(number < counts, 0.0, MASKED)
    head = iota((BLOCK, WIDTH), 1) // HEAD_DIM

    def one_block(yy, none):
        mine = table[row_of(yy, z, c)]

        n = jnp.int32(0)
        for j in range(BLOCKS):
            chosen[n] = j
            n = n + jnp.where(table[j] == mine, 1, 0)

        def gather(i, none):
            j = chosen[i]
            at = pl.multiple_of(i * 16, 16)
            come = pl.multiple_of(lax.div(j, PLACES) * 16, 16)
            for f in range(OWNED):
                kvc[f, pl.ds(at, 16), :] = kvp[lax.rem(j, PLACES), f, pl.ds(come, 16), :]
            bias[pl.ds(at, 16), :] = every[pl.ds(pl.multiple_of(j * 16, 16), 16), :]
            return none

        lax.fori_loop(0, n, gather, 0)
        tiles = lax.div(n + 15, 16)

        def tail(i, none):
            bias[pl.ds(pl.multiple_of(i * 16, 16), 16), :] = jnp.full((16, WIDTH), MASKED, F32)
            return none

        lax.fori_loop(n, tiles * 16, tail, 0)

        for f in range(OWNED):
            query = jnp.concatenate([qp[yy * XS + xx, f] for xx in range(XS)], axis=0)
            stack[f] = jnp.concatenate(
                [jnp.where(head == h, query, jnp.zeros_like(query)) for h in range(HEADS)],
                axis=0,
            )
        def first_tile():
            mask = jnp.concatenate([bias[0:TILE, :]] * HEADS, axis=1)
            for f in range(OWNED):
                scores = lax.dot_general(
                    kvc[f, 0:TILE, 0:WIDTH],
                    stack[f],
                    (((1,), (1,)), ((), ())),
                    preferred_element_type=F32,
                )
                scores = scores + mask
                top = jnp.max(scores, axis=0, keepdims=True)
                shares = jnp.exp2(scores - top)
                tops[f] = top
                totals[f] = jnp.sum(shares, axis=0, keepdims=True)
                got = lax.dot_general(
                    kvc[f, 0:TILE, WIDTH:],
                    shares.astype(BF16),
                    (((0,), (0,)), ((), ())),
                    preferred_element_type=F32,
                )
                for h in range(HEADS):
                    rows = slice(h * HEAD_DIM, (h + 1) * HEAD_DIM)
                    cols = slice(h * BLOCK, (h + 1) * BLOCK)
                    accs[f, rows, :] = got[rows, cols]

        first_tile()
        def one_tile(kt, none):
            at = pl.multiple_of(kt * TILE, TILE)
            mask = bias[pl.ds(at, TILE), :]
            mask = jnp.concatenate([mask] * HEADS, axis=1)
            for f in range(OWNED):
                top = tops[f]
                scores = lax.dot_general(
                    kvc[f, pl.ds(at, TILE), 0:WIDTH],
                    stack[f],
                    (((1,), (1,)), ((), ())),
                    preferred_element_type=F32,
                )
                scores = scores + mask
                new_top = jnp.maximum(top, jnp.max(scores, axis=0, keepdims=True))
                shares = jnp.exp2(scores - new_top)
                fade = jnp.exp2(top - new_top)
                tops[f] = new_top
                totals[f] = totals[f] * fade + jnp.sum(shares, axis=0, keepdims=True)
                got = lax.dot_general(
                    kvc[f, pl.ds(at, TILE), WIDTH:],
                    shares.astype(BF16),
                    (((0,), (0,)), ((), ())),
                    preferred_element_type=F32,
                )
                for h in range(HEADS):
                    rows = slice(h * HEAD_DIM, (h + 1) * HEAD_DIM)
                    cols = slice(h * BLOCK, (h + 1) * BLOCK)
                    accs[f, rows, :] = accs[f, rows, :] * fade[:, cols] + got[rows, cols]
            return none

        lax.fori_loop(1, tiles, one_tile, 0)
        for f in range(OWNED):
            total = totals[f]
            attended = jnp.concatenate(
                [
                    accs[f, h * HEAD_DIM : (h + 1) * HEAD_DIM, :]
                    * (1.0 / total[:, h * BLOCK : (h + 1) * BLOCK])
                    for h in range(HEADS)
                ],
                axis=0,
            ).astype(BF16)
            got = lax.dot_general(
                attended, wout[...], (((0,), (0,)), ((), ())), preferred_element_type=F32
            )
            for xx in range(XS):
                mixed = q_in[yy * XS + xx, f].astype(F32)
                out[yy * XS + xx, f] = (mixed + got[xx * GROUP : (xx + 1) * GROUP]).astype(BF16)
        return none

    lax.fori_loop(0, YS, one_block, 0)


def back_kernel(done, out, landed, wide, send_sems, recv_sems, own_sem):
    row, x, y, z, c = position()
    owner = y * XS + x
    barrier = pltpu.get_barrier_semaphore()
    steps = [(dy, dx) for dy in range(YS) for dx in range(XS) if dx or dy]
    steps.sort(key=lambda step: min(step[0], YS - step[0]) + min(step[1], XS - step[1]))
    for dy, dx in steps:
        peer = (row_of(around(y, dy, YS), z, c), around(x, dx, XS))
        pl.semaphore_signal(barrier, inc=1, device_id=peer, device_id_type=MESH)
    keep = pltpu.make_async_copy(done.at[owner], landed.at[owner], own_sem.at[0])
    keep.start()
    pl.semaphore_wait(barrier, OWNERS - 1)
    sent = []
    for dy, dx in steps:
        k = dy * XS + dx
        ty, tx = around(y, dy, YS), around(x, dx, XS)
        copy = remote(
            done.at[ty * XS + tx],
            landed.at[owner],
            send_sems.at[k],
            recv_sems.at[k],
            row_of(ty, z, c),
            tx,
        )
        copy.start()
        sent.append(copy)

    def place(g):
        for f in range(OWNED):
            wide[pl.ds(g * OWNED + f, GROUP, stride=FEATS), :] = landed[g, f].astype(F32)

    keep.wait()
    place(owner)
    for dy, dx in steps:
        k = dy * XS + dx
        g = around(y, -dy, YS) * XS + around(x, -dx, XS)
        remote(landed.at[g], landed.at[g], send_sems.at[k], recv_sems.at[k], row, x).wait_recv()
        place(g)

    def finish(i, none):
        some = wide[pl.ds(pl.multiple_of(i * 4 * FEATS, 64), 4 * FEATS), :]
        out[pl.ds(i * 4, 4)] = some.reshape(4, FEATS, WIDTH).astype(BF16)
        return none

    lax.fori_loop(0, GROUP // 4, finish, 0, unroll=2)
    for copy in sent:
        copy.wait_send()


def item_call(query, key, block_table, train, item_qkv, item_out):
    moved = jax.ShapeDtypeStruct((OWNERS, OWNED, GROUP, WIDTH), BF16)
    return pl.pallas_call(
        item_kernel,
        name="item",
        out_shape=moved,
        in_specs=[VMEM, VMEM, SMEM, VMEM, VMEM, VMEM],
        out_specs=VMEM,
        scratch_shapes=[
            pltpu.VMEM((OWNERS, OWNED, GROUP, WIDTH), BF16),
            pltpu.VMEM((PLACES, OWNED, KEYS, 2 * WIDTH), BF16),
            pltpu.VMEM((OWNED, PLACES * KEYS, 2 * WIDTH), BF16),
            pltpu.VMEM((PLACES * KEYS, WIDTH), F32),
            pltpu.VMEM((OWNED, HEADS * BLOCK, WIDTH), BF16),
            pltpu.VMEM((OWNED, 1, HEADS * BLOCK), F32),
            pltpu.VMEM((OWNED, 1, HEADS * BLOCK), F32),
            pltpu.VMEM((OWNED, WIDTH, BLOCK), F32),
            pltpu.VMEM((PLACES * KEYS, WIDTH), F32),
            pltpu.SMEM((BLOCKS + 8,), jnp.int32),
        ],
        compiler_params=pltpu.CompilerParams(vmem_limit_bytes=ITEM_VMEM),
    )(query, key, block_table, train, item_qkv, item_out)


def on_device(cells, block_table, row_live, row_train, feat_qkv, feat_out, item_qkv, item_out):
    train = row_train.reshape(BLOCKS, BLOCK)
    live = row_live.reshape(BLOCKS, BLOCK)
    by_feature = jnp.transpose(cells, (1, 0, 2))
    dma = pltpu.SemaphoreType.DMA
    moved = jax.ShapeDtypeStruct((OWNERS, OWNED, GROUP, WIDTH), BF16)
    query, key = pl.pallas_call(
        mix_kernel,
        name="mix",
        out_shape=(moved, jax.ShapeDtypeStruct((PLACES, OWNED, KEYS, WIDTH), BF16)),
        in_specs=[ANY, SMEM, VMEM, SMEM, VMEM, VMEM],
        out_specs=(VMEM, VMEM),
        scratch_shapes=[
            pltpu.VMEM((SHARD, BLOCK, WIDTH), BF16),
            pltpu.VMEM((FEATS, GROUP, WIDTH), BF16),
            pltpu.VMEM((SHARD, WIDTH), F32),
            pltpu.VMEM((SHARD, WIDTH), F32),
            pltpu.VMEM((FEATS, WIDTH), F32),
            pltpu.VMEM((FEATS, WIDTH), F32),
            pltpu.VMEM((8, WIDTH), F32),
            pltpu.VMEM((XS, 8, WIDTH), F32),
            pltpu.VMEM((8, WIDTH), F32),
            pltpu.VMEM((YS * CS, 8, WIDTH), F32),
            pltpu.VMEM((2, YS * CS, WIDTH), F32),
            pltpu.VMEM((ZS, 2, YS * CS, WIDTH), F32),
            pltpu.VMEM((BLOCKS, WIDTH), F32),
            pltpu.VMEM((GROUP * FEATS, WIDTH), F32),
            pltpu.VMEM((GROUP, FEATS, WIDTH), BF16),
            pltpu.VMEM((GROUP, FEATS, 3 * WIDTH), BF16),
            pltpu.VMEM((GROUP, FEATS, WIDTH), BF16),
            pltpu.VMEM((GROUP * FEATS, WIDTH), F32),
            pltpu.VMEM((FEATS, GROUP, WIDTH), BF16),
            pltpu.VMEM((FEATS * 8, WIDTH), F32),
            pltpu.VMEM((FEATS, 8, WIDTH), BF16),
            pltpu.VMEM((OWNERS, OWNED, 8, WIDTH), BF16),
            dma((2,)),
            dma((XS,)), dma((XS,)), dma((XS,)), dma((XS,)),
            dma((8,)), dma((8,)), dma((8,)), dma((8,)),
            dma((OWNERS,)), dma((OWNERS,)), dma((2 * OWNERS,)), dma((2 * OWNERS,)),
            dma((4 * OWNED,)), dma((4 * OWNED,)), dma((3 * OWNED,)), dma((3 * OWNED,)),
            dma((8 * OWNED,)), dma((8 * OWNED,)),
        ],
        compiler_params=pltpu.CompilerParams(
            collective_id=0, has_side_effects=True, vmem_limit_bytes=MIX_VMEM
        ),
    )(by_feature, block_table, live, row_train, feat_qkv, feat_out)
    done = item_call(query, key, block_table, train, item_qkv, item_out)
    return pl.pallas_call(
        back_kernel,
        name="back",
        out_shape=jax.ShapeDtypeStruct((GROUP, FEATS, WIDTH), BF16),
        in_specs=[ANY],
        out_specs=VMEM,
        scratch_shapes=[
            pltpu.VMEM((OWNERS, OWNED, GROUP, WIDTH), BF16),
            pltpu.VMEM((GROUP * FEATS, WIDTH), F32),
            dma((OWNERS,)), dma((OWNERS,)), dma((1,)),
        ],
        compiler_params=pltpu.CompilerParams(
            collective_id=1, has_side_effects=True, vmem_limit_bytes=BACK_VMEM
        ),
    )(done)


def solution(mesh):
    return jax.shard_map(
        on_device,
        mesh=mesh,
        in_specs=(P("rows", "feat", None), P(), P(), P(), P(), P(), P(), P()),
        out_specs=P(("rows", "feat"), None, None),
        check_vma=False,
    )
```

```python
import jax
import jax.numpy as jnp
from jax import lax
from jax.experimental import pallas as pl
from jax.experimental.pallas import tpu as pltpu
from jax.sharding import PartitionSpec as P

HEADS = 4
HEAD_DIM = 32
WIDTH = 128
KEEP = 4
XS, YS, ZS, CS = 4, 4, 8, 2
BLOCKS = YS * ZS * CS
BLOCK = 128
FEATS = 80
SHARD = 20
OWNED = 5
GROUP = 32
OWNERS = XS * YS
PLACES = ZS * CS
KEYS = YS * XS * KEEP
TILE = 256
EPSILON = 1e-05
MASKED = -1e30
SCALE = HEAD_DIM**-0.5 * 1.4426950408889634
MESH = pl.DeviceIdType.MESH
MIX_VMEM = 20 << 20
ITEM_VMEM = 20 << 20
BACK_VMEM = 8 << 20
F32 = jnp.float32
BF16 = jnp.bfloat16
VMEM = pl.BlockSpec(memory_space=pltpu.VMEM)
SMEM = pl.BlockSpec(memory_space=pltpu.SMEM)
ANY = pl.BlockSpec(memory_space=pl.ANY)
HBM = pl.BlockSpec(memory_space=pltpu.HBM)


def iota(shape, dim):
    return lax.broadcasted_iota(jnp.int32, shape, dim)


def row_of(y, z, c):
    return y * (ZS * CS) + z * CS + c


def around(at, step, size):
    return lax.rem(at + step + size, size)


def remote(source, target, send, recv, row, feat):
    return pltpu.make_async_remote_copy(
        src_ref=source,
        dst_ref=target,
        send_sem=send,
        recv_sem=recv,
        device_id=(row, feat),
        device_id_type=MESH,
    )


def stay(*arrays):
    return [pltpu.with_memory_space_constraint(a, pltpu.HBM) for a in arrays]


def position():
    row = lax.axis_index("rows")
    x = lax.axis_index("feat")
    y = lax.div(row, ZS * CS)
    z = lax.rem(lax.div(row, CS), ZS)
    c = lax.rem(row, CS)
    return row, x, y, z, c


def mix_kernel(
    cells, table_in, live_in, train_in, wqkv_in, wout_in, q_out, kv_out,
    table, live, train, wqkv, wout, in_sem, own, xbuf, part, level, mean_of, inv_of, st_src, sx, sy_src, sy, sz_src, sz, counts, nrm, rows, qkv, att, mix, send,
    key_wide, key_send, key_in,
    own_sem, xs, xr, ss, sr, ys, yr, zs, zr, ks, kr, qs, qr, rs, rr, ls, lr, ps, pr,
):
    row, x, y, z, c = position()
    owner = y * XS + x

    fetch = pltpu.make_async_copy(cells, own, own_sem.at[0])
    fetch.start()
    loads = [
        pltpu.make_async_copy(source, target, in_sem.at[i])
        for i, (source, target) in enumerate(
            ((live_in, live), (table_in, table), (train_in, train), (wqkv_in, wqkv), (wout_in, wout))
        )
    ]
    for load in loads:
        load.start()
    barrier = pltpu.get_barrier_semaphore()
    greet = []
    for dy in range(YS):
        for dx in range(XS):
            if dx or dy:
                greet.append((row_of(around(y, dy, YS), z, c), around(x, dx, XS)))
        greet.append((row_of(around(y, dy, YS), z, 1 - c), x))
    for dz in range(1, ZS):
        greet.append((row_of(y, around(z, dz, ZS), c), x))
    for peer in greet:
        pl.semaphore_signal(barrier, inc=1, device_id=peer, device_id_type=MESH)
    fetch.wait()
    for load in loads:
        load.wait()

    square = iota((BLOCK, WIDTH), 0) == iota((BLOCK, WIDTH), 1)
    flags = live[pl.ds(row, 1), :].astype(F32)
    weight = jnp.broadcast_to(
        jnp.sum(jnp.where(square, flags, 0.0), axis=1, keepdims=True), (BLOCK, WIDTH)
    )
    entries = jnp.broadcast_to(jnp.sum(flags, axis=1, keepdims=True) * WIDTH, (SHARD, WIDTH))

    def add_first(f, none):
        part[pl.ds(f, 1), :] = jnp.sum(own[f].astype(F32) * weight, axis=0, keepdims=True)
        return none

    lax.fori_loop(0, SHARD, add_first, 0, unroll=4)
    first = jnp.sum(part[...], axis=1, keepdims=True)
    level[...] = jnp.broadcast_to(first, (SHARD, WIDTH)) / entries

    def add_second(f, none):
        off = own[f].astype(F32) - level[pl.ds(f, 1), :]
        part[pl.ds(f, 1), :] = jnp.sum(off * off * weight, axis=0, keepdims=True)
        return none

    lax.fori_loop(0, SHARD, add_second, 0, unroll=4)
    second = jnp.sum(part[...], axis=1, keepdims=True)
    lane = iota((SHARD, WIDTH), 1)
    sub = iota((SHARD, WIDTH), 0)
    spot = lane == sub + GROUP * x

    def to_row(column):
        return jnp.sum(jnp.where(spot, column, 0.0), axis=0, keepdims=True)

    st_src[...] = jnp.concatenate(
        [to_row(first), to_row(second), jnp.zeros((6, WIDTH), F32)], axis=0
    )
    counts[...] = WIDTH * jnp.dot(
        live[...].astype(F32).astype(BF16),
        jnp.ones((BLOCK, WIDTH), BF16),
        preferred_element_type=F32,
    )
    key_wide[...] = jnp.zeros_like(key_wide)
    pl.semaphore_wait(barrier, len(greet))

    stat_x = []
    for d in range(1, XS):
        copy = remote(st_src, sx.at[x], ss.at[d], sr.at[d], row, around(x, d, XS))
        copy.start()
        stat_x.append(copy)
    bulk = []
    for d in (1, 3, 2):
        to = around(x, d, XS)
        copy = remote(
            cells.at[:, pl.ds(pl.multiple_of(to * GROUP, GROUP), GROUP)],
            xbuf.at[pl.ds(x * SHARD, SHARD)],
            xs.at[d],
            xr.at[d],
            row,
            to,
        )
        copy.start()
        bulk.append((d, copy))
    keep = pltpu.make_async_copy(
        own.at[:, pl.ds(pl.multiple_of(x * GROUP, GROUP), GROUP)],
        xbuf.at[pl.ds(x * SHARD, SHARD)],
        own_sem.at[1],
    )
    keep.start()
    sx[x] = st_src[...]
    for d in range(1, XS):
        came = around(x, -d, XS)
        remote(st_src, sx.at[came], ss.at[d], sr.at[d], row, x).wait_recv()
    merged = sx[0] + sx[1] + sx[2] + sx[3]
    sy_src[...] = merged
    here = y * CS + c
    sy[here] = merged
    stat_y = []
    for dy in range(YS):
        for dc in range(CS):
            if dy or dc:
                k = dy * CS + dc
                to = row_of(around(y, dy, YS), z, around(c, dc, CS))
                copy = remote(sy_src, sy.at[here], ys.at[k], yr.at[k], to, x)
                copy.start()
                stat_y.append(copy)
    for dy in range(YS):
        for dc in range(CS):
            if dy or dc:
                k = dy * CS + dc
                came = around(y, -dy, YS) * CS + around(c, dc, CS)
                remote(sy_src, sy.at[came], ys.at[k], yr.at[k], row, x).wait_recv()
    for k in range(2):
        tile = jnp.concatenate([sy[i, k : k + 1, :] for i in range(YS * CS)], axis=0)
        sz_src[k] = tile
        sz[z, k] = tile
    stat_z = []
    for d in range(1, ZS):
        copy = remote(
            sz_src, sz.at[z], zs.at[d], zr.at[d], row_of(y, around(z, d, ZS), c), x
        )
        copy.start()
        stat_z.append(copy)
    spots = [jnp.int32(0)] * KEEP
    seen = jnp.int32(0)
    for r in range(GROUP):
        flag = train[row * BLOCK + x * GROUP + r]
        for j in range(KEEP):
            spots[j] = jnp.where((flag == 1) & (seen == j), r, spots[j])
        seen = seen + flag
    mine = table[row]
    weights = [jnp.where(table[b] == mine, 1.0, 0.0).astype(F32) for b in range(BLOCKS)]
    entries_all = jnp.zeros((1, WIDTH), F32)
    for b in range(BLOCKS):
        entries_all = entries_all + weights[b] * counts[b : b + 1, :]
    for d in range(1, ZS):
        came = around(z, -d, ZS)
        remote(sz_src, sz.at[came], zs.at[d], zr.at[d], row, x).wait_recv()

    places = [
        (zz, i, row_of(i // CS, zz, i % CS)) for zz in range(ZS) for i in range(YS * CS)
    ]
    acc = jnp.zeros((1, WIDTH), F32)
    for zz, i, b in places:
        acc = acc + weights[b] * sz[zz, 0, i : i + 1, :]
    mean_row = acc / entries_all
    spread = jnp.zeros((1, WIDTH), F32)
    for zz, i, b in places:
        entries_b = counts[b : b + 1, :]
        off = sz[zz, 0, i : i + 1, :] / entries_b - mean_row
        spread = spread + weights[b] * (sz[zz, 1, i : i + 1, :] + entries_b * (off * off))
    inv_row = lax.rsqrt(spread / entries_all + EPSILON)

    for d, _ in bulk:
        came = xbuf.at[pl.ds(around(x, -d, XS) * SHARD, SHARD)]
        remote(came, came, xs.at[d], xr.at[d], row, x).wait_recv()
    keep.wait()
    for s in range(XS):
        pick = lane == sub + GROUP * s
        for ref, values in ((mean_of, mean_row), (inv_of, inv_row)):
            column = jnp.sum(jnp.where(pick, values, 0.0), axis=1, keepdims=True)
            ref[SHARD * s : SHARD * (s + 1), :] = jnp.broadcast_to(column, (SHARD, WIDTH))

    def norm(f, none):
        value = (xbuf[f].astype(F32) - mean_of[pl.ds(f, 1), :]) * inv_of[pl.ds(f, 1), :]
        nrm[pl.ds(pl.multiple_of(f * GROUP, GROUP), GROUP), :] = value.astype(BF16).astype(F32)
        return none

    lax.fori_loop(0, FEATS, norm, 0, unroll=4)

    def by_row(r, none):
        rows[r] = nrm[pl.ds(r, FEATS, stride=GROUP), :].astype(BF16)
        return none

    lax.fori_loop(0, GROUP, by_row, 0, unroll=4)

    def project(i, none):
        some = rows[pl.ds(i * 4, 4)].reshape(4 * FEATS, WIDTH)
        out = jnp.dot(some, wqkv[...], preferred_element_type=F32)
        qkv[pl.ds(i * 4, 4), :, 0:WIDTH] = (
            (out[:, :WIDTH] * SCALE).astype(BF16).reshape(4, FEATS, WIDTH)
        )
        qkv[pl.ds(i * 4, 4), :, WIDTH:] = (
            out[:, WIDTH:].astype(BF16).reshape(4, FEATS, 2 * WIDTH)
        )
        return none

    lax.fori_loop(0, GROUP // 4, project, 0)

    head = iota((FEATS, WIDTH), 1) // HEAD_DIM
    def attended(r):
        query = qkv[r, :, 0:WIDTH]
        key = qkv[r, :, WIDTH : 2 * WIDTH]
        value = qkv[r, :, 2 * WIDTH :]
        keys = jnp.concatenate(
            [jnp.where(head == h, key, jnp.zeros_like(key)) for h in range(HEADS)], axis=0
        )
        values = jnp.concatenate(
            [jnp.where(head == h, value, jnp.zeros_like(value)) for h in range(HEADS)], axis=0
        )
        scores = lax.dot_general(
            keys, query, (((1,), (1,)), ((), ())), preferred_element_type=F32
        )
        shares = []
        for h in range(HEADS):
            some = scores[h * FEATS : (h + 1) * FEATS]
            some = jnp.exp2(some - jnp.max(some, axis=0, keepdims=True))
            shares.append((some * (1.0 / jnp.sum(some, axis=0, keepdims=True))).astype(BF16))
        return lax.dot_general(
            jnp.concatenate(shares, axis=0),
            values,
            (((0,), (0,)), ((), ())),
            preferred_element_type=F32,
        ).astype(BF16)

    found = [attended(spot) for spot in spots]
    for j in range(KEEP):
        out = jnp.dot(found[j], wout[...], preferred_element_type=F32)
        out = out + rows[spots[j]].astype(F32)
        key_wide[pl.ds(KEEP * lax.rem(x, 2) + j, FEATS, stride=8), :] = out
    key_send[...] = key_wide[...].reshape(FEATS, 8, WIDTH).astype(BF16)
    peers = []
    for dy in range(YS):
        for dx in range(XS):
            if dx or dy:
                ty, tx = around(y, dy, YS), around(x, dx, XS)
                peers.append((dy * XS + dx, ty * XS + tx, row_of(ty, z, c), tx))
    sent = []
    key_moved = []
    for k, to, to_row, tx in peers:
        copy = remote(
            key_send.at[pl.ds(to * OWNED, OWNED)], key_in.at[owner], ks.at[k], kr.at[k], to_row, tx
        )
        copy.start()
        key_moved.append(copy)
    key_in[owner] = key_send[pl.ds(owner * OWNED, OWNED)]

    moved = []

    def half(part):
        first_row = part * (GROUP // 2)

        def attend(r, none):
            att[r] = attended(r)
            return none

        lax.fori_loop(first_row, first_row + GROUP // 2, attend, 0, unroll=16)

        def update(i, none):
            some = att[pl.ds(i * 4, 4)].reshape(4 * FEATS, WIDTH)
            out = jnp.dot(some, wout[...], preferred_element_type=F32)
            out = out + rows[pl.ds(i * 4, 4)].reshape(4 * FEATS, WIDTH).astype(F32)
            mix[pl.ds(i * 4 * FEATS, 4 * FEATS), :] = out
            return none

        lax.fori_loop(part * 4, part * 4 + 4, update, 0, unroll=2)

        def turn(f, none):
            send[f, first_row : first_row + GROUP // 2, :] = mix[
                pl.ds(first_row * FEATS + f, GROUP // 2, stride=FEATS), :
            ].astype(BF16)
            return none

        lax.fori_loop(0, FEATS, turn, 0, unroll=8)
        these = pl.ds(first_row, GROUP // 2)
        for k, to, to_row, tx in peers:
            copy = remote(
                send.at[pl.ds(to * OWNED, OWNED), these],
                q_out.at[owner, :, these],
                qs.at[part * OWNERS + k],
                qr.at[part * OWNERS + k],
                to_row,
                tx,
            )
            copy.start()
            moved.append(copy)
        q_out[owner, :, first_row : first_row + GROUP // 2, :] = send[
            pl.ds(owner * OWNED, OWNED), first_row : first_row + GROUP // 2, :
        ]

    half(0)

    for copy in key_moved:
        copy.wait_recv()
    spot_here = z * CS + c
    for yy in range(YS):
        for f in range(OWNED):
            low = key_in[yy * XS, f].astype(F32) + key_in[yy * XS + 1, f].astype(F32)
            high = key_in[yy * XS + 2, f].astype(F32) + key_in[yy * XS + 3, f].astype(F32)
            kv_out[spot_here, f, yy * 16 : yy * 16 + 16, :] = jnp.concatenate(
                [low, high], axis=0
            ).astype(BF16)

    right, left = row_of(y, around(z, 1, ZS), c), row_of(y, around(z, -1, ZS), c)
    other = row_of(y, z, 1 - c)

    def slot(d, f):
        return kv_out.at[around(z, d, ZS) * CS + c, f]

    def over(d, f):
        k = (d + 4) * OWNED + f
        copy = remote(slot(d, f), slot(d, f), ps.at[k], pr.at[k], other, x)
        copy.start()
        sent.append(copy)

    def go_right(k, f):
        k_f = k * OWNED + f
        copy = remote(slot(-k, f), slot(-k, f), rs.at[k_f], rr.at[k_f], right, x)
        copy.start()
        sent.append(copy)

    def go_left(k, f):
        k_f = k * OWNED + f
        copy = remote(slot(k, f), slot(k, f), ls.at[k_f], lr.at[k_f], left, x)
        copy.start()
        sent.append(copy)

    for f in range(OWNED):
        go_right(0, f)
        go_left(0, f)
    for f in range(OWNED):
        over(0, f)

    half(1)

    for k in range(4):
        for f in range(OWNED):
            k_f = k * OWNED + f
            came = slot(-1 - k, f)
            remote(came, came, rs.at[k_f], rr.at[k_f], right, x).wait_recv()
            if k < 3:
                go_right(k + 1, f)
            over(-1 - k, f)
            if k < 3:
                came = slot(1 + k, f)
                remote(came, came, ls.at[k_f], lr.at[k_f], left, x).wait_recv()
                if k < 2:
                    go_left(k + 1, f)
                over(1 + k, f)
    for copy in moved:
        copy.wait_recv()
    for d in range(-4, 4):
        for f in range(OWNED):
            came = kv_out.at[around(z, d, ZS) * CS + 1 - c, f]
            k = (d + 4) * OWNED + f
            remote(came, came, ps.at[k], pr.at[k], other, x).wait_recv()

    for copy in stat_x + [copy for _, copy in bulk] + stat_y + stat_z + key_moved + moved + sent:
        copy.wait_send()


def item_kernel(
    q_in, kv_in, table_in, train_in, wqkv_in, wout_in, out,
    table, train, wqkv, wout, in_sem,
    qp, kvp, kvc, bias, stack, tops, totals, accs, every, chosen,
):
    row, x, y, z, c = position()
    loads = [
        pltpu.make_async_copy(source, target, in_sem.at[i])
        for i, (source, target) in enumerate(
            ((wqkv_in, wqkv), (table_in, table), (train_in, train), (wout_in, wout))
        )
    ]
    for load in loads:
        load.start()
    kvc[...] = jnp.zeros_like(kvc)
    for load in loads:
        load.wait()

    def project_q(i, none):
        part = q_in[i].reshape(OWNED * GROUP, WIDTH)
        got = jnp.dot(part, wqkv[:, :WIDTH], preferred_element_type=F32)
        qp[i] = (got * SCALE).astype(BF16).reshape(OWNED, GROUP, WIDTH)
        return none

    lax.fori_loop(0, OWNERS, project_q, 0, unroll=4)

    def project_kv(i, none):
        part = kv_in[i].reshape(OWNED * KEYS, WIDTH)
        got = jnp.dot(part, wqkv[:, WIDTH:], preferred_element_type=F32)
        kvp[i] = got.astype(BF16).reshape(OWNED, KEYS, 2 * WIDTH)
        return none

    lax.fori_loop(0, PLACES, project_kv, 0, unroll=4)

    group = (iota((OWNERS, BLOCK), 1) // GROUP == iota((OWNERS, BLOCK), 0) // KEEP)
    spread = train[...].astype(F32)[:, None, :] * group.astype(F32)[None]
    counts = jnp.dot(
        spread.reshape(BLOCKS * OWNERS, BLOCK).astype(BF16),
        jnp.ones((BLOCK, WIDTH), BF16),
        preferred_element_type=F32,
    )
    number = (iota((BLOCKS * OWNERS, WIDTH), 0) % KEEP).astype(F32)
    every[...] = jnp.where(number < counts, 0.0, MASKED)
    head = iota((BLOCK, WIDTH), 1) // HEAD_DIM

    def one_block(yy, none):
        mine = table[row_of(yy, z, c)]

        n = jnp.int32(0)
        for j in range(BLOCKS):
            chosen[n] = j
            n = n + jnp.where(table[j] == mine, 1, 0)

        def gather(i, none):
            j = chosen[i]
            at = pl.multiple_of(i * 16, 16)
            come = pl.multiple_of(lax.div(j, PLACES) * 16, 16)
            for f in range(OWNED):
                kvc[f, pl.ds(at, 16), :] = kvp[lax.rem(j, PLACES), f, pl.ds(come, 16), :]
            bias[pl.ds(at, 16), :] = every[pl.ds(pl.multiple_of(j * 16, 16), 16), :]
            return none

        lax.fori_loop(0, n, gather, 0)
        tiles = lax.div(n + 15, 16)

        def tail(i, none):
            bias[pl.ds(pl.multiple_of(i * 16, 16), 16), :] = jnp.full((16, WIDTH), MASKED, F32)
            return none

        lax.fori_loop(n, tiles * 16, tail, 0)

        for f in range(OWNED):
            query = jnp.concatenate([qp[yy * XS + xx, f] for xx in range(XS)], axis=0)
            stack[f] = jnp.concatenate(
                [jnp.where(head == h, query, jnp.zeros_like(query)) for h in range(HEADS)],
                axis=0,
            )
        def first_tile():
            mask = jnp.concatenate([bias[0:TILE, :]] * HEADS, axis=1)
            for f in range(OWNED):
                scores = lax.dot_general(
                    kvc[f, 0:TILE, 0:WIDTH],
                    stack[f],
                    (((1,), (1,)), ((), ())),
                    preferred_element_type=F32,
                )
                scores = scores + mask
                top = jnp.max(scores, axis=0, keepdims=True)
                shares = jnp.exp2(scores - top)
                tops[f] = top
                totals[f] = jnp.sum(shares, axis=0, keepdims=True)
                got = lax.dot_general(
                    kvc[f, 0:TILE, WIDTH:],
                    shares.astype(BF16),
                    (((0,), (0,)), ((), ())),
                    preferred_element_type=F32,
                )
                for h in range(HEADS):
                    rows = slice(h * HEAD_DIM, (h + 1) * HEAD_DIM)
                    cols = slice(h * BLOCK, (h + 1) * BLOCK)
                    accs[f, rows, :] = got[rows, cols]

        first_tile()
        def one_tile(kt, none):
            at = pl.multiple_of(kt * TILE, TILE)
            mask = bias[pl.ds(at, TILE), :]
            mask = jnp.concatenate([mask] * HEADS, axis=1)
            for f in range(OWNED):
                top = tops[f]
                scores = lax.dot_general(
                    kvc[f, pl.ds(at, TILE), 0:WIDTH],
                    stack[f],
                    (((1,), (1,)), ((), ())),
                    preferred_element_type=F32,
                )
                scores = scores + mask
                new_top = jnp.maximum(top, jnp.max(scores, axis=0, keepdims=True))
                shares = jnp.exp2(scores - new_top)
                fade = jnp.exp2(top - new_top)
                tops[f] = new_top
                totals[f] = totals[f] * fade + jnp.sum(shares, axis=0, keepdims=True)
                got = lax.dot_general(
                    kvc[f, pl.ds(at, TILE), WIDTH:],
                    shares.astype(BF16),
                    (((0,), (0,)), ((), ())),
                    preferred_element_type=F32,
                )
                for h in range(HEADS):
                    rows = slice(h * HEAD_DIM, (h + 1) * HEAD_DIM)
                    cols = slice(h * BLOCK, (h + 1) * BLOCK)
                    accs[f, rows, :] = accs[f, rows, :] * fade[:, cols] + got[rows, cols]
            return none

        lax.fori_loop(1, tiles, one_tile, 0)
        for f in range(OWNED):
            total = totals[f]
            attended = jnp.concatenate(
                [
                    accs[f, h * HEAD_DIM : (h + 1) * HEAD_DIM, :]
                    * (1.0 / total[:, h * BLOCK : (h + 1) * BLOCK])
                    for h in range(HEADS)
                ],
                axis=0,
            ).astype(BF16)
            got = lax.dot_general(
                attended, wout[...], (((0,), (0,)), ((), ())), preferred_element_type=F32
            )
            for xx in range(XS):
                mixed = q_in[yy * XS + xx, f].astype(F32)
                out[yy * XS + xx, f] = (mixed + got[xx * GROUP : (xx + 1) * GROUP]).astype(BF16)
        return none

    lax.fori_loop(0, YS, one_block, 0)


def back_kernel(done, out, landed, wide, send_sems, recv_sems, own_sem):
    row, x, y, z, c = position()
    owner = y * XS + x
    barrier = pltpu.get_barrier_semaphore()
    steps = [(dy, dx) for dy in range(YS) for dx in range(XS) if dx or dy]
    steps.sort(key=lambda step: min(step[0], YS - step[0]) + min(step[1], XS - step[1]))
    for dy, dx in steps:
        peer = (row_of(around(y, dy, YS), z, c), around(x, dx, XS))
        pl.semaphore_signal(barrier, inc=1, device_id=peer, device_id_type=MESH)
    keep = pltpu.make_async_copy(done.at[owner], landed.at[owner], own_sem.at[0])
    keep.start()
    pl.semaphore_wait(barrier, OWNERS - 1)
    sent = []
    for dy, dx in steps:
        k = dy * XS + dx
        ty, tx = around(y, dy, YS), around(x, dx, XS)
        copy = remote(
            done.at[ty * XS + tx],
            landed.at[owner],
            send_sems.at[k],
            recv_sems.at[k],
            row_of(ty, z, c),
            tx,
        )
        copy.start()
        sent.append(copy)

    def place(g):
        for f in range(OWNED):
            wide[pl.ds(g * OWNED + f, GROUP, stride=FEATS), :] = landed[g, f].astype(F32)

    keep.wait()
    place(owner)
    for dy, dx in steps:
        k = dy * XS + dx
        g = around(y, -dy, YS) * XS + around(x, -dx, XS)
        remote(landed.at[g], landed.at[g], send_sems.at[k], recv_sems.at[k], row, x).wait_recv()
        place(g)

    def finish(i, none):
        some = wide[pl.ds(pl.multiple_of(i * 4 * FEATS, 64), 4 * FEATS), :]
        out[pl.ds(i * 4, 4)] = some.reshape(4, FEATS, WIDTH).astype(BF16)
        return none

    lax.fori_loop(0, GROUP // 4, finish, 0, unroll=2)
    for copy in sent:
        copy.wait_send()


def item_call(query, key, block_table, train, item_qkv, item_out):
    moved = jax.ShapeDtypeStruct((OWNERS, OWNED, GROUP, WIDTH), BF16)
    return pl.pallas_call(
        item_kernel,
        name="item",
        out_shape=moved,
        in_specs=[VMEM, VMEM, HBM, HBM, HBM, HBM],
        out_specs=VMEM,
        scratch_shapes=[
            pltpu.SMEM((BLOCKS,), jnp.int32),
            pltpu.VMEM((BLOCKS, BLOCK), jnp.int32),
            pltpu.VMEM((WIDTH, 3 * WIDTH), BF16),
            pltpu.VMEM((WIDTH, WIDTH), BF16),
            pltpu.SemaphoreType.DMA((4,)),
            pltpu.VMEM((OWNERS, OWNED, GROUP, WIDTH), BF16),
            pltpu.VMEM((PLACES, OWNED, KEYS, 2 * WIDTH), BF16),
            pltpu.VMEM((OWNED, PLACES * KEYS, 2 * WIDTH), BF16),
            pltpu.VMEM((PLACES * KEYS, WIDTH), F32),
            pltpu.VMEM((OWNED, HEADS * BLOCK, WIDTH), BF16),
            pltpu.VMEM((OWNED, 1, HEADS * BLOCK), F32),
            pltpu.VMEM((OWNED, 1, HEADS * BLOCK), F32),
            pltpu.VMEM((OWNED, WIDTH, BLOCK), F32),
            pltpu.VMEM((PLACES * KEYS, WIDTH), F32),
            pltpu.SMEM((BLOCKS + 8,), jnp.int32),
        ],
        compiler_params=pltpu.CompilerParams(vmem_limit_bytes=ITEM_VMEM),
    )(query, key, *stay(block_table, train, item_qkv, item_out))


def on_device(cells, block_table, row_live, row_train, feat_qkv, feat_out, item_qkv, item_out):
    train = row_train.reshape(BLOCKS, BLOCK)
    live = row_live.reshape(BLOCKS, BLOCK)
    by_feature = jnp.transpose(cells, (1, 0, 2))
    dma = pltpu.SemaphoreType.DMA
    moved = jax.ShapeDtypeStruct((OWNERS, OWNED, GROUP, WIDTH), BF16)
    query, key = pl.pallas_call(
        mix_kernel,
        name="mix",
        out_shape=(moved, jax.ShapeDtypeStruct((PLACES, OWNED, KEYS, WIDTH), BF16)),
        in_specs=[HBM] * 6,
        out_specs=(VMEM, VMEM),
        scratch_shapes=[
            pltpu.SMEM((BLOCKS,), jnp.int32),
            pltpu.VMEM((BLOCKS, BLOCK), jnp.int32),
            pltpu.SMEM((BLOCKS * BLOCK,), jnp.int32),
            pltpu.VMEM((WIDTH, 3 * WIDTH), BF16),
            pltpu.VMEM((WIDTH, WIDTH), BF16),
            dma((5,)),
            pltpu.VMEM((SHARD, BLOCK, WIDTH), BF16),
            pltpu.VMEM((FEATS, GROUP, WIDTH), BF16),
            pltpu.VMEM((SHARD, WIDTH), F32),
            pltpu.VMEM((SHARD, WIDTH), F32),
            pltpu.VMEM((FEATS, WIDTH), F32),
            pltpu.VMEM((FEATS, WIDTH), F32),
            pltpu.VMEM((8, WIDTH), F32),
            pltpu.VMEM((XS, 8, WIDTH), F32),
            pltpu.VMEM((8, WIDTH), F32),
            pltpu.VMEM((YS * CS, 8, WIDTH), F32),
            pltpu.VMEM((2, YS * CS, WIDTH), F32),
            pltpu.VMEM((ZS, 2, YS * CS, WIDTH), F32),
            pltpu.VMEM((BLOCKS, WIDTH), F32),
            pltpu.VMEM((GROUP * FEATS, WIDTH), F32),
            pltpu.VMEM((GROUP, FEATS, WIDTH), BF16),
            pltpu.VMEM((GROUP, FEATS, 3 * WIDTH), BF16),
            pltpu.VMEM((GROUP, FEATS, WIDTH), BF16),
            pltpu.VMEM((GROUP * FEATS, WIDTH), F32),
            pltpu.VMEM((FEATS, GROUP, WIDTH), BF16),
            pltpu.VMEM((FEATS * 8, WIDTH), F32),
            pltpu.VMEM((FEATS, 8, WIDTH), BF16),
            pltpu.VMEM((OWNERS, OWNED, 8, WIDTH), BF16),
            dma((2,)),
            dma((XS,)), dma((XS,)), dma((XS,)), dma((XS,)),
            dma((8,)), dma((8,)), dma((8,)), dma((8,)),
            dma((OWNERS,)), dma((OWNERS,)), dma((2 * OWNERS,)), dma((2 * OWNERS,)),
            dma((4 * OWNED,)), dma((4 * OWNED,)), dma((3 * OWNED,)), dma((3 * OWNED,)),
            dma((8 * OWNED,)), dma((8 * OWNED,)),
        ],
        compiler_params=pltpu.CompilerParams(
            collective_id=0, has_side_effects=True, vmem_limit_bytes=MIX_VMEM
        ),
    )(*stay(by_feature, block_table, live, row_train, feat_qkv, feat_out))
    done = item_call(query, key, block_table, train, item_qkv, item_out)
    return pl.pallas_call(
        back_kernel,
        name="back",
        out_shape=jax.ShapeDtypeStruct((GROUP, FEATS, WIDTH), BF16),
        in_specs=[ANY],
        out_specs=VMEM,
        scratch_shapes=[
            pltpu.VMEM((OWNERS, OWNED, GROUP, WIDTH), BF16),
            pltpu.VMEM((GROUP * FEATS, WIDTH), F32),
            dma((OWNERS,)), dma((OWNERS,)), dma((1,)),
        ],
        compiler_params=pltpu.CompilerParams(
            collective_id=1, has_side_effects=True, vmem_limit_bytes=BACK_VMEM
        ),
    )(done)


def solution(mesh):
    return jax.shard_map(
        on_device,
        mesh=mesh,
        in_specs=(P("rows", "feat", None), P(), P(), P(), P(), P(), P(), P()),
        out_specs=P(("rows", "feat"), None, None),
        check_vma=False,
    )
```

```python
import jax
import jax.numpy as jnp
from jax import lax
from jax.experimental import pallas as pl
from jax.experimental.pallas import tpu as pltpu
from jax.sharding import PartitionSpec as P

HEADS = 4
HEAD_DIM = 32
WIDTH = 128
KEEP = 4
XS, YS, ZS, CS = 4, 4, 8, 2
BLOCKS = YS * ZS * CS
BLOCK = 128
FEATS = 80
SHARD = 20
OWNED = 5
GROUP = 32
OWNERS = XS * YS
PLACES = ZS * CS
KEYS = YS * XS * KEEP
TILE = 256
EPSILON = 1e-05
MASKED = -1e30
SCALE = HEAD_DIM**-0.5 * 1.4426950408889634
MESH = pl.DeviceIdType.MESH
MIX_VMEM = 20 << 20
ITEM_VMEM = 20 << 20
BACK_VMEM = 12 << 20
F32 = jnp.float32
BF16 = jnp.bfloat16
VMEM = pl.BlockSpec(memory_space=pltpu.VMEM)
SMEM = pl.BlockSpec(memory_space=pltpu.SMEM)
ANY = pl.BlockSpec(memory_space=pl.ANY)
HBM = pl.BlockSpec(memory_space=pltpu.HBM)


def iota(shape, dim):
    return lax.broadcasted_iota(jnp.int32, shape, dim)


def row_of(y, z, c):
    return y * (ZS * CS) + z * CS + c


def around(at, step, size):
    return lax.rem(at + step + size, size)


def remote(source, target, send, recv, row, feat):
    return pltpu.make_async_remote_copy(
        src_ref=source,
        dst_ref=target,
        send_sem=send,
        recv_sem=recv,
        device_id=(row, feat),
        device_id_type=MESH,
    )


def stay(*arrays):
    return [pltpu.with_memory_space_constraint(a, pltpu.HBM) for a in arrays]


def position():
    row = lax.axis_index("rows")
    x = lax.axis_index("feat")
    y = lax.div(row, ZS * CS)
    z = lax.rem(lax.div(row, CS), ZS)
    c = lax.rem(row, CS)
    return row, x, y, z, c


def mix_kernel(
    cells, table_in, live_in, train_in, wqkv_in, wout_in, q_out, kv_out,
    table, live, train, wqkv, wout, in_sem, own, xbuf, part, level, mean_of, inv_of, st_src, sx, sy_src, sy, sz_src, sz, counts, nrm, rows, qkv, att, mix, send,
    key_wide, key_send, key_in,
    own_sem, xs, xr, ss, sr, ys, yr, zs, zr, ks, kr, qs, qr, rs, rr, ls, lr, ps, pr,
):
    row, x, y, z, c = position()
    owner = y * XS + x

    fetch = pltpu.make_async_copy(cells, own, own_sem.at[0])
    fetch.start()
    loads = [
        pltpu.make_async_copy(source, target, in_sem.at[i])
        for i, (source, target) in enumerate(
            ((live_in, live), (table_in, table), (train_in, train), (wqkv_in, wqkv), (wout_in, wout))
        )
    ]
    for load in loads:
        load.start()
    barrier = pltpu.get_barrier_semaphore()
    greet = []
    for dy in range(YS):
        for dx in range(XS):
            if dx or dy:
                greet.append((row_of(around(y, dy, YS), z, c), around(x, dx, XS)))
        greet.append((row_of(around(y, dy, YS), z, 1 - c), x))
    for dz in range(1, ZS):
        greet.append((row_of(y, around(z, dz, ZS), c), x))
    for peer in greet:
        pl.semaphore_signal(barrier, inc=1, device_id=peer, device_id_type=MESH)
    fetch.wait()
    for load in loads:
        load.wait()

    square = iota((BLOCK, WIDTH), 0) == iota((BLOCK, WIDTH), 1)
    flags = live[pl.ds(row, 1), :].astype(F32)
    weight = jnp.broadcast_to(
        jnp.sum(jnp.where(square, flags, 0.0), axis=1, keepdims=True), (BLOCK, WIDTH)
    )
    entries = jnp.broadcast_to(jnp.sum(flags, axis=1, keepdims=True) * WIDTH, (SHARD, WIDTH))

    def add_first(f, none):
        part[pl.ds(f, 1), :] = jnp.sum(own[f].astype(F32) * weight, axis=0, keepdims=True)
        return none

    lax.fori_loop(0, SHARD, add_first, 0, unroll=4)
    first = jnp.sum(part[...], axis=1, keepdims=True)
    level[...] = jnp.broadcast_to(first, (SHARD, WIDTH)) / entries

    def add_second(f, none):
        off = own[f].astype(F32) - level[pl.ds(f, 1), :]
        part[pl.ds(f, 1), :] = jnp.sum(off * off * weight, axis=0, keepdims=True)
        return none

    lax.fori_loop(0, SHARD, add_second, 0, unroll=4)
    second = jnp.sum(part[...], axis=1, keepdims=True)
    lane = iota((SHARD, WIDTH), 1)
    sub = iota((SHARD, WIDTH), 0)
    spot = lane == sub + GROUP * x

    def to_row(column):
        return jnp.sum(jnp.where(spot, column, 0.0), axis=0, keepdims=True)

    st_src[...] = jnp.concatenate(
        [to_row(first), to_row(second), jnp.zeros((6, WIDTH), F32)], axis=0
    )
    counts[...] = WIDTH * jnp.dot(
        live[...].astype(F32).astype(BF16),
        jnp.ones((BLOCK, WIDTH), BF16),
        preferred_element_type=F32,
    )
    key_wide[...] = jnp.zeros_like(key_wide)
    pl.semaphore_wait(barrier, len(greet))

    stat_x = []
    for d in range(1, XS):
        copy = remote(st_src, sx.at[x], ss.at[d], sr.at[d], row, around(x, d, XS))
        copy.start()
        stat_x.append(copy)
    bulk = []
    for d in (1, 3, 2):
        to = around(x, d, XS)
        copy = remote(
            cells.at[:, pl.ds(pl.multiple_of(to * GROUP, GROUP), GROUP)],
            xbuf.at[pl.ds(x * SHARD, SHARD)],
            xs.at[d],
            xr.at[d],
            row,
            to,
        )
        copy.start()
        bulk.append((d, copy))
    keep = pltpu.make_async_copy(
        own.at[:, pl.ds(pl.multiple_of(x * GROUP, GROUP), GROUP)],
        xbuf.at[pl.ds(x * SHARD, SHARD)],
        own_sem.at[1],
    )
    keep.start()
    sx[x] = st_src[...]
    for d in range(1, XS):
        came = around(x, -d, XS)
        remote(st_src, sx.at[came], ss.at[d], sr.at[d], row, x).wait_recv()
    merged = sx[0] + sx[1] + sx[2] + sx[3]
    sy_src[...] = merged
    here = y * CS + c
    sy[here] = merged
    stat_y = []
    for dy in range(YS):
        for dc in range(CS):
            if dy or dc:
                k = dy * CS + dc
                to = row_of(around(y, dy, YS), z, around(c, dc, CS))
                copy = remote(sy_src, sy.at[here], ys.at[k], yr.at[k], to, x)
                copy.start()
                stat_y.append(copy)
    for dy in range(YS):
        for dc in range(CS):
            if dy or dc:
                k = dy * CS + dc
                came = around(y, -dy, YS) * CS + around(c, dc, CS)
                remote(sy_src, sy.at[came], ys.at[k], yr.at[k], row, x).wait_recv()
    for k in range(2):
        tile = jnp.concatenate([sy[i, k : k + 1, :] for i in range(YS * CS)], axis=0)
        sz_src[k] = tile
        sz[z, k] = tile
    stat_z = []
    for d in range(1, ZS):
        copy = remote(
            sz_src, sz.at[z], zs.at[d], zr.at[d], row_of(y, around(z, d, ZS), c), x
        )
        copy.start()
        stat_z.append(copy)
    spots = [jnp.int32(0)] * KEEP
    seen = jnp.int32(0)
    for r in range(GROUP):
        flag = train[row * BLOCK + x * GROUP + r]
        for j in range(KEEP):
            spots[j] = jnp.where((flag == 1) & (seen == j), r, spots[j])
        seen = seen + flag
    mine = table[row]
    weights = [jnp.where(table[b] == mine, 1.0, 0.0).astype(F32) for b in range(BLOCKS)]
    entries_all = jnp.zeros((1, WIDTH), F32)
    for b in range(BLOCKS):
        entries_all = entries_all + weights[b] * counts[b : b + 1, :]
    for d in range(1, ZS):
        came = around(z, -d, ZS)
        remote(sz_src, sz.at[came], zs.at[d], zr.at[d], row, x).wait_recv()

    places = [
        (zz, i, row_of(i // CS, zz, i % CS)) for zz in range(ZS) for i in range(YS * CS)
    ]
    acc = jnp.zeros((1, WIDTH), F32)
    for zz, i, b in places:
        acc = acc + weights[b] * sz[zz, 0, i : i + 1, :]
    mean_row = acc / entries_all
    spread = jnp.zeros((1, WIDTH), F32)
    for zz, i, b in places:
        entries_b = counts[b : b + 1, :]
        off = sz[zz, 0, i : i + 1, :] / entries_b - mean_row
        spread = spread + weights[b] * (sz[zz, 1, i : i + 1, :] + entries_b * (off * off))
    inv_row = lax.rsqrt(spread / entries_all + EPSILON)

    for d, _ in bulk:
        came = xbuf.at[pl.ds(around(x, -d, XS) * SHARD, SHARD)]
        remote(came, came, xs.at[d], xr.at[d], row, x).wait_recv()
    keep.wait()
    for s in range(XS):
        pick = lane == sub + GROUP * s
        for ref, values in ((mean_of, mean_row), (inv_of, inv_row)):
            column = jnp.sum(jnp.where(pick, values, 0.0), axis=1, keepdims=True)
            ref[SHARD * s : SHARD * (s + 1), :] = jnp.broadcast_to(column, (SHARD, WIDTH))

    def norm(f, none):
        value = (xbuf[f].astype(F32) - mean_of[pl.ds(f, 1), :]) * inv_of[pl.ds(f, 1), :]
        nrm[pl.ds(pl.multiple_of(f * GROUP, GROUP), GROUP), :] = value.astype(BF16).astype(F32)
        return none

    lax.fori_loop(0, FEATS, norm, 0, unroll=4)

    def by_row(r, none):
        rows[r] = nrm[pl.ds(r, FEATS, stride=GROUP), :].astype(BF16)
        return none

    lax.fori_loop(0, GROUP, by_row, 0, unroll=4)

    def project(i, none):
        some = rows[pl.ds(i * 4, 4)].reshape(4 * FEATS, WIDTH)
        out = jnp.dot(some, wqkv[...], preferred_element_type=F32)
        qkv[pl.ds(i * 4, 4), :, 0:WIDTH] = (
            (out[:, :WIDTH] * SCALE).astype(BF16).reshape(4, FEATS, WIDTH)
        )
        qkv[pl.ds(i * 4, 4), :, WIDTH:] = (
            out[:, WIDTH:].astype(BF16).reshape(4, FEATS, 2 * WIDTH)
        )
        return none

    lax.fori_loop(0, GROUP // 4, project, 0)

    head = iota((FEATS, WIDTH), 1) // HEAD_DIM
    def attended(r):
        query = qkv[r, :, 0:WIDTH]
        key = qkv[r, :, WIDTH : 2 * WIDTH]
        value = qkv[r, :, 2 * WIDTH :]
        keys = jnp.concatenate(
            [jnp.where(head == h, key, jnp.zeros_like(key)) for h in range(HEADS)], axis=0
        )
        values = jnp.concatenate(
            [jnp.where(head == h, value, jnp.zeros_like(value)) for h in range(HEADS)], axis=0
        )
        scores = lax.dot_general(
            keys, query, (((1,), (1,)), ((), ())), preferred_element_type=F32
        )
        shares = []
        for h in range(HEADS):
            some = scores[h * FEATS : (h + 1) * FEATS]
            some = jnp.exp2(some - jnp.max(some, axis=0, keepdims=True))
            shares.append((some * (1.0 / jnp.sum(some, axis=0, keepdims=True))).astype(BF16))
        return lax.dot_general(
            jnp.concatenate(shares, axis=0),
            values,
            (((0,), (0,)), ((), ())),
            preferred_element_type=F32,
        ).astype(BF16)

    found = [attended(spot) for spot in spots]
    for j in range(KEEP):
        out = jnp.dot(found[j], wout[...], preferred_element_type=F32)
        out = out + rows[spots[j]].astype(F32)
        key_wide[pl.ds(KEEP * lax.rem(x, 2) + j, FEATS, stride=8), :] = out
    key_send[...] = key_wide[...].reshape(FEATS, 8, WIDTH).astype(BF16)
    peers = []
    for dy in range(YS):
        for dx in range(XS):
            if dx or dy:
                ty, tx = around(y, dy, YS), around(x, dx, XS)
                peers.append((dy * XS + dx, ty * XS + tx, row_of(ty, z, c), tx))
    sent = []
    key_moved = []
    for k, to, to_row, tx in peers:
        copy = remote(
            key_send.at[pl.ds(to * OWNED, OWNED)], key_in.at[owner], ks.at[k], kr.at[k], to_row, tx
        )
        copy.start()
        key_moved.append(copy)
    key_in[owner] = key_send[pl.ds(owner * OWNED, OWNED)]

    moved = []

    def half(part):
        first_row = part * (GROUP // 2)

        def attend(r, none):
            att[r] = attended(r)
            return none

        lax.fori_loop(first_row, first_row + GROUP // 2, attend, 0, unroll=16)

        def update(i, none):
            some = att[pl.ds(i * 4, 4)].reshape(4 * FEATS, WIDTH)
            out = jnp.dot(some, wout[...], preferred_element_type=F32)
            out = out + rows[pl.ds(i * 4, 4)].reshape(4 * FEATS, WIDTH).astype(F32)
            mix[pl.ds(i * 4 * FEATS, 4 * FEATS), :] = out
            return none

        lax.fori_loop(part * 4, part * 4 + 4, update, 0, unroll=2)

        def turn(f, none):
            send[f, first_row : first_row + GROUP // 2, :] = mix[
                pl.ds(first_row * FEATS + f, GROUP // 2, stride=FEATS), :
            ].astype(BF16)
            return none

        lax.fori_loop(0, FEATS, turn, 0, unroll=8)
        these = pl.ds(first_row, GROUP // 2)
        for k, to, to_row, tx in peers:
            copy = remote(
                send.at[pl.ds(to * OWNED, OWNED), these],
                q_out.at[owner, :, these],
                qs.at[part * OWNERS + k],
                qr.at[part * OWNERS + k],
                to_row,
                tx,
            )
            copy.start()
            moved.append(copy)
        q_out[owner, :, first_row : first_row + GROUP // 2, :] = send[
            pl.ds(owner * OWNED, OWNED), first_row : first_row + GROUP // 2, :
        ]

    half(0)

    for copy in key_moved:
        copy.wait_recv()
    spot_here = z * CS + c
    for yy in range(YS):
        for f in range(OWNED):
            low = key_in[yy * XS, f].astype(F32) + key_in[yy * XS + 1, f].astype(F32)
            high = key_in[yy * XS + 2, f].astype(F32) + key_in[yy * XS + 3, f].astype(F32)
            kv_out[spot_here, f, yy * 16 : yy * 16 + 16, :] = jnp.concatenate(
                [low, high], axis=0
            ).astype(BF16)

    right, left = row_of(y, around(z, 1, ZS), c), row_of(y, around(z, -1, ZS), c)
    other = row_of(y, z, 1 - c)

    def slot(d, f):
        return kv_out.at[around(z, d, ZS) * CS + c, f]

    def over(d, f):
        k = (d + 4) * OWNED + f
        copy = remote(slot(d, f), slot(d, f), ps.at[k], pr.at[k], other, x)
        copy.start()
        sent.append(copy)

    def go_right(k, f):
        k_f = k * OWNED + f
        copy = remote(slot(-k, f), slot(-k, f), rs.at[k_f], rr.at[k_f], right, x)
        copy.start()
        sent.append(copy)

    def go_left(k, f):
        k_f = k * OWNED + f
        copy = remote(slot(k, f), slot(k, f), ls.at[k_f], lr.at[k_f], left, x)
        copy.start()
        sent.append(copy)

    for f in range(OWNED):
        go_right(0, f)
        go_left(0, f)
    for f in range(OWNED):
        over(0, f)

    half(1)

    for k in range(4):
        for f in range(OWNED):
            k_f = k * OWNED + f
            came = slot(-1 - k, f)
            remote(came, came, rs.at[k_f], rr.at[k_f], right, x).wait_recv()
            if k < 3:
                go_right(k + 1, f)
            over(-1 - k, f)
            if k < 3:
                came = slot(1 + k, f)
                remote(came, came, ls.at[k_f], lr.at[k_f], left, x).wait_recv()
                if k < 2:
                    go_left(k + 1, f)
                over(1 + k, f)
    for copy in moved:
        copy.wait_recv()
    for d in range(-4, 4):
        for f in range(OWNED):
            came = kv_out.at[around(z, d, ZS) * CS + 1 - c, f]
            k = (d + 4) * OWNED + f
            remote(came, came, ps.at[k], pr.at[k], other, x).wait_recv()

    for copy in stat_x + [copy for _, copy in bulk] + stat_y + stat_z + key_moved + moved + sent:
        copy.wait_send()


def attend_tile(key, value, stacked, mask, top, total, acc):
    scores = lax.dot_general(
        key, stacked, (((1,), (1,)), ((), ())), preferred_element_type=F32
    )
    scores = scores + mask
    new_top = jnp.maximum(top, jnp.max(scores, axis=0, keepdims=True))
    shares = jnp.exp2(scores - new_top)
    fade = jnp.exp2(top - new_top)
    total = total * fade + jnp.sum(shares, axis=0, keepdims=True)
    got = lax.dot_general(
        value, shares.astype(BF16), (((0,), (0,)), ((), ())), preferred_element_type=F32
    )
    parts = []
    for h in range(HEADS):
        rows = slice(h * HEAD_DIM, (h + 1) * HEAD_DIM)
        cols = slice(h * BLOCK, (h + 1) * BLOCK)
        parts.append(acc[rows] * fade[:, cols] + got[rows, cols])
    return new_top, total, jnp.concatenate(parts, axis=0)


def stack_heads(query):
    head = iota((BLOCK, WIDTH), 1) // HEAD_DIM
    return jnp.concatenate(
        [jnp.where(head == h, query, jnp.zeros_like(query)) for h in range(HEADS)], axis=0
    )


def list_kernel(
    q_in, kv_in, table_in, train_in, wqkv_in,
    qp, kv_first, bias_first, tops, totals, accs,
    table, train, wqkv, in_sem, kvp, kv_more, bias_more, every, chosen,
):
    row, x, y, z, c = position()
    loads = [
        pltpu.make_async_copy(source, target, in_sem.at[i])
        for i, (source, target) in enumerate(
            ((wqkv_in, wqkv), (table_in, table), (train_in, train))
        )
    ]
    for load in loads:
        load.start()
    tops[...] = jnp.full_like(tops, MASKED)
    totals[...] = jnp.zeros_like(totals)
    accs[...] = jnp.zeros_like(accs)
    for load in loads:
        load.wait()

    def project_q(i, none):
        part = q_in[i].reshape(OWNED * GROUP, WIDTH)
        got = jnp.dot(part, wqkv[:, :WIDTH], preferred_element_type=F32)
        qp[i] = (got * SCALE).astype(BF16).reshape(OWNED, GROUP, WIDTH)
        return none

    lax.fori_loop(0, OWNERS, project_q, 0, unroll=4)

    def project_kv(i, none):
        part = kv_in[i].reshape(OWNED * KEYS, WIDTH)
        got = jnp.dot(part, wqkv[:, WIDTH:], preferred_element_type=F32)
        kvp[i] = got.astype(BF16).reshape(OWNED, KEYS, 2 * WIDTH)
        return none

    lax.fori_loop(0, PLACES, project_kv, 0, unroll=4)

    group = (iota((OWNERS, BLOCK), 1) // GROUP == iota((OWNERS, BLOCK), 0) // KEEP)
    spread = train[...].astype(F32)[:, None, :] * group.astype(F32)[None]
    counts = jnp.dot(
        spread.reshape(BLOCKS * OWNERS, BLOCK).astype(BF16),
        jnp.ones((BLOCK, WIDTH), BF16),
        preferred_element_type=F32,
    )
    number = (iota((BLOCKS * OWNERS, WIDTH), 0) % KEEP).astype(F32)
    every[...] = jnp.where(number < counts, 0.0, MASKED)
    nothing = jnp.zeros((16, 2 * WIDTH), BF16)
    masked = jnp.full((16, WIDTH), MASKED, F32)

    def one_block(yy, none):
        mine = table[row_of(yy, z, c)]
        n = jnp.int32(0)
        for j in range(BLOCKS):
            chosen[n] = j
            n = n + jnp.where(table[j] == mine, 1, 0)
        tiles = lax.div(n + 15, 16)

        def gather(i, none):
            j = chosen[i]
            at = pl.multiple_of(i * 16, 16)
            come = pl.multiple_of(lax.div(j, PLACES) * 16, 16)
            for f in range(OWNED):
                kv_first[yy, f, pl.ds(at, 16), :] = kvp[lax.rem(j, PLACES), f, pl.ds(come, 16), :]
            bias_first[yy, pl.ds(at, 16), :] = every[pl.ds(pl.multiple_of(j * 16, 16), 16), :]
            return none

        lax.fori_loop(0, jnp.minimum(n, 16), gather, 0)

        def tail(i, none):
            at = pl.multiple_of(i * 16, 16)
            for f in range(OWNED):
                kv_first[yy, f, pl.ds(at, 16), :] = nothing
            bias_first[yy, pl.ds(at, 16), :] = masked
            return none

        lax.fori_loop(jnp.minimum(n, 16), 16, tail, 0)

        @pl.when(tiles > 1)
        def _():
            def gather_more(i, none):
                j = chosen[i]
                at = pl.multiple_of((i - 16) * 16, 16)
                come = pl.multiple_of(lax.div(j, PLACES) * 16, 16)
                for f in range(OWNED):
                    kv_more[f, pl.ds(at, 16), :] = kvp[lax.rem(j, PLACES), f, pl.ds(come, 16), :]
                bias_more[pl.ds(at, 16), :] = every[pl.ds(pl.multiple_of(j * 16, 16), 16), :]
                return none

            lax.fori_loop(16, n, gather_more, 0)

            def tail_more(i, none):
                at = pl.multiple_of((i - 16) * 16, 16)
                for f in range(OWNED):
                    kv_more[f, pl.ds(at, 16), :] = nothing
                bias_more[pl.ds(at, 16), :] = masked
                return none

            lax.fori_loop(n, tiles * 16, tail_more, 0)

            def one_tile(kt, none):
                at = pl.multiple_of((kt - 1) * TILE, TILE)
                mask = jnp.concatenate([bias_more[pl.ds(at, TILE), :]] * HEADS, axis=1)
                for f in range(OWNED):
                    query = jnp.concatenate([qp[yy * XS + xx, f] for xx in range(XS)], axis=0)
                    tops[yy, f], totals[yy, f], accs[yy, f] = attend_tile(
                        kv_more[f, pl.ds(at, TILE), 0:WIDTH],
                        kv_more[f, pl.ds(at, TILE), WIDTH:],
                        stack_heads(query),
                        mask,
                        tops[yy, f],
                        totals[yy, f],
                        accs[yy, f],
                    )
                return none

            lax.fori_loop(1, tiles, one_tile, 0)

        return none

    lax.fori_loop(0, YS, one_block, 0)


def back_kernel(
    q_in, qp, kv_first, bias_first, tops, totals, accs, wout_in, out,
    wout, done, landed, wide, send_sems, recv_sems, own_sem,
):
    row, x, y, z, c = position()
    owner = y * XS + x
    load = pltpu.make_async_copy(wout_in, wout, own_sem.at[0])
    load.start()
    barrier = pltpu.get_barrier_semaphore()
    for dy in range(YS):
        for dx in range(XS):
            if dx or dy:
                peer = (row_of(around(y, dy, YS), z, c), around(x, dx, XS))
                pl.semaphore_signal(barrier, inc=1, device_id=peer, device_id_type=MESH)
    load.wait()
    sent = []

    def place(g):
        for f in range(OWNED):
            wide[pl.ds(g * OWNED + f, GROUP, stride=FEATS), :] = landed[g, f].astype(F32)

    def take(dy):
        for dx in (1, 3, 2, 0):
            if dx or dy:
                k = dy * XS + dx
                g = around(y, -dy, YS) * XS + around(x, -dx, XS)
                remote(
                    landed.at[g], landed.at[g], send_sems.at[k], recv_sems.at[k], row, x
                ).wait_recv()
                place(g)

    order = (2, 1, 3, 0)
    for turn, dy in enumerate(order):
        yy = around(y, dy, YS)
        mask = jnp.concatenate([bias_first[yy]] * HEADS, axis=1)
        for f in range(OWNED):
            query = jnp.concatenate([qp[yy * XS + xx, f] for xx in range(XS)], axis=0)
            _, total, acc = attend_tile(
                kv_first[yy, f, :, 0:WIDTH],
                kv_first[yy, f, :, WIDTH:],
                stack_heads(query),
                mask,
                tops[yy, f],
                totals[yy, f],
                accs[yy, f],
            )
            attended = jnp.concatenate(
                [
                    acc[h * HEAD_DIM : (h + 1) * HEAD_DIM]
                    * (1.0 / total[:, h * BLOCK : (h + 1) * BLOCK])
                    for h in range(HEADS)
                ],
                axis=0,
            ).astype(BF16)
            got = lax.dot_general(
                attended, wout[...], (((0,), (0,)), ((), ())), preferred_element_type=F32
            )
            for xx in range(XS):
                mixed = q_in[yy * XS + xx, f].astype(F32)
                done[yy * XS + xx, f] = (mixed + got[xx * GROUP : (xx + 1) * GROUP]).astype(BF16)
        if turn == 0:
            pl.semaphore_wait(barrier, OWNERS - 1)
        for dx in (2, 1, 3, 0):
            if dx or dy:
                k = dy * XS + dx
                tx = around(x, dx, XS)
                copy = remote(
                    done.at[yy * XS + tx],
                    landed.at[owner],
                    send_sems.at[k],
                    recv_sems.at[k],
                    row_of(yy, z, c),
                    tx,
                )
                copy.start()
                sent.append(copy)
        if turn >= 2:
            take(order[turn - 2])
    landed[owner] = done[owner]
    place(owner)
    take(order[2])
    take(order[3])

    def finish(i, none):
        some = wide[pl.ds(pl.multiple_of(i * 4 * FEATS, 64), 4 * FEATS), :]
        out[pl.ds(i * 4, 4)] = some.reshape(4, FEATS, WIDTH).astype(BF16)
        return none

    lax.fori_loop(0, GROUP // 4, finish, 0, unroll=2)
    for copy in sent:
        copy.wait_send()


def list_call(query, key, block_table, train, item_qkv):
    shape = jax.ShapeDtypeStruct
    state = shape((YS, OWNED, 1, HEADS * BLOCK), F32)
    return pl.pallas_call(
        list_kernel,
        name="list",
        out_shape=(
            shape((OWNERS, OWNED, GROUP, WIDTH), BF16),
            shape((YS, OWNED, TILE, 2 * WIDTH), BF16),
            shape((YS, TILE, WIDTH), F32),
            state,
            state,
            shape((YS, OWNED, WIDTH, BLOCK), F32),
        ),
        in_specs=[VMEM, VMEM, HBM, HBM, HBM],
        out_specs=(VMEM,) * 6,
        scratch_shapes=[
            pltpu.SMEM((BLOCKS,), jnp.int32),
            pltpu.VMEM((BLOCKS, BLOCK), jnp.int32),
            pltpu.VMEM((WIDTH, 3 * WIDTH), BF16),
            pltpu.SemaphoreType.DMA((3,)),
            pltpu.VMEM((PLACES, OWNED, KEYS, 2 * WIDTH), BF16),
            pltpu.VMEM((OWNED, PLACES * KEYS, 2 * WIDTH), BF16),
            pltpu.VMEM((PLACES * KEYS, WIDTH), F32),
            pltpu.VMEM((PLACES * KEYS, WIDTH), F32),
            pltpu.SMEM((BLOCKS + 8,), jnp.int32),
        ],
        compiler_params=pltpu.CompilerParams(vmem_limit_bytes=ITEM_VMEM),
    )(query, key, *stay(block_table, train, item_qkv))


def on_device(cells, block_table, row_live, row_train, feat_qkv, feat_out, item_qkv, item_out):
    train = row_train.reshape(BLOCKS, BLOCK)
    live = row_live.reshape(BLOCKS, BLOCK)
    by_feature = jnp.transpose(cells, (1, 0, 2))
    dma = pltpu.SemaphoreType.DMA
    moved = jax.ShapeDtypeStruct((OWNERS, OWNED, GROUP, WIDTH), BF16)
    query, key = pl.pallas_call(
        mix_kernel,
        name="mix",
        out_shape=(moved, jax.ShapeDtypeStruct((PLACES, OWNED, KEYS, WIDTH), BF16)),
        in_specs=[HBM] * 6,
        out_specs=(VMEM, VMEM),
        scratch_shapes=[
            pltpu.SMEM((BLOCKS,), jnp.int32),
            pltpu.VMEM((BLOCKS, BLOCK), jnp.int32),
            pltpu.SMEM((BLOCKS * BLOCK,), jnp.int32),
            pltpu.VMEM((WIDTH, 3 * WIDTH), BF16),
            pltpu.VMEM((WIDTH, WIDTH), BF16),
            dma((5,)),
            pltpu.VMEM((SHARD, BLOCK, WIDTH), BF16),
            pltpu.VMEM((FEATS, GROUP, WIDTH), BF16),
            pltpu.VMEM((SHARD, WIDTH), F32),
            pltpu.VMEM((SHARD, WIDTH), F32),
            pltpu.VMEM((FEATS, WIDTH), F32),
            pltpu.VMEM((FEATS, WIDTH), F32),
            pltpu.VMEM((8, WIDTH), F32),
            pltpu.VMEM((XS, 8, WIDTH), F32),
            pltpu.VMEM((8, WIDTH), F32),
            pltpu.VMEM((YS * CS, 8, WIDTH), F32),
            pltpu.VMEM((2, YS * CS, WIDTH), F32),
            pltpu.VMEM((ZS, 2, YS * CS, WIDTH), F32),
            pltpu.VMEM((BLOCKS, WIDTH), F32),
            pltpu.VMEM((GROUP * FEATS, WIDTH), F32),
            pltpu.VMEM((GROUP, FEATS, WIDTH), BF16),
            pltpu.VMEM((GROUP, FEATS, 3 * WIDTH), BF16),
            pltpu.VMEM((GROUP, FEATS, WIDTH), BF16),
            pltpu.VMEM((GROUP * FEATS, WIDTH), F32),
            pltpu.VMEM((FEATS, GROUP, WIDTH), BF16),
            pltpu.VMEM((FEATS * 8, WIDTH), F32),
            pltpu.VMEM((FEATS, 8, WIDTH), BF16),
            pltpu.VMEM((OWNERS, OWNED, 8, WIDTH), BF16),
            dma((2,)),
            dma((XS,)), dma((XS,)), dma((XS,)), dma((XS,)),
            dma((8,)), dma((8,)), dma((8,)), dma((8,)),
            dma((OWNERS,)), dma((OWNERS,)), dma((2 * OWNERS,)), dma((2 * OWNERS,)),
            dma((4 * OWNED,)), dma((4 * OWNED,)), dma((3 * OWNED,)), dma((3 * OWNED,)),
            dma((8 * OWNED,)), dma((8 * OWNED,)),
        ],
        compiler_params=pltpu.CompilerParams(
            collective_id=0, has_side_effects=True, vmem_limit_bytes=MIX_VMEM
        ),
    )(*stay(by_feature, block_table, live, row_train, feat_qkv, feat_out))
    listed = list_call(query, key, block_table, train, item_qkv)
    return pl.pallas_call(
        back_kernel,
        name="back",
        out_shape=jax.ShapeDtypeStruct((GROUP, FEATS, WIDTH), BF16),
        in_specs=[VMEM] * 7 + [HBM],
        out_specs=VMEM,
        scratch_shapes=[
            pltpu.VMEM((WIDTH, WIDTH), BF16),
            pltpu.VMEM((OWNERS, OWNED, GROUP, WIDTH), BF16),
            pltpu.VMEM((OWNERS, OWNED, GROUP, WIDTH), BF16),
            pltpu.VMEM((GROUP * FEATS, WIDTH), F32),
            dma((OWNERS,)), dma((OWNERS,)), dma((1,)),
        ],
        compiler_params=pltpu.CompilerParams(
            collective_id=1, has_side_effects=True, vmem_limit_bytes=BACK_VMEM
        ),
    )(query, *listed, *stay(item_out))


def solution(mesh):
    return jax.shard_map(
        on_device,
        mesh=mesh,
        in_specs=(P("rows", "feat", None), P(), P(), P(), P(), P(), P(), P()),
        out_specs=P(("rows", "feat"), None, None),
        check_vma=False,
    )
```

```python
import jax
import jax.numpy as jnp
from jax import lax
from jax.experimental import pallas as pl
from jax.experimental.pallas import tpu as pltpu
from jax.sharding import PartitionSpec as P

HEADS = 4
HEAD_DIM = 32
WIDTH = 128
KEEP = 4
XS, YS, ZS, CS = 4, 4, 8, 2
BLOCKS = YS * ZS * CS
BLOCK = 128
FEATS = 80
SHARD = 20
OWNED = 5
GROUP = 32
OWNERS = XS * YS
PLACES = ZS * CS
KEYS = YS * XS * KEEP
TILE = 256
EPSILON = 1e-05
MASKED = -1e30
SCALE = HEAD_DIM**-0.5 * 1.4426950408889634
MESH = pl.DeviceIdType.MESH
CHUNKS = ((0, 1), (1, 1), (2, 1), (3, 1), (4, 1))
FROM_RIGHT = 3
MIX_VMEM = 20 << 20
ITEM_VMEM = 20 << 20
BACK_VMEM = 12 << 20
F32 = jnp.float32
BF16 = jnp.bfloat16
VMEM = pl.BlockSpec(memory_space=pltpu.VMEM)
SMEM = pl.BlockSpec(memory_space=pltpu.SMEM)
ANY = pl.BlockSpec(memory_space=pl.ANY)
HBM = pl.BlockSpec(memory_space=pltpu.HBM)


def iota(shape, dim):
    return lax.broadcasted_iota(jnp.int32, shape, dim)


def row_of(y, z, c):
    return y * (ZS * CS) + z * CS + c


def around(at, step, size):
    return lax.rem(at + step + size, size)


def remote(source, target, send, recv, row, feat):
    return pltpu.make_async_remote_copy(
        src_ref=source,
        dst_ref=target,
        send_sem=send,
        recv_sem=recv,
        device_id=(row, feat),
        device_id_type=MESH,
    )


def stay(*arrays):
    return [pltpu.with_memory_space_constraint(a, pltpu.HBM) for a in arrays]


def position():
    row = lax.axis_index("rows")
    x = lax.axis_index("feat")
    y = lax.div(row, ZS * CS)
    z = lax.rem(lax.div(row, CS), ZS)
    c = lax.rem(row, CS)
    return row, x, y, z, c


def mix_kernel(
    cells, table_in, live_in, train_in, wqkv_in, wout_in, q_out, kv_out,
    table, live, train, wqkv, wout, in_sem, own, xbuf, part, level, mean_of, inv_of, st_src, sxy, sz_src, sz, counts, nrm, rows, qkv, att, mix, send,
    key_wide, key_send, key_in,
    own_sem, xs, xr, ss, sr, zs, zr, ks, kr, qs, qr, rs, rr, ls, lr, ps, pr,
):
    row, x, y, z, c = position()
    owner = y * XS + x

    fetch = pltpu.make_async_copy(cells, own, own_sem.at[0])
    fetch.start()
    loads = [
        pltpu.make_async_copy(source, target, in_sem.at[i])
        for i, (source, target) in enumerate(
            ((live_in, live), (table_in, table), (train_in, train), (wqkv_in, wqkv), (wout_in, wout))
        )
    ]
    for load in loads:
        load.start()
    barrier = pltpu.get_barrier_semaphore()
    greet = []
    plane = [
        (dx, dy, dc) for dy in range(YS) for dc in range(CS) for dx in range(XS) if dx or dy or dc
    ]
    for dx, dy, dc in plane:
        greet.append((row_of(around(y, dy, YS), z, around(c, dc, CS)), around(x, dx, XS)))
    for dz in range(1, ZS):
        greet.append((row_of(y, around(z, dz, ZS), c), x))
    for peer in greet:
        pl.semaphore_signal(barrier, inc=1, device_id=peer, device_id_type=MESH)
    fetch.wait()
    for load in loads:
        load.wait()

    square = iota((BLOCK, WIDTH), 0) == iota((BLOCK, WIDTH), 1)
    flags = live[pl.ds(row, 1), :].astype(F32)
    weight = jnp.broadcast_to(
        jnp.sum(jnp.where(square, flags, 0.0), axis=1, keepdims=True), (BLOCK, WIDTH)
    )
    entries = jnp.broadcast_to(jnp.sum(flags, axis=1, keepdims=True) * WIDTH, (SHARD, WIDTH))

    def add_first(f, none):
        part[pl.ds(f, 1), :] = jnp.sum(own[f].astype(F32) * weight, axis=0, keepdims=True)
        return none

    lax.fori_loop(0, SHARD, add_first, 0, unroll=4)
    first = jnp.sum(part[...], axis=1, keepdims=True)
    level[...] = jnp.broadcast_to(first, (SHARD, WIDTH)) / entries

    def add_second(f, none):
        off = own[f].astype(F32) - level[pl.ds(f, 1), :]
        part[pl.ds(f, 1), :] = jnp.sum(off * off * weight, axis=0, keepdims=True)
        return none

    lax.fori_loop(0, SHARD, add_second, 0, unroll=4)
    second = jnp.sum(part[...], axis=1, keepdims=True)
    lane = iota((SHARD, WIDTH), 1)
    sub = iota((SHARD, WIDTH), 0)
    spot = lane == sub + GROUP * x

    def to_row(column):
        return jnp.sum(jnp.where(spot, column, 0.0), axis=0, keepdims=True)

    st_src[...] = jnp.concatenate(
        [to_row(first), to_row(second)], axis=0
    )
    counts[...] = WIDTH * jnp.dot(
        live[...].astype(F32).astype(BF16),
        jnp.ones((BLOCK, WIDTH), BF16),
        preferred_element_type=F32,
    )
    key_wide[...] = jnp.zeros_like(key_wide)
    pl.semaphore_wait(barrier, len(greet))

    here = y * CS + c
    stat_xy = []
    for dx, dy, dc in plane:
        k = (dy * CS + dc) * XS + dx
        to = row_of(around(y, dy, YS), z, around(c, dc, CS))
        copy = remote(st_src, sxy.at[here, x], ss.at[k], sr.at[k], to, around(x, dx, XS))
        copy.start()
        stat_xy.append(copy)
    bulk = []
    for d in (1, 3, 2):
        to = around(x, d, XS)
        copy = remote(
            cells.at[:, pl.ds(pl.multiple_of(to * GROUP, GROUP), GROUP)],
            xbuf.at[pl.ds(x * SHARD, SHARD)],
            xs.at[d],
            xr.at[d],
            row,
            to,
        )
        copy.start()
        bulk.append((d, copy))
    keep = pltpu.make_async_copy(
        own.at[:, pl.ds(pl.multiple_of(x * GROUP, GROUP), GROUP)],
        xbuf.at[pl.ds(x * SHARD, SHARD)],
        own_sem.at[1],
    )
    keep.start()
    sxy[here, x] = st_src[...]
    for dx, dy, dc in plane:
        k = (dy * CS + dc) * XS + dx
        came = sxy.at[around(y, -dy, YS) * CS + around(c, dc, CS), around(x, -dx, XS)]
        remote(came, came, ss.at[k], sr.at[k], row, x).wait_recv()
    merged = [
        sxy[i, 0] + sxy[i, 1] + sxy[i, 2] + sxy[i, 3] for i in range(YS * CS)
    ]
    for k in range(2):
        tile = jnp.concatenate([merged[i][k : k + 1] for i in range(YS * CS)], axis=0)
        sz_src[k] = tile
        sz[z, k] = tile
    stat_z = []
    for d in range(1, ZS):
        copy = remote(
            sz_src, sz.at[z], zs.at[d], zr.at[d], row_of(y, around(z, d, ZS), c), x
        )
        copy.start()
        stat_z.append(copy)
    spots = [jnp.int32(0)] * KEEP
    seen = jnp.int32(0)
    for r in range(GROUP):
        flag = train[row * BLOCK + x * GROUP + r]
        for j in range(KEEP):
            spots[j] = jnp.where((flag == 1) & (seen == j), r, spots[j])
        seen = seen + flag
    mine = table[row]
    weights = [jnp.where(table[b] == mine, 1.0, 0.0).astype(F32) for b in range(BLOCKS)]
    entries_all = jnp.zeros((1, WIDTH), F32)
    for b in range(BLOCKS):
        entries_all = entries_all + weights[b] * counts[b : b + 1, :]
    for d in range(1, ZS):
        came = around(z, -d, ZS)
        remote(sz_src, sz.at[came], zs.at[d], zr.at[d], row, x).wait_recv()

    places = [
        (zz, i, row_of(i // CS, zz, i % CS)) for zz in range(ZS) for i in range(YS * CS)
    ]
    acc = jnp.zeros((1, WIDTH), F32)
    for zz, i, b in places:
        acc = acc + weights[b] * sz[zz, 0, i : i + 1, :]
    mean_row = acc / entries_all
    spread = jnp.zeros((1, WIDTH), F32)
    for zz, i, b in places:
        entries_b = counts[b : b + 1, :]
        off = sz[zz, 0, i : i + 1, :] / entries_b - mean_row
        spread = spread + weights[b] * (sz[zz, 1, i : i + 1, :] + entries_b * (off * off))
    inv_row = lax.rsqrt(spread / entries_all + EPSILON)

    for d, _ in bulk:
        came = xbuf.at[pl.ds(around(x, -d, XS) * SHARD, SHARD)]
        remote(came, came, xs.at[d], xr.at[d], row, x).wait_recv()
    keep.wait()
    for s in range(XS):
        pick = lane == sub + GROUP * s
        for ref, values in ((mean_of, mean_row), (inv_of, inv_row)):
            column = jnp.sum(jnp.where(pick, values, 0.0), axis=1, keepdims=True)
            ref[SHARD * s : SHARD * (s + 1), :] = jnp.broadcast_to(column, (SHARD, WIDTH))

    def norm(f, none):
        value = (xbuf[f].astype(F32) - mean_of[pl.ds(f, 1), :]) * inv_of[pl.ds(f, 1), :]
        nrm[pl.ds(pl.multiple_of(f * GROUP, GROUP), GROUP), :] = value.astype(BF16).astype(F32)
        return none

    lax.fori_loop(0, FEATS, norm, 0, unroll=8)

    def by_row(r, none):
        rows[r] = nrm[pl.ds(r, FEATS, stride=GROUP), :].astype(BF16)
        return none

    lax.fori_loop(0, GROUP, by_row, 0, unroll=8)

    def project(i, none):
        some = rows[pl.ds(i * 4, 4)].reshape(4 * FEATS, WIDTH)
        out = jnp.dot(some, wqkv[...], preferred_element_type=F32)
        qkv[pl.ds(i * 4, 4), :, 0:WIDTH] = (
            (out[:, :WIDTH] * SCALE).astype(BF16).reshape(4, FEATS, WIDTH)
        )
        qkv[pl.ds(i * 4, 4), :, WIDTH:] = (
            out[:, WIDTH:].astype(BF16).reshape(4, FEATS, 2 * WIDTH)
        )
        return none

    lax.fori_loop(0, GROUP // 4, project, 0, unroll=4)

    head = iota((FEATS, WIDTH), 1) // HEAD_DIM
    def attended(r):
        query = qkv[r, :, 0:WIDTH]
        key = qkv[r, :, WIDTH : 2 * WIDTH]
        value = qkv[r, :, 2 * WIDTH :]
        keys = jnp.concatenate(
            [jnp.where(head == h, key, jnp.zeros_like(key)) for h in range(HEADS)], axis=0
        )
        values = jnp.concatenate(
            [jnp.where(head == h, value, jnp.zeros_like(value)) for h in range(HEADS)], axis=0
        )
        scores = lax.dot_general(
            keys, query, (((1,), (1,)), ((), ())), preferred_element_type=F32
        )
        shares = []
        for h in range(HEADS):
            some = scores[h * FEATS : (h + 1) * FEATS]
            some = jnp.exp2(some - jnp.max(some, axis=0, keepdims=True))
            shares.append((some * (1.0 / jnp.sum(some, axis=0, keepdims=True))).astype(BF16))
        return lax.dot_general(
            jnp.concatenate(shares, axis=0),
            values,
            (((0,), (0,)), ((), ())),
            preferred_element_type=F32,
        ).astype(BF16)

    found = [attended(spot) for spot in spots]
    for j in range(KEEP):
        out = jnp.dot(found[j], wout[...], preferred_element_type=F32)
        out = out + rows[spots[j]].astype(F32)
        key_wide[pl.ds(KEEP * lax.rem(x, 2) + j, FEATS, stride=8), :] = out
    key_send[...] = key_wide[...].reshape(FEATS, 8, WIDTH).astype(BF16)
    peers = []
    for dy in range(YS):
        for dx in range(XS):
            if dx or dy:
                ty, tx = around(y, dy, YS), around(x, dx, XS)
                peers.append((dy * XS + dx, ty * XS + tx, row_of(ty, z, c), tx))
    sent = []
    key_moved = []
    for k, to, to_row, tx in peers:
        copy = remote(
            key_send.at[pl.ds(to * OWNED, OWNED)], key_in.at[owner], ks.at[k], kr.at[k], to_row, tx
        )
        copy.start()
        key_moved.append(copy)
    key_in[owner] = key_send[pl.ds(owner * OWNED, OWNED)]

    moved = []

    def half(part):
        first_row = part * (GROUP // 2)

        def attend(r, none):
            att[r] = attended(r)
            return none

        lax.fori_loop(first_row, first_row + GROUP // 2, attend, 0, unroll=16)

        def update(i, none):
            some = att[pl.ds(i * 4, 4)].reshape(4 * FEATS, WIDTH)
            out = jnp.dot(some, wout[...], preferred_element_type=F32)
            out = out + rows[pl.ds(i * 4, 4)].reshape(4 * FEATS, WIDTH).astype(F32)
            mix[pl.ds(i * 4 * FEATS, 4 * FEATS), :] = out
            return none

        lax.fori_loop(part * 4, part * 4 + 4, update, 0, unroll=2)

        def turn(f, none):
            send[f, first_row : first_row + GROUP // 2, :] = mix[
                pl.ds(first_row * FEATS + f, GROUP // 2, stride=FEATS), :
            ].astype(BF16)
            return none

        lax.fori_loop(0, FEATS, turn, 0, unroll=8)
        these = pl.ds(first_row, GROUP // 2)
        for k, to, to_row, tx in peers:
            copy = remote(
                send.at[pl.ds(to * OWNED, OWNED), these],
                q_out.at[owner, :, these],
                qs.at[part * OWNERS + k],
                qr.at[part * OWNERS + k],
                to_row,
                tx,
            )
            copy.start()
            moved.append(copy)
        q_out[owner, :, first_row : first_row + GROUP // 2, :] = send[
            pl.ds(owner * OWNED, OWNED), first_row : first_row + GROUP // 2, :
        ]

    half(0)

    for copy in key_moved:
        copy.wait_recv()
    spot_here = z * CS + c
    for yy in range(YS):
        for f in range(OWNED):
            low = key_in[yy * XS, f].astype(F32) + key_in[yy * XS + 1, f].astype(F32)
            high = key_in[yy * XS + 2, f].astype(F32) + key_in[yy * XS + 3, f].astype(F32)
            kv_out[spot_here, f, yy * 16 : yy * 16 + 16, :] = jnp.concatenate(
                [low, high], axis=0
            ).astype(BF16)

    right, left = row_of(y, around(z, 1, ZS), c), row_of(y, around(z, -1, ZS), c)
    other = row_of(y, z, 1 - c)

    count = len(CHUNKS)

    def slot(d, i):
        return kv_out.at[around(z, d, ZS) * CS + c, pl.ds(CHUNKS[i][0], CHUNKS[i][1])]

    def hop(d, i, sems, k, to):
        send_sems, recv_sems = sems
        at = k * count + i
        copy = remote(slot(d, i), slot(d, i), send_sems.at[at], recv_sems.at[at], to, x)
        copy.start()
        sent.append(copy)

    def lands(d, i, sems, k, to):
        at = k * count + i
        remote(slot(d, i), slot(d, i), sems[0].at[at], sems[1].at[at], to, x).wait_recv()

    def over(d, i):
        hop(d, i, (ps, pr), d + 4, other)

    def on_right(k, i):
        return k < 3 or (k == 3 and i < FROM_RIGHT)

    def on_left(k, i):
        return k < 3 or (k == 3 and i >= FROM_RIGHT)

    for i in range(count):
        hop(0, i, (rs, rr), 0, right)
        hop(0, i, (ls, lr), 0, left)
    for i in range(count):
        over(0, i)

    half(1)

    for k in range(4):
        for i in range(count):
            if on_right(k, i):
                lands(-1 - k, i, (rs, rr), k, right)
                if on_right(k + 1, i):
                    hop(-1 - k, i, (rs, rr), k + 1, right)
                over(-1 - k, i)
            if on_left(k, i):
                lands(1 + k, i, (ls, lr), k, left)
                if on_left(k + 1, i):
                    hop(1 + k, i, (ls, lr), k + 1, left)
                over(1 + k if k < 3 else -4, i)
    for copy in moved:
        copy.wait_recv()
    for d in range(-4, 4):
        for i in range(count):
            came = kv_out.at[
                around(z, d, ZS) * CS + 1 - c, pl.ds(CHUNKS[i][0], CHUNKS[i][1])
            ]
            at = (d + 4) * count + i
            remote(came, came, ps.at[at], pr.at[at], other, x).wait_recv()

    for copy in stat_xy + [copy for _, copy in bulk] + stat_z + key_moved + moved + sent:
        copy.wait_send()


def attend_tile(key, value, stacked, mask, top, total, acc):
    scores = lax.dot_general(
        key, stacked, (((1,), (1,)), ((), ())), preferred_element_type=F32
    )
    scores = scores + mask
    new_top = jnp.maximum(top, jnp.max(scores, axis=0, keepdims=True))
    shares = jnp.exp2(scores - new_top)
    fade = jnp.exp2(top - new_top)
    total = total * fade + jnp.sum(shares, axis=0, keepdims=True)
    got = lax.dot_general(
        value, shares.astype(BF16), (((0,), (0,)), ((), ())), preferred_element_type=F32
    )
    parts = []
    for h in range(HEADS):
        rows = slice(h * HEAD_DIM, (h + 1) * HEAD_DIM)
        cols = slice(h * BLOCK, (h + 1) * BLOCK)
        parts.append(acc[rows] * fade[:, cols] + got[rows, cols])
    return new_top, total, jnp.concatenate(parts, axis=0)


def stack_heads(query):
    head = iota((BLOCK, WIDTH), 1) // HEAD_DIM
    return jnp.concatenate(
        [jnp.where(head == h, query, jnp.zeros_like(query)) for h in range(HEADS)], axis=0
    )


def list_kernel(
    q_in, kv_in, table_in, train_in, wqkv_in,
    qp, kv_first, bias_first, tops, totals, accs,
    table, train, wqkv, in_sem, kvp, kv_more, bias_more, every, chosen,
):
    row, x, y, z, c = position()
    loads = [
        pltpu.make_async_copy(source, target, in_sem.at[i])
        for i, (source, target) in enumerate(
            ((wqkv_in, wqkv), (table_in, table), (train_in, train))
        )
    ]
    for load in loads:
        load.start()
    tops[...] = jnp.full_like(tops, MASKED)
    totals[...] = jnp.zeros_like(totals)
    accs[...] = jnp.zeros_like(accs)
    for load in loads:
        load.wait()

    def project_q(i, none):
        part = q_in[i].reshape(OWNED * GROUP, WIDTH)
        got = jnp.dot(part, wqkv[:, :WIDTH], preferred_element_type=F32)
        qp[i] = (got * SCALE).astype(BF16).reshape(OWNED, GROUP, WIDTH)
        return none

    lax.fori_loop(0, OWNERS, project_q, 0, unroll=4)

    def project_kv(i, none):
        part = kv_in[i].reshape(OWNED * KEYS, WIDTH)
        got = jnp.dot(part, wqkv[:, WIDTH:], preferred_element_type=F32)
        kvp[i] = got.astype(BF16).reshape(OWNED, KEYS, 2 * WIDTH)
        return none

    lax.fori_loop(0, PLACES, project_kv, 0, unroll=4)

    group = (iota((OWNERS, BLOCK), 1) // GROUP == iota((OWNERS, BLOCK), 0) // KEEP)
    spread = train[...].astype(F32)[:, None, :] * group.astype(F32)[None]
    counts = jnp.dot(
        spread.reshape(BLOCKS * OWNERS, BLOCK).astype(BF16),
        jnp.ones((BLOCK, WIDTH), BF16),
        preferred_element_type=F32,
    )
    number = (iota((BLOCKS * OWNERS, WIDTH), 0) % KEEP).astype(F32)
    every[...] = jnp.where(number < counts, 0.0, MASKED)
    nothing = jnp.zeros((16, 2 * WIDTH), BF16)
    masked = jnp.full((16, WIDTH), MASKED, F32)

    def one_block(yy, none):
        mine = table[row_of(yy, z, c)]
        n = jnp.int32(0)
        for j in range(BLOCKS):
            chosen[n] = j
            n = n + jnp.where(table[j] == mine, 1, 0)
        tiles = lax.div(n + 15, 16)

        def gather(i, none):
            j = chosen[i]
            at = pl.multiple_of(i * 16, 16)
            come = pl.multiple_of(lax.div(j, PLACES) * 16, 16)
            for f in range(OWNED):
                kv_first[yy, f, pl.ds(at, 16), :] = kvp[lax.rem(j, PLACES), f, pl.ds(come, 16), :]
            bias_first[yy, pl.ds(at, 16), :] = every[pl.ds(pl.multiple_of(j * 16, 16), 16), :]
            return none

        lax.fori_loop(0, jnp.minimum(n, 16), gather, 0)

        def tail(i, none):
            at = pl.multiple_of(i * 16, 16)
            for f in range(OWNED):
                kv_first[yy, f, pl.ds(at, 16), :] = nothing
            bias_first[yy, pl.ds(at, 16), :] = masked
            return none

        lax.fori_loop(jnp.minimum(n, 16), 16, tail, 0)

        @pl.when(tiles > 1)
        def _():
            def gather_more(i, none):
                j = chosen[i]
                at = pl.multiple_of((i - 16) * 16, 16)
                come = pl.multiple_of(lax.div(j, PLACES) * 16, 16)
                for f in range(OWNED):
                    kv_more[f, pl.ds(at, 16), :] = kvp[lax.rem(j, PLACES), f, pl.ds(come, 16), :]
                bias_more[pl.ds(at, 16), :] = every[pl.ds(pl.multiple_of(j * 16, 16), 16), :]
                return none

            lax.fori_loop(16, n, gather_more, 0)

            def tail_more(i, none):
                at = pl.multiple_of((i - 16) * 16, 16)
                for f in range(OWNED):
                    kv_more[f, pl.ds(at, 16), :] = nothing
                bias_more[pl.ds(at, 16), :] = masked
                return none

            lax.fori_loop(n, tiles * 16, tail_more, 0)

            def one_tile(kt, none):
                at = pl.multiple_of((kt - 1) * TILE, TILE)
                mask = jnp.concatenate([bias_more[pl.ds(at, TILE), :]] * HEADS, axis=1)
                for f in range(OWNED):
                    query = jnp.concatenate([qp[yy * XS + xx, f] for xx in range(XS)], axis=0)
                    tops[yy, f], totals[yy, f], accs[yy, f] = attend_tile(
                        kv_more[f, pl.ds(at, TILE), 0:WIDTH],
                        kv_more[f, pl.ds(at, TILE), WIDTH:],
                        stack_heads(query),
                        mask,
                        tops[yy, f],
                        totals[yy, f],
                        accs[yy, f],
                    )
                return none

            lax.fori_loop(1, tiles, one_tile, 0)

        return none

    lax.fori_loop(0, YS, one_block, 0)


def back_kernel(
    q_in, qp, kv_first, bias_first, tops, totals, accs, wout_in, out,
    wout, done, landed, wide, send_sems, recv_sems, own_sem,
):
    row, x, y, z, c = position()
    owner = y * XS + x
    load = pltpu.make_async_copy(wout_in, wout, own_sem.at[0])
    load.start()
    barrier = pltpu.get_barrier_semaphore()
    for dy in range(YS):
        for dx in range(XS):
            if dx or dy:
                peer = (row_of(around(y, dy, YS), z, c), around(x, dx, XS))
                pl.semaphore_signal(barrier, inc=1, device_id=peer, device_id_type=MESH)
    load.wait()
    sent = []

    def place(g):
        for f in range(OWNED):
            wide[pl.ds(g * OWNED + f, GROUP, stride=FEATS), :] = landed[g, f].astype(F32)

    def take(dy):
        for dx in (1, 3, 2, 0):
            if dx or dy:
                k = dy * XS + dx
                g = around(y, -dy, YS) * XS + around(x, -dx, XS)
                remote(
                    landed.at[g], landed.at[g], send_sems.at[k], recv_sems.at[k], row, x
                ).wait_recv()
                place(g)

    order = (2, 1, 3, 0)
    for turn, dy in enumerate(order):
        yy = around(y, dy, YS)
        mask = jnp.concatenate([bias_first[yy]] * HEADS, axis=1)
        for f in range(OWNED):
            query = jnp.concatenate([qp[yy * XS + xx, f] for xx in range(XS)], axis=0)
            _, total, acc = attend_tile(
                kv_first[yy, f, :, 0:WIDTH],
                kv_first[yy, f, :, WIDTH:],
                stack_heads(query),
                mask,
                tops[yy, f],
                totals[yy, f],
                accs[yy, f],
            )
            attended = jnp.concatenate(
                [
                    acc[h * HEAD_DIM : (h + 1) * HEAD_DIM]
                    * (1.0 / total[:, h * BLOCK : (h + 1) * BLOCK])
                    for h in range(HEADS)
                ],
                axis=0,
            ).astype(BF16)
            got = lax.dot_general(
                attended, wout[...], (((0,), (0,)), ((), ())), preferred_element_type=F32
            )
            for xx in range(XS):
                mixed = q_in[yy * XS + xx, f].astype(F32)
                done[yy * XS + xx, f] = (mixed + got[xx * GROUP : (xx + 1) * GROUP]).astype(BF16)
        if turn == 0:
            pl.semaphore_wait(barrier, OWNERS - 1)
        for dx in (2, 1, 3, 0):
            if dx or dy:
                k = dy * XS + dx
                tx = around(x, dx, XS)
                copy = remote(
                    done.at[yy * XS + tx],
                    landed.at[owner],
                    send_sems.at[k],
                    recv_sems.at[k],
                    row_of(yy, z, c),
                    tx,
                )
                copy.start()
                sent.append(copy)
        if turn >= 2:
            take(order[turn - 2])
    landed[owner] = done[owner]
    place(owner)
    take(order[2])
    take(order[3])

    def finish(i, none):
        some = wide[pl.ds(pl.multiple_of(i * 4 * FEATS, 64), 4 * FEATS), :]
        out[pl.ds(i * 4, 4)] = some.reshape(4, FEATS, WIDTH).astype(BF16)
        return none

    lax.fori_loop(0, GROUP // 4, finish, 0, unroll=2)
    for copy in sent:
        copy.wait_send()


def list_call(query, key, block_table, train, item_qkv):
    shape = jax.ShapeDtypeStruct
    state = shape((YS, OWNED, 1, HEADS * BLOCK), F32)
    return pl.pallas_call(
        list_kernel,
        name="list",
        out_shape=(
            shape((OWNERS, OWNED, GROUP, WIDTH), BF16),
            shape((YS, OWNED, TILE, 2 * WIDTH), BF16),
            shape((YS, TILE, WIDTH), F32),
            state,
            state,
            shape((YS, OWNED, WIDTH, BLOCK), F32),
        ),
        in_specs=[VMEM, VMEM, HBM, HBM, HBM],
        out_specs=(VMEM,) * 6,
        scratch_shapes=[
            pltpu.SMEM((BLOCKS,), jnp.int32),
            pltpu.VMEM((BLOCKS, BLOCK), jnp.int32),
            pltpu.VMEM((WIDTH, 3 * WIDTH), BF16),
            pltpu.SemaphoreType.DMA((3,)),
            pltpu.VMEM((PLACES, OWNED, KEYS, 2 * WIDTH), BF16),
            pltpu.VMEM((OWNED, PLACES * KEYS, 2 * WIDTH), BF16),
            pltpu.VMEM((PLACES * KEYS, WIDTH), F32),
            pltpu.VMEM((PLACES * KEYS, WIDTH), F32),
            pltpu.SMEM((BLOCKS + 8,), jnp.int32),
        ],
        compiler_params=pltpu.CompilerParams(vmem_limit_bytes=ITEM_VMEM),
    )(query, key, *stay(block_table, train, item_qkv))


def on_device(cells, block_table, row_live, row_train, feat_qkv, feat_out, item_qkv, item_out):
    train = row_train.reshape(BLOCKS, BLOCK)
    live = row_live.reshape(BLOCKS, BLOCK)
    by_feature = jnp.transpose(cells, (1, 0, 2))
    dma = pltpu.SemaphoreType.DMA
    moved = jax.ShapeDtypeStruct((OWNERS, OWNED, GROUP, WIDTH), BF16)
    query, key = pl.pallas_call(
        mix_kernel,
        name="mix",
        out_shape=(moved, jax.ShapeDtypeStruct((PLACES, OWNED, KEYS, WIDTH), BF16)),
        in_specs=[HBM] * 6,
        out_specs=(VMEM, VMEM),
        scratch_shapes=[
            pltpu.SMEM((BLOCKS,), jnp.int32),
            pltpu.VMEM((BLOCKS, BLOCK), jnp.int32),
            pltpu.SMEM((BLOCKS * BLOCK,), jnp.int32),
            pltpu.VMEM((WIDTH, 3 * WIDTH), BF16),
            pltpu.VMEM((WIDTH, WIDTH), BF16),
            dma((5,)),
            pltpu.VMEM((SHARD, BLOCK, WIDTH), BF16),
            pltpu.VMEM((FEATS, GROUP, WIDTH), BF16),
            pltpu.VMEM((SHARD, WIDTH), F32),
            pltpu.VMEM((SHARD, WIDTH), F32),
            pltpu.VMEM((FEATS, WIDTH), F32),
            pltpu.VMEM((FEATS, WIDTH), F32),
            pltpu.VMEM((2, WIDTH), F32),
            pltpu.VMEM((YS * CS, XS, 2, WIDTH), F32),
            pltpu.VMEM((2, YS * CS, WIDTH), F32),
            pltpu.VMEM((ZS, 2, YS * CS, WIDTH), F32),
            pltpu.VMEM((BLOCKS, WIDTH), F32),
            pltpu.VMEM((GROUP * FEATS, WIDTH), F32),
            pltpu.VMEM((GROUP, FEATS, WIDTH), BF16),
            pltpu.VMEM((GROUP, FEATS, 3 * WIDTH), BF16),
            pltpu.VMEM((GROUP, FEATS, WIDTH), BF16),
            pltpu.VMEM((GROUP * FEATS, WIDTH), F32),
            pltpu.VMEM((FEATS, GROUP, WIDTH), BF16),
            pltpu.VMEM((FEATS * 8, WIDTH), F32),
            pltpu.VMEM((FEATS, 8, WIDTH), BF16),
            pltpu.VMEM((OWNERS, OWNED, 8, WIDTH), BF16),
            dma((2,)),
            dma((XS,)), dma((XS,)), dma((OWNERS * CS,)), dma((OWNERS * CS,)),
            dma((8,)), dma((8,)),
            dma((OWNERS,)), dma((OWNERS,)), dma((2 * OWNERS,)), dma((2 * OWNERS,)),
            dma((4 * OWNED,)), dma((4 * OWNED,)), dma((4 * OWNED,)), dma((4 * OWNED,)),
            dma((8 * OWNED,)), dma((8 * OWNED,)),
        ],
        compiler_params=pltpu.CompilerParams(
            collective_id=0, has_side_effects=True, vmem_limit_bytes=MIX_VMEM
        ),
    )(*stay(by_feature, block_table, live, row_train, feat_qkv, feat_out))
    listed = list_call(query, key, block_table, train, item_qkv)
    return pl.pallas_call(
        back_kernel,
        name="back",
        out_shape=jax.ShapeDtypeStruct((GROUP, FEATS, WIDTH), BF16),
        in_specs=[VMEM] * 7 + [HBM],
        out_specs=VMEM,
        scratch_shapes=[
            pltpu.VMEM((WIDTH, WIDTH), BF16),
            pltpu.VMEM((OWNERS, OWNED, GROUP, WIDTH), BF16),
            pltpu.VMEM((OWNERS, OWNED, GROUP, WIDTH), BF16),
            pltpu.VMEM((GROUP * FEATS, WIDTH), F32),
            dma((OWNERS,)), dma((OWNERS,)), dma((1,)),
        ],
        compiler_params=pltpu.CompilerParams(
            collective_id=1, has_side_effects=True, vmem_limit_bytes=BACK_VMEM
        ),
    )(query, *listed, *stay(item_out))


def solution(mesh):
    return jax.shard_map(
        on_device,
        mesh=mesh,
        in_specs=(P("rows", "feat", None), P(), P(), P(), P(), P(), P(), P()),
        out_specs=P(("rows", "feat"), None, None),
        check_vma=False,
    )
```

```python
import jax
import jax.numpy as jnp
from jax import lax
from jax.experimental import pallas as pl
from jax.experimental.pallas import tpu as pltpu
from jax.sharding import PartitionSpec as P

HEADS = 4
HEAD_DIM = 32
WIDTH = 128
KEEP = 4
XS, YS, ZS, CS = 4, 4, 8, 2
BLOCKS = YS * ZS * CS
BLOCK = 128
FEATS = 80
SHARD = 20
OWNED = 5
GROUP = 32
OWNERS = XS * YS
PLACES = ZS * CS
KEYS = YS * XS * KEEP
TILE = 256
EPSILON = 1e-05
MASKED = -1e30
SCALE = HEAD_DIM**-0.5 * 1.4426950408889634
MESH = pl.DeviceIdType.MESH
CHUNKS = ((0, 1), (1, 1), (2, 1), (3, 1), (4, 1))
FROM_RIGHT = 3
MIX_VMEM = 20 << 20
ITEM_VMEM = 20 << 20
BACK_VMEM = 12 << 20
F32 = jnp.float32
BF16 = jnp.bfloat16
VMEM = pl.BlockSpec(memory_space=pltpu.VMEM)
SMEM = pl.BlockSpec(memory_space=pltpu.SMEM)
ANY = pl.BlockSpec(memory_space=pl.ANY)
HBM = pl.BlockSpec(memory_space=pltpu.HBM)


def iota(shape, dim):
    return lax.broadcasted_iota(jnp.int32, shape, dim)


def row_of(y, z, c):
    return y * (ZS * CS) + z * CS + c


def around(at, step, size):
    return lax.rem(at + step + size, size)


def remote(source, target, send, recv, row, feat):
    return pltpu.make_async_remote_copy(
        src_ref=source,
        dst_ref=target,
        send_sem=send,
        recv_sem=recv,
        device_id=(row, feat),
        device_id_type=MESH,
    )


def stay(*arrays):
    return [pltpu.with_memory_space_constraint(a, pltpu.HBM) for a in arrays]


def position():
    row = lax.axis_index("rows")
    x = lax.axis_index("feat")
    y = lax.div(row, ZS * CS)
    z = lax.rem(lax.div(row, CS), ZS)
    c = lax.rem(row, CS)
    return row, x, y, z, c


def mix_kernel(
    cells, table_in, live_in, train_in, wqkv_in, wout_in, item_in, q_out, qp, kvp,
    kv_out, key_rows, key_qkv, item_w, table, live, train, wqkv, wout, in_sem, own, xbuf, part, level, mean_of, inv_of, st_src, sxy, sz_src, sz, counts, nrm, rows, qkv, att, mix, send,
    key_wide, key_send, key_in,
    own_sem, xs, xr, ss, sr, zs, zr, ks, kr, qs, qr, rs, rr, ls, lr, ps, pr,
):
    row, x, y, z, c = position()
    owner = y * XS + x

    fetch = pltpu.make_async_copy(cells, own, own_sem.at[0])
    fetch.start()
    loads = [
        pltpu.make_async_copy(source, target, in_sem.at[i])
        for i, (source, target) in enumerate(
            ((live_in, live), (table_in, table), (train_in, train), (wqkv_in, wqkv), (wout_in, wout),
             (item_in, item_w))
        )
    ]
    for load in loads:
        load.start()
    barrier = pltpu.get_barrier_semaphore()
    greet = []
    plane = [
        (dx, dy, dc) for dy in range(YS) for dc in range(CS) for dx in range(XS) if dx or dy or dc
    ]
    for dx, dy, dc in plane:
        greet.append((row_of(around(y, dy, YS), z, around(c, dc, CS)), around(x, dx, XS)))
    for dz in range(1, ZS):
        greet.append((row_of(y, around(z, dz, ZS), c), x))
    for peer in greet:
        pl.semaphore_signal(barrier, inc=1, device_id=peer, device_id_type=MESH)
    fetch.wait()
    for load in loads:
        load.wait()

    square = iota((BLOCK, WIDTH), 0) == iota((BLOCK, WIDTH), 1)
    flags = live[pl.ds(row, 1), :].astype(F32)
    weight = jnp.broadcast_to(
        jnp.sum(jnp.where(square, flags, 0.0), axis=1, keepdims=True), (BLOCK, WIDTH)
    )
    entries = jnp.broadcast_to(jnp.sum(flags, axis=1, keepdims=True) * WIDTH, (SHARD, WIDTH))

    def add_first(f, none):
        part[pl.ds(f, 1), :] = jnp.sum(own[f].astype(F32) * weight, axis=0, keepdims=True)
        return none

    lax.fori_loop(0, SHARD, add_first, 0, unroll=4)
    first = jnp.sum(part[...], axis=1, keepdims=True)
    level[...] = jnp.broadcast_to(first, (SHARD, WIDTH)) / entries

    def add_second(f, none):
        off = own[f].astype(F32) - level[pl.ds(f, 1), :]
        part[pl.ds(f, 1), :] = jnp.sum(off * off * weight, axis=0, keepdims=True)
        return none

    lax.fori_loop(0, SHARD, add_second, 0, unroll=4)
    second = jnp.sum(part[...], axis=1, keepdims=True)
    lane = iota((SHARD, WIDTH), 1)
    sub = iota((SHARD, WIDTH), 0)
    spot = lane == sub + GROUP * x

    def to_row(column):
        return jnp.sum(jnp.where(spot, column, 0.0), axis=0, keepdims=True)

    st_src[...] = jnp.concatenate(
        [to_row(first), to_row(second)], axis=0
    )
    counts[...] = WIDTH * jnp.dot(
        live[...].astype(F32).astype(BF16),
        jnp.ones((BLOCK, WIDTH), BF16),
        preferred_element_type=F32,
    )
    key_wide[...] = jnp.zeros_like(key_wide)
    pl.semaphore_wait(barrier, len(greet))

    here = y * CS + c
    stat_xy = []
    for dx, dy, dc in plane:
        k = (dy * CS + dc) * XS + dx
        to = row_of(around(y, dy, YS), z, around(c, dc, CS))
        copy = remote(st_src, sxy.at[here, x], ss.at[k], sr.at[k], to, around(x, dx, XS))
        copy.start()
        stat_xy.append(copy)
    bulk = []
    for d in (1, 3, 2):
        to = around(x, d, XS)
        copy = remote(
            cells.at[:, pl.ds(pl.multiple_of(to * GROUP, GROUP), GROUP)],
            xbuf.at[pl.ds(x * SHARD, SHARD)],
            xs.at[d],
            xr.at[d],
            row,
            to,
        )
        copy.start()
        bulk.append((d, copy))
    keep = pltpu.make_async_copy(
        own.at[:, pl.ds(pl.multiple_of(x * GROUP, GROUP), GROUP)],
        xbuf.at[pl.ds(x * SHARD, SHARD)],
        own_sem.at[1],
    )
    keep.start()
    sxy[here, x] = st_src[...]
    for dx, dy, dc in plane:
        k = (dy * CS + dc) * XS + dx
        came = sxy.at[around(y, -dy, YS) * CS + around(c, dc, CS), around(x, -dx, XS)]
        remote(came, came, ss.at[k], sr.at[k], row, x).wait_recv()
    merged = [
        sxy[i, 0] + sxy[i, 1] + sxy[i, 2] + sxy[i, 3] for i in range(YS * CS)
    ]
    for k in range(2):
        tile = jnp.concatenate([merged[i][k : k + 1] for i in range(YS * CS)], axis=0)
        sz_src[k] = tile
        sz[z, k] = tile
    stat_z = []
    for d in range(1, ZS):
        copy = remote(
            sz_src, sz.at[z], zs.at[d], zr.at[d], row_of(y, around(z, d, ZS), c), x
        )
        copy.start()
        stat_z.append(copy)
    spots = [jnp.int32(0)] * KEEP
    seen = jnp.int32(0)
    for r in range(GROUP):
        flag = train[row * BLOCK + x * GROUP + r]
        for j in range(KEEP):
            spots[j] = jnp.where((flag == 1) & (seen == j), r, spots[j])
        seen = seen + flag
    here_table = table[row]
    weights = [jnp.where(table[b] == here_table, 1.0, 0.0).astype(F32) for b in range(BLOCKS)]
    entries_all = jnp.zeros((1, WIDTH), F32)
    for b in range(BLOCKS):
        entries_all = entries_all + weights[b] * counts[b : b + 1, :]
    for d in range(1, ZS):
        came = around(z, -d, ZS)
        remote(sz_src, sz.at[came], zs.at[d], zr.at[d], row, x).wait_recv()

    places = [
        (zz, i, row_of(i // CS, zz, i % CS)) for zz in range(ZS) for i in range(YS * CS)
    ]
    acc = jnp.zeros((1, WIDTH), F32)
    for zz, i, b in places:
        acc = acc + weights[b] * sz[zz, 0, i : i + 1, :]
    mean_row = acc / entries_all
    spread = jnp.zeros((1, WIDTH), F32)
    for zz, i, b in places:
        entries_b = counts[b : b + 1, :]
        off = sz[zz, 0, i : i + 1, :] / entries_b - mean_row
        spread = spread + weights[b] * (sz[zz, 1, i : i + 1, :] + entries_b * (off * off))
    inv_row = lax.rsqrt(spread / entries_all + EPSILON)

    for d, _ in bulk:
        came = xbuf.at[pl.ds(around(x, -d, XS) * SHARD, SHARD)]
        remote(came, came, xs.at[d], xr.at[d], row, x).wait_recv()
    keep.wait()
    for s in range(XS):
        pick = lane == sub + GROUP * s
        for ref, values in ((mean_of, mean_row), (inv_of, inv_row)):
            column = jnp.sum(jnp.where(pick, values, 0.0), axis=1, keepdims=True)
            ref[SHARD * s : SHARD * (s + 1), :] = jnp.broadcast_to(column, (SHARD, WIDTH))

    def norm(f, none):
        value = (xbuf[f].astype(F32) - mean_of[pl.ds(f, 1), :]) * inv_of[pl.ds(f, 1), :]
        nrm[pl.ds(pl.multiple_of(f * GROUP, GROUP), GROUP), :] = value.astype(BF16).astype(F32)
        return none

    lax.fori_loop(0, FEATS, norm, 0, unroll=8)

    def by_row(r, none):
        rows[r] = nrm[pl.ds(r, FEATS, stride=GROUP), :].astype(BF16)
        return none

    lax.fori_loop(0, GROUP, by_row, 0, unroll=8)

    head = iota((FEATS, WIDTH), 1) // HEAD_DIM
    def attended(source, r):
        query = source[r, :, 0:WIDTH]
        key = source[r, :, WIDTH : 2 * WIDTH]
        value = source[r, :, 2 * WIDTH :]
        keys = jnp.concatenate(
            [jnp.where(head == h, key, jnp.zeros_like(key)) for h in range(HEADS)], axis=0
        )
        values = jnp.concatenate(
            [jnp.where(head == h, value, jnp.zeros_like(value)) for h in range(HEADS)], axis=0
        )
        scores = lax.dot_general(
            keys, query, (((1,), (1,)), ((), ())), preferred_element_type=F32
        )
        shares = []
        for h in range(HEADS):
            some = scores[h * FEATS : (h + 1) * FEATS]
            some = jnp.exp2(some - jnp.max(some, axis=0, keepdims=True))
            shares.append((some * (1.0 / jnp.sum(some, axis=0, keepdims=True))).astype(BF16))
        return lax.dot_general(
            jnp.concatenate(shares, axis=0),
            values,
            (((0,), (0,)), ((), ())),
            preferred_element_type=F32,
        ).astype(BF16)

    for j in range(KEEP):
        key_rows[j] = rows[spots[j]]
    some = key_rows[...].reshape(KEEP * FEATS, WIDTH)
    out = jnp.dot(some, wqkv[...], preferred_element_type=F32)
    key_qkv[:, :, 0:WIDTH] = (out[:, :WIDTH] * SCALE).astype(BF16).reshape(KEEP, FEATS, WIDTH)
    key_qkv[:, :, WIDTH:] = out[:, WIDTH:].astype(BF16).reshape(KEEP, FEATS, 2 * WIDTH)
    found = jnp.concatenate([attended(key_qkv, j) for j in range(KEEP)], axis=0)
    out = jnp.dot(found, wout[...], preferred_element_type=F32)
    out = out + key_rows[...].reshape(KEEP * FEATS, WIDTH).astype(F32)
    for j in range(KEEP):
        key_wide[pl.ds(KEEP * lax.rem(x, 2) + j, FEATS, stride=8), :] = out[
            j * FEATS : (j + 1) * FEATS
        ]
    key_send[...] = key_wide[...].reshape(FEATS, 8, WIDTH).astype(BF16)
    peers = []
    for dy in range(YS):
        for dx in range(XS):
            if dx or dy:
                ty, tx = around(y, dy, YS), around(x, dx, XS)
                peers.append((dy * XS + dx, ty * XS + tx, row_of(ty, z, c), tx))
    sent = []
    key_moved = []
    for k, to, to_row, tx in peers:
        copy = remote(
            key_send.at[pl.ds(to * OWNED, OWNED)], key_in.at[owner], ks.at[k], kr.at[k], to_row, tx
        )
        copy.start()
        key_moved.append(copy)
    key_in[owner] = key_send[pl.ds(owner * OWNED, OWNED)]

    def project(i, none):
        some = rows[pl.ds(i * 4, 4)].reshape(4 * FEATS, WIDTH)
        out = jnp.dot(some, wqkv[...], preferred_element_type=F32)
        qkv[pl.ds(i * 4, 4), :, 0:WIDTH] = (
            (out[:, :WIDTH] * SCALE).astype(BF16).reshape(4, FEATS, WIDTH)
        )
        qkv[pl.ds(i * 4, 4), :, WIDTH:] = (
            out[:, WIDTH:].astype(BF16).reshape(4, FEATS, 2 * WIDTH)
        )
        return none

    lax.fori_loop(0, GROUP // 4, project, 0, unroll=4)

    moved = []

    def attend_rows(low, size):
        def attend(r, none):
            att[r] = attended(qkv, r)
            return none

        lax.fori_loop(low, low + size, attend, 0, unroll=size)

    def send_rows(low, size):
        def update(i, none):
            some = att[pl.ds(i * 4, 4)].reshape(4 * FEATS, WIDTH)
            out = jnp.dot(some, wout[...], preferred_element_type=F32)
            out = out + rows[pl.ds(i * 4, 4)].reshape(4 * FEATS, WIDTH).astype(F32)
            mix[pl.ds(i * 4 * FEATS, 4 * FEATS), :] = out
            return none

        lax.fori_loop(low // 4, (low + size) // 4, update, 0, unroll=2)

        def turn(f, none):
            send[f, low : low + size, :] = mix[
                pl.ds(low * FEATS + f, size, stride=FEATS), :
            ].astype(BF16)
            return none

        lax.fori_loop(0, FEATS, turn, 0, unroll=8)
        these = pl.ds(low, size)
        for k, to, to_row, tx in peers:
            at = (low // 8) * OWNERS + k
            copy = remote(
                send.at[pl.ds(to * OWNED, OWNED), these],
                q_out.at[owner, :, these],
                qs.at[at],
                qr.at[at],
                to_row,
                tx,
            )
            copy.start()
            moved.append(copy)
        q_out[owner, :, low : low + size, :] = send[
            pl.ds(owner * OWNED, OWNED), low : low + size, :
        ]

    attend_rows(0, 16)

    for copy in key_moved:
        copy.wait_recv()
    spot_here = z * CS + c
    for yy in range(YS):
        for f in range(OWNED):
            low = key_in[yy * XS, f].astype(F32) + key_in[yy * XS + 1, f].astype(F32)
            high = key_in[yy * XS + 2, f].astype(F32) + key_in[yy * XS + 3, f].astype(F32)
            kv_out[spot_here, f, yy * 16 : yy * 16 + 16, :] = jnp.concatenate(
                [low, high], axis=0
            ).astype(BF16)

    right, left = row_of(y, around(z, 1, ZS), c), row_of(y, around(z, -1, ZS), c)
    other = row_of(y, z, 1 - c)

    count = len(CHUNKS)

    def slot(d, i):
        return kv_out.at[around(z, d, ZS) * CS + c, pl.ds(CHUNKS[i][0], CHUNKS[i][1])]

    def hop(d, i, sems, k, to):
        send_sems, recv_sems = sems
        at = k * count + i
        copy = remote(slot(d, i), slot(d, i), send_sems.at[at], recv_sems.at[at], to, x)
        copy.start()
        sent.append(copy)

    def lands(d, i, sems, k, to):
        at = k * count + i
        remote(slot(d, i), slot(d, i), sems[0].at[at], sems[1].at[at], to, x).wait_recv()

    def over(d, i):
        hop(d, i, (ps, pr), d + 4, other)

    def on_right(k, i):
        return k < 3 or (k == 3 and i < FROM_RIGHT)

    def on_left(k, i):
        return k < 3 or (k == 3 and i >= FROM_RIGHT)

    for i in range(count):
        hop(0, i, (rs, rr), 0, right)
        hop(0, i, (ls, lr), 0, left)
    for i in range(count):
        over(0, i)

    def ring_step(k):
        for i in range(count):
            if on_right(k, i):
                lands(-1 - k, i, (rs, rr), k, right)
                if on_right(k + 1, i):
                    hop(-1 - k, i, (rs, rr), k + 1, right)
                over(-1 - k, i)
            if on_left(k, i):
                lands(1 + k, i, (ls, lr), k, left)
                if on_left(k + 1, i):
                    hop(1 + k, i, (ls, lr), k + 1, left)
                over(1 + k if k < 3 else -4, i)

    def project_place(at):
        some = kv_out[at].reshape(OWNED * KEYS, WIDTH)
        got = jnp.dot(some, item_w[:, WIDTH:], preferred_element_type=F32)
        kvp[at] = got.astype(BF16).reshape(OWNED, KEYS, 2 * WIDTH)

    def mine(d):
        project_place(around(z, d, ZS) * CS + c)

    def others(d):
        at = around(z, d, ZS) * CS + 1 - c
        for i in range(count):
            came = kv_out.at[at, pl.ds(CHUNKS[i][0], CHUNKS[i][1])]
            k = (d + 4) * count + i
            remote(came, came, ps.at[k], pr.at[k], other, x).wait_recv()
        project_place(at)

    send_rows(0, 16)
    attend_rows(16, 8)
    send_rows(16, 8)
    ring_step(0)
    attend_rows(24, 8)
    send_rows(24, 8)
    ring_step(1)
    for d in (0, -1, 1):
        mine(d)
    others(0)
    ring_step(2)
    for copy in moved:
        copy.wait_recv()

    def project_q(i, none):
        some = q_out[i].reshape(OWNED * GROUP, WIDTH)
        got = jnp.dot(some, item_w[:, :WIDTH], preferred_element_type=F32)
        qp[i] = (got * SCALE).astype(BF16).reshape(OWNED, GROUP, WIDTH)
        return none

    lax.fori_loop(0, OWNERS, project_q, 0, unroll=4)
    mine(-2)
    mine(2)
    others(-1)
    others(1)
    ring_step(3)
    others(-2)
    others(2)
    mine(-3)
    mine(3)
    mine(-4)
    for d in (-3, 3, -4):
        others(d)

    for copy in stat_xy + [copy for _, copy in bulk] + stat_z + key_moved + moved + sent:
        copy.wait_send()


def attend_tile(key, value, stacked, mask, top, total, acc):
    scores = lax.dot_general(
        key, stacked, (((1,), (1,)), ((), ())), preferred_element_type=F32
    )
    scores = scores + mask
    new_top = jnp.maximum(top, jnp.max(scores, axis=0, keepdims=True))
    shares = jnp.exp2(scores - new_top)
    fade = jnp.exp2(top - new_top)
    total = total * fade + jnp.sum(shares, axis=0, keepdims=True)
    got = lax.dot_general(
        value, shares.astype(BF16), (((0,), (0,)), ((), ())), preferred_element_type=F32
    )
    parts = []
    for h in range(HEADS):
        rows = slice(h * HEAD_DIM, (h + 1) * HEAD_DIM)
        cols = slice(h * BLOCK, (h + 1) * BLOCK)
        parts.append(acc[rows] * fade[:, cols] + got[rows, cols])
    return new_top, total, jnp.concatenate(parts, axis=0)


def stack_heads(query):
    head = iota((BLOCK, WIDTH), 1) // HEAD_DIM
    return jnp.concatenate(
        [jnp.where(head == h, query, jnp.zeros_like(query)) for h in range(HEADS)], axis=0
    )


def list_kernel(
    qp, kvp, table_in, train_in,
    kv_first, bias_first, tops, totals, accs,
    table, train, in_sem, kv_more, bias_more, every, chosen,
):
    row, x, y, z, c = position()
    loads = [
        pltpu.make_async_copy(source, target, in_sem.at[i])
        for i, (source, target) in enumerate(
            ((table_in, table), (train_in, train))
        )
    ]
    for load in loads:
        load.start()
    tops[...] = jnp.full_like(tops, MASKED)
    totals[...] = jnp.zeros_like(totals)
    accs[...] = jnp.zeros_like(accs)
    for load in loads:
        load.wait()

    group = (iota((OWNERS, BLOCK), 1) // GROUP == iota((OWNERS, BLOCK), 0) // KEEP)
    spread = train[...].astype(F32)[:, None, :] * group.astype(F32)[None]
    counts = jnp.dot(
        spread.reshape(BLOCKS * OWNERS, BLOCK).astype(BF16),
        jnp.ones((BLOCK, WIDTH), BF16),
        preferred_element_type=F32,
    )
    number = (iota((BLOCKS * OWNERS, WIDTH), 0) % KEEP).astype(F32)
    every[...] = jnp.where(number < counts, 0.0, MASKED)
    nothing = jnp.zeros((16, 2 * WIDTH), BF16)
    masked = jnp.full((16, WIDTH), MASKED, F32)

    def one_block(yy, none):
        mine = table[row_of(yy, z, c)]
        n = jnp.int32(0)
        for j in range(BLOCKS):
            chosen[n] = j
            n = n + jnp.where(table[j] == mine, 1, 0)
        tiles = lax.div(n + 15, 16)

        def gather(i, none):
            j = chosen[i]
            at = pl.multiple_of(i * 16, 16)
            come = pl.multiple_of(lax.div(j, PLACES) * 16, 16)
            for f in range(OWNED):
                kv_first[yy, f, pl.ds(at, 16), :] = kvp[lax.rem(j, PLACES), f, pl.ds(come, 16), :]
            bias_first[yy, pl.ds(at, 16), :] = every[pl.ds(pl.multiple_of(j * 16, 16), 16), :]
            return none

        lax.fori_loop(0, jnp.minimum(n, 16), gather, 0)

        def tail(i, none):
            at = pl.multiple_of(i * 16, 16)
            for f in range(OWNED):
                kv_first[yy, f, pl.ds(at, 16), :] = nothing
            bias_first[yy, pl.ds(at, 16), :] = masked
            return none

        lax.fori_loop(jnp.minimum(n, 16), 16, tail, 0)

        @pl.when(tiles > 1)
        def _():
            def gather_more(i, none):
                j = chosen[i]
                at = pl.multiple_of((i - 16) * 16, 16)
                come = pl.multiple_of(lax.div(j, PLACES) * 16, 16)
                for f in range(OWNED):
                    kv_more[f, pl.ds(at, 16), :] = kvp[lax.rem(j, PLACES), f, pl.ds(come, 16), :]
                bias_more[pl.ds(at, 16), :] = every[pl.ds(pl.multiple_of(j * 16, 16), 16), :]
                return none

            lax.fori_loop(16, n, gather_more, 0)

            def tail_more(i, none):
                at = pl.multiple_of((i - 16) * 16, 16)
                for f in range(OWNED):
                    kv_more[f, pl.ds(at, 16), :] = nothing
                bias_more[pl.ds(at, 16), :] = masked
                return none

            lax.fori_loop(n, tiles * 16, tail_more, 0)

            def one_tile(kt, none):
                at = pl.multiple_of((kt - 1) * TILE, TILE)
                mask = jnp.concatenate([bias_more[pl.ds(at, TILE), :]] * HEADS, axis=1)
                for f in range(OWNED):
                    query = jnp.concatenate([qp[yy * XS + xx, f] for xx in range(XS)], axis=0)
                    tops[yy, f], totals[yy, f], accs[yy, f] = attend_tile(
                        kv_more[f, pl.ds(at, TILE), 0:WIDTH],
                        kv_more[f, pl.ds(at, TILE), WIDTH:],
                        stack_heads(query),
                        mask,
                        tops[yy, f],
                        totals[yy, f],
                        accs[yy, f],
                    )
                return none

            lax.fori_loop(1, tiles, one_tile, 0)

        return none

    lax.fori_loop(0, YS, one_block, 0)


def back_kernel(
    q_in, qp, kv_first, bias_first, tops, totals, accs, wout_in, out,
    wout, done, landed, wide, send_sems, recv_sems, own_sem,
):
    row, x, y, z, c = position()
    owner = y * XS + x
    load = pltpu.make_async_copy(wout_in, wout, own_sem.at[0])
    load.start()
    barrier = pltpu.get_barrier_semaphore()
    for dy in range(YS):
        for dx in range(XS):
            if dx or dy:
                peer = (row_of(around(y, dy, YS), z, c), around(x, dx, XS))
                pl.semaphore_signal(barrier, inc=1, device_id=peer, device_id_type=MESH)
    load.wait()
    sent = []

    def place(g):
        for f in range(OWNED):
            wide[pl.ds(g * OWNED + f, GROUP, stride=FEATS), :] = landed[g, f].astype(F32)

    def take(dy):
        for dx in (1, 3, 2, 0):
            if dx or dy:
                k = dy * XS + dx
                g = around(y, -dy, YS) * XS + around(x, -dx, XS)
                remote(
                    landed.at[g], landed.at[g], send_sems.at[k], recv_sems.at[k], row, x
                ).wait_recv()
                place(g)

    order = (2, 1, 3, 0)
    for turn, dy in enumerate(order):
        yy = around(y, dy, YS)
        mask = jnp.concatenate([bias_first[yy]] * HEADS, axis=1)
        for f in range(OWNED):
            query = jnp.concatenate([qp[yy * XS + xx, f] for xx in range(XS)], axis=0)
            _, total, acc = attend_tile(
                kv_first[yy, f, :, 0:WIDTH],
                kv_first[yy, f, :, WIDTH:],
                stack_heads(query),
                mask,
                tops[yy, f],
                totals[yy, f],
                accs[yy, f],
            )
            attended = jnp.concatenate(
                [
                    acc[h * HEAD_DIM : (h + 1) * HEAD_DIM]
                    * (1.0 / total[:, h * BLOCK : (h + 1) * BLOCK])
                    for h in range(HEADS)
                ],
                axis=0,
            ).astype(BF16)
            got = lax.dot_general(
                attended, wout[...], (((0,), (0,)), ((), ())), preferred_element_type=F32
            )
            for xx in range(XS):
                mixed = q_in[yy * XS + xx, f].astype(F32)
                done[yy * XS + xx, f] = (mixed + got[xx * GROUP : (xx + 1) * GROUP]).astype(BF16)
        if turn == 0:
            pl.semaphore_wait(barrier, OWNERS - 1)
        for dx in (2, 1, 3, 0):
            if dx or dy:
                k = dy * XS + dx
                tx = around(x, dx, XS)
                copy = remote(
                    done.at[yy * XS + tx],
                    landed.at[owner],
                    send_sems.at[k],
                    recv_sems.at[k],
                    row_of(yy, z, c),
                    tx,
                )
                copy.start()
                sent.append(copy)
        if turn >= 2:
            take(order[turn - 2])
    landed[owner] = done[owner]
    place(owner)
    take(order[2])
    take(order[3])

    def finish(i, none):
        some = wide[pl.ds(pl.multiple_of(i * 4 * FEATS, 64), 4 * FEATS), :]
        out[pl.ds(i * 4, 4)] = some.reshape(4, FEATS, WIDTH).astype(BF16)
        return none

    lax.fori_loop(0, GROUP // 4, finish, 0, unroll=2)
    for copy in sent:
        copy.wait_send()


def list_call(query, key, block_table, train):
    shape = jax.ShapeDtypeStruct
    state = shape((YS, OWNED, 1, HEADS * BLOCK), F32)
    return pl.pallas_call(
        list_kernel,
        name="list",
        out_shape=(
            shape((YS, OWNED, TILE, 2 * WIDTH), BF16),
            shape((YS, TILE, WIDTH), F32),
            state,
            state,
            shape((YS, OWNED, WIDTH, BLOCK), F32),
        ),
        in_specs=[VMEM, VMEM, HBM, HBM],
        out_specs=(VMEM,) * 5,
        scratch_shapes=[
            pltpu.SMEM((BLOCKS,), jnp.int32),
            pltpu.VMEM((BLOCKS, BLOCK), jnp.int32),
            pltpu.SemaphoreType.DMA((2,)),
            pltpu.VMEM((OWNED, PLACES * KEYS, 2 * WIDTH), BF16),
            pltpu.VMEM((PLACES * KEYS, WIDTH), F32),
            pltpu.VMEM((PLACES * KEYS, WIDTH), F32),
            pltpu.SMEM((BLOCKS + 8,), jnp.int32),
        ],
        compiler_params=pltpu.CompilerParams(vmem_limit_bytes=ITEM_VMEM),
    )(query, key, *stay(block_table, train))


def on_device(cells, block_table, row_live, row_train, feat_qkv, feat_out, item_qkv, item_out):
    train = row_train.reshape(BLOCKS, BLOCK)
    live = row_live.reshape(BLOCKS, BLOCK)
    by_feature = jnp.transpose(cells, (1, 0, 2))
    dma = pltpu.SemaphoreType.DMA
    moved = jax.ShapeDtypeStruct((OWNERS, OWNED, GROUP, WIDTH), BF16)
    mixed, query, key = pl.pallas_call(
        mix_kernel,
        name="mix",
        out_shape=(
            moved,
            moved,
            jax.ShapeDtypeStruct((PLACES, OWNED, KEYS, 2 * WIDTH), BF16),
        ),
        in_specs=[HBM] * 7,
        out_specs=(VMEM,) * 3,
        scratch_shapes=[
            pltpu.VMEM((PLACES, OWNED, KEYS, WIDTH), BF16),
            pltpu.VMEM((KEEP, FEATS, WIDTH), BF16),
            pltpu.VMEM((KEEP, FEATS, 3 * WIDTH), BF16),
            pltpu.VMEM((WIDTH, 3 * WIDTH), BF16),
            pltpu.SMEM((BLOCKS,), jnp.int32),
            pltpu.VMEM((BLOCKS, BLOCK), jnp.int32),
            pltpu.SMEM((BLOCKS * BLOCK,), jnp.int32),
            pltpu.VMEM((WIDTH, 3 * WIDTH), BF16),
            pltpu.VMEM((WIDTH, WIDTH), BF16),
            dma((6,)),
            pltpu.VMEM((SHARD, BLOCK, WIDTH), BF16),
            pltpu.VMEM((FEATS, GROUP, WIDTH), BF16),
            pltpu.VMEM((SHARD, WIDTH), F32),
            pltpu.VMEM((SHARD, WIDTH), F32),
            pltpu.VMEM((FEATS, WIDTH), F32),
            pltpu.VMEM((FEATS, WIDTH), F32),
            pltpu.VMEM((2, WIDTH), F32),
            pltpu.VMEM((YS * CS, XS, 2, WIDTH), F32),
            pltpu.VMEM((2, YS * CS, WIDTH), F32),
            pltpu.VMEM((ZS, 2, YS * CS, WIDTH), F32),
            pltpu.VMEM((BLOCKS, WIDTH), F32),
            pltpu.VMEM((GROUP * FEATS, WIDTH), F32),
            pltpu.VMEM((GROUP, FEATS, WIDTH), BF16),
            pltpu.VMEM((GROUP, FEATS, 3 * WIDTH), BF16),
            pltpu.VMEM((GROUP, FEATS, WIDTH), BF16),
            pltpu.VMEM((GROUP * FEATS, WIDTH), F32),
            pltpu.VMEM((FEATS, GROUP, WIDTH), BF16),
            pltpu.VMEM((FEATS * 8, WIDTH), F32),
            pltpu.VMEM((FEATS, 8, WIDTH), BF16),
            pltpu.VMEM((OWNERS, OWNED, 8, WIDTH), BF16),
            dma((2,)),
            dma((XS,)), dma((XS,)), dma((OWNERS * CS,)), dma((OWNERS * CS,)),
            dma((8,)), dma((8,)),
            dma((OWNERS,)), dma((OWNERS,)), dma((4 * OWNERS,)), dma((4 * OWNERS,)),
            dma((4 * OWNED,)), dma((4 * OWNED,)), dma((4 * OWNED,)), dma((4 * OWNED,)),
            dma((8 * OWNED,)), dma((8 * OWNED,)),
        ],
        compiler_params=pltpu.CompilerParams(
            collective_id=0, has_side_effects=True, vmem_limit_bytes=MIX_VMEM
        ),
    )(*stay(by_feature, block_table, live, row_train, feat_qkv, feat_out, item_qkv))
    listed = list_call(query, key, block_table, train)
    return pl.pallas_call(
        back_kernel,
        name="back",
        out_shape=jax.ShapeDtypeStruct((GROUP, FEATS, WIDTH), BF16),
        in_specs=[VMEM] * 7 + [HBM],
        out_specs=VMEM,
        scratch_shapes=[
            pltpu.VMEM((WIDTH, WIDTH), BF16),
            pltpu.VMEM((OWNERS, OWNED, GROUP, WIDTH), BF16),
            pltpu.VMEM((OWNERS, OWNED, GROUP, WIDTH), BF16),
            pltpu.VMEM((GROUP * FEATS, WIDTH), F32),
            dma((OWNERS,)), dma((OWNERS,)), dma((1,)),
        ],
        compiler_params=pltpu.CompilerParams(
            collective_id=1, has_side_effects=True, vmem_limit_bytes=BACK_VMEM
        ),
    )(mixed, query, *listed, *stay(item_out))


def solution(mesh):
    return jax.shard_map(
        on_device,
        mesh=mesh,
        in_specs=(P("rows", "feat", None), P(), P(), P(), P(), P(), P(), P()),
        out_specs=P(("rows", "feat"), None, None),
        check_vma=False,
    )
```

```python
import jax
import jax.numpy as jnp
from jax import lax
from jax.experimental import pallas as pl
from jax.experimental.pallas import tpu as pltpu
from jax.sharding import PartitionSpec as P

HEADS = 4
HEAD_DIM = 32
WIDTH = 128
KEEP = 4
XS, YS, ZS, CS = 4, 4, 8, 2
BLOCKS = YS * ZS * CS
BLOCK = 128
FEATS = 80
SHARD = 20
OWNED = 5
GROUP = 32
OWNERS = XS * YS
PLACES = ZS * CS
KEYS = YS * XS * KEEP
TILE = 256
EPSILON = 1e-05
MASKED = -1e30
SCALE = HEAD_DIM**-0.5 * 1.4426950408889634
MESH = pl.DeviceIdType.MESH
MIX_VMEM = 20 << 20
ITEM_VMEM = 20 << 20
BACK_VMEM = 12 << 20
F32 = jnp.float32
BF16 = jnp.bfloat16
VMEM = pl.BlockSpec(memory_space=pltpu.VMEM)
SMEM = pl.BlockSpec(memory_space=pltpu.SMEM)
ANY = pl.BlockSpec(memory_space=pl.ANY)
HBM = pl.BlockSpec(memory_space=pltpu.HBM)


def iota(shape, dim):
    return lax.broadcasted_iota(jnp.int32, shape, dim)


def row_of(y, z, c):
    return y * (ZS * CS) + z * CS + c


def around(at, step, size):
    return lax.rem(at + step + size, size)


def remote(source, target, send, recv, row, feat):
    return pltpu.make_async_remote_copy(
        src_ref=source,
        dst_ref=target,
        send_sem=send,
        recv_sem=recv,
        device_id=(row, feat),
        device_id_type=MESH,
    )


def stay(*arrays):
    return [pltpu.with_memory_space_constraint(a, pltpu.HBM) for a in arrays]


def position():
    row = lax.axis_index("rows")
    x = lax.axis_index("feat")
    y = lax.div(row, ZS * CS)
    z = lax.rem(lax.div(row, CS), ZS)
    c = lax.rem(row, CS)
    return row, x, y, z, c


def mix_kernel(
    cells, table_in, live_in, train_in, wqkv_in, wout_in, item_in, q_out, qp, kvp,
    kv_out, key_rows, key_qkv, item_w, table, live, train, wqkv, wout, in_sem, own, xbuf, part, level, mean_of, inv_of, st_src, sxy, sz_src, sz, counts, nrm, rows, qkv, att, mix, send,
    key_wide, key_send, key_in,
    own_sem, xs, xr, ss, sr, zs, zr, ks, kr, qs, qr, rs, rr, ls, lr, ps, pr,
):
    row, x, y, z, c = position()
    owner = y * XS + x

    fetch = pltpu.make_async_copy(cells, own, own_sem.at[0])
    fetch.start()
    loads = [
        pltpu.make_async_copy(source, target, in_sem.at[i])
        for i, (source, target) in enumerate(
            ((live_in, live), (table_in, table), (train_in, train), (wqkv_in, wqkv), (wout_in, wout),
             (item_in, item_w))
        )
    ]
    for load in loads:
        load.start()
    barrier = pltpu.get_barrier_semaphore()
    greet = []
    plane = [
        (dx, dy, dc) for dy in range(YS) for dc in range(CS) for dx in range(XS) if dx or dy or dc
    ]
    for dx, dy, dc in plane:
        greet.append((row_of(around(y, dy, YS), z, around(c, dc, CS)), around(x, dx, XS)))
    for dz in range(1, ZS):
        greet.append((row_of(y, around(z, dz, ZS), c), x))
    for peer in greet:
        pl.semaphore_signal(barrier, inc=1, device_id=peer, device_id_type=MESH)
    fetch.wait()
    for load in loads:
        load.wait()

    square = iota((BLOCK, WIDTH), 0) == iota((BLOCK, WIDTH), 1)
    flags = live[pl.ds(row, 1), :].astype(F32)
    weight = jnp.broadcast_to(
        jnp.sum(jnp.where(square, flags, 0.0), axis=1, keepdims=True), (BLOCK, WIDTH)
    )
    entries = jnp.broadcast_to(jnp.sum(flags, axis=1, keepdims=True) * WIDTH, (SHARD, WIDTH))

    def add_first(f, none):
        part[pl.ds(f, 1), :] = jnp.sum(own[f].astype(F32) * weight, axis=0, keepdims=True)
        return none

    lax.fori_loop(0, SHARD, add_first, 0, unroll=4)
    first = jnp.sum(part[...], axis=1, keepdims=True)
    level[...] = jnp.broadcast_to(first, (SHARD, WIDTH)) / entries

    def add_second(f, none):
        off = own[f].astype(F32) - level[pl.ds(f, 1), :]
        part[pl.ds(f, 1), :] = jnp.sum(off * off * weight, axis=0, keepdims=True)
        return none

    lax.fori_loop(0, SHARD, add_second, 0, unroll=4)
    second = jnp.sum(part[...], axis=1, keepdims=True)
    lane = iota((SHARD, WIDTH), 1)
    sub = iota((SHARD, WIDTH), 0)
    spot = lane == sub + GROUP * x

    def to_row(column):
        return jnp.sum(jnp.where(spot, column, 0.0), axis=0, keepdims=True)

    st_src[...] = jnp.concatenate(
        [to_row(first), to_row(second)], axis=0
    )
    counts[...] = WIDTH * jnp.dot(
        live[...].astype(F32).astype(BF16),
        jnp.ones((BLOCK, WIDTH), BF16),
        preferred_element_type=F32,
    )
    key_wide[...] = jnp.zeros_like(key_wide)
    pl.semaphore_wait(barrier, len(greet))

    here = y * CS + c
    stat_xy = []
    for dx, dy, dc in plane:
        k = (dy * CS + dc) * XS + dx
        to = row_of(around(y, dy, YS), z, around(c, dc, CS))
        copy = remote(st_src, sxy.at[here, x], ss.at[k], sr.at[k], to, around(x, dx, XS))
        copy.start()
        stat_xy.append(copy)
    bulk = []
    for d in (1, 3, 2):
        to = around(x, d, XS)
        copy = remote(
            cells.at[:, pl.ds(pl.multiple_of(to * GROUP, GROUP), GROUP)],
            xbuf.at[pl.ds(x * SHARD, SHARD)],
            xs.at[d],
            xr.at[d],
            row,
            to,
        )
        copy.start()
        bulk.append((d, copy))
    keep = pltpu.make_async_copy(
        own.at[:, pl.ds(pl.multiple_of(x * GROUP, GROUP), GROUP)],
        xbuf.at[pl.ds(x * SHARD, SHARD)],
        own_sem.at[1],
    )
    keep.start()
    sxy[here, x] = st_src[...]
    for dx, dy, dc in plane:
        k = (dy * CS + dc) * XS + dx
        came = sxy.at[around(y, -dy, YS) * CS + around(c, dc, CS), around(x, -dx, XS)]
        remote(came, came, ss.at[k], sr.at[k], row, x).wait_recv()
    merged = [
        sxy[i, 0] + sxy[i, 1] + sxy[i, 2] + sxy[i, 3] for i in range(YS * CS)
    ]
    for k in range(2):
        tile = jnp.concatenate([merged[i][k : k + 1] for i in range(YS * CS)], axis=0)
        sz_src[k] = tile
        sz[z, k] = tile
    stat_z = []
    for d in range(1, ZS):
        copy = remote(
            sz_src, sz.at[z], zs.at[d], zr.at[d], row_of(y, around(z, d, ZS), c), x
        )
        copy.start()
        stat_z.append(copy)
    spots = [jnp.int32(0)] * KEEP
    seen = jnp.int32(0)
    for r in range(GROUP):
        flag = train[row * BLOCK + x * GROUP + r]
        for j in range(KEEP):
            spots[j] = jnp.where((flag == 1) & (seen == j), r, spots[j])
        seen = seen + flag
    here_table = table[row]
    weights = [jnp.where(table[b] == here_table, 1.0, 0.0).astype(F32) for b in range(BLOCKS)]
    entries_all = jnp.zeros((1, WIDTH), F32)
    for b in range(BLOCKS):
        entries_all = entries_all + weights[b] * counts[b : b + 1, :]
    for d in range(1, ZS):
        came = around(z, -d, ZS)
        remote(sz_src, sz.at[came], zs.at[d], zr.at[d], row, x).wait_recv()

    places = [
        (zz, i, row_of(i // CS, zz, i % CS)) for zz in range(ZS) for i in range(YS * CS)
    ]
    acc = jnp.zeros((1, WIDTH), F32)
    for zz, i, b in places:
        acc = acc + weights[b] * sz[zz, 0, i : i + 1, :]
    mean_row = acc / entries_all
    spread = jnp.zeros((1, WIDTH), F32)
    for zz, i, b in places:
        entries_b = counts[b : b + 1, :]
        off = sz[zz, 0, i : i + 1, :] / entries_b - mean_row
        spread = spread + weights[b] * (sz[zz, 1, i : i + 1, :] + entries_b * (off * off))
    inv_row = lax.rsqrt(spread / entries_all + EPSILON)

    for d, _ in bulk:
        came = xbuf.at[pl.ds(around(x, -d, XS) * SHARD, SHARD)]
        remote(came, came, xs.at[d], xr.at[d], row, x).wait_recv()
    keep.wait()
    for s in range(XS):
        pick = lane == sub + GROUP * s
        for ref, values in ((mean_of, mean_row), (inv_of, inv_row)):
            column = jnp.sum(jnp.where(pick, values, 0.0), axis=1, keepdims=True)
            ref[SHARD * s : SHARD * (s + 1), :] = jnp.broadcast_to(column, (SHARD, WIDTH))

    def norm(f, none):
        value = (xbuf[f].astype(F32) - mean_of[pl.ds(f, 1), :]) * inv_of[pl.ds(f, 1), :]
        nrm[pl.ds(pl.multiple_of(f * GROUP, GROUP), GROUP), :] = value.astype(BF16).astype(F32)
        return none

    lax.fori_loop(0, FEATS, norm, 0, unroll=8)

    def by_row(r, none):
        rows[r] = nrm[pl.ds(r, FEATS, stride=GROUP), :].astype(BF16)
        return none

    lax.fori_loop(0, GROUP, by_row, 0, unroll=8)

    head = iota((FEATS, WIDTH), 1) // HEAD_DIM
    def attended(source, r):
        query = source[r, :, 0:WIDTH]
        key = source[r, :, WIDTH : 2 * WIDTH]
        value = source[r, :, 2 * WIDTH :]
        keys = jnp.concatenate(
            [jnp.where(head == h, key, jnp.zeros_like(key)) for h in range(HEADS)], axis=0
        )
        values = jnp.concatenate(
            [jnp.where(head == h, value, jnp.zeros_like(value)) for h in range(HEADS)], axis=0
        )
        scores = lax.dot_general(
            keys, query, (((1,), (1,)), ((), ())), preferred_element_type=F32
        )
        shares = []
        for h in range(HEADS):
            some = scores[h * FEATS : (h + 1) * FEATS]
            some = jnp.exp2(some - jnp.max(some, axis=0, keepdims=True))
            shares.append((some * (1.0 / jnp.sum(some, axis=0, keepdims=True))).astype(BF16))
        return lax.dot_general(
            jnp.concatenate(shares, axis=0),
            values,
            (((0,), (0,)), ((), ())),
            preferred_element_type=F32,
        ).astype(BF16)

    for j in range(KEEP):
        key_rows[j] = rows[spots[j]]
    some = key_rows[...].reshape(KEEP * FEATS, WIDTH)
    out = jnp.dot(some, wqkv[...], preferred_element_type=F32)
    key_qkv[:, :, 0:WIDTH] = (out[:, :WIDTH] * SCALE).astype(BF16).reshape(KEEP, FEATS, WIDTH)
    key_qkv[:, :, WIDTH:] = out[:, WIDTH:].astype(BF16).reshape(KEEP, FEATS, 2 * WIDTH)
    found = jnp.concatenate([attended(key_qkv, j) for j in range(KEEP)], axis=0)
    out = jnp.dot(found, wout[...], preferred_element_type=F32)
    out = out + key_rows[...].reshape(KEEP * FEATS, WIDTH).astype(F32)
    for j in range(KEEP):
        key_wide[pl.ds(KEEP * lax.rem(x, 2) + j, FEATS, stride=8), :] = out[
            j * FEATS : (j + 1) * FEATS
        ]
    key_send[...] = key_wide[...].reshape(FEATS, 8, WIDTH).astype(BF16)
    peers = []
    for dy in range(YS):
        for dx in range(XS):
            if dx or dy:
                ty, tx = around(y, dy, YS), around(x, dx, XS)
                peers.append((dy * XS + dx, ty * XS + tx, row_of(ty, z, c), tx))
    sent = []
    key_moved = []
    for k, to, to_row, tx in peers:
        copy = remote(
            key_send.at[pl.ds(to * OWNED, OWNED)], key_in.at[owner], ks.at[k], kr.at[k], to_row, tx
        )
        copy.start()
        key_moved.append(copy)
    key_in[owner] = key_send[pl.ds(owner * OWNED, OWNED)]

    def project(i, none):
        some = rows[pl.ds(i * 4, 4)].reshape(4 * FEATS, WIDTH)
        out = jnp.dot(some, wqkv[...], preferred_element_type=F32)
        qkv[pl.ds(i * 4, 4), :, 0:WIDTH] = (
            (out[:, :WIDTH] * SCALE).astype(BF16).reshape(4, FEATS, WIDTH)
        )
        qkv[pl.ds(i * 4, 4), :, WIDTH:] = (
            out[:, WIDTH:].astype(BF16).reshape(4, FEATS, 2 * WIDTH)
        )
        return none

    lax.fori_loop(0, GROUP // 4, project, 0, unroll=4)

    moved = []

    def attend_rows(low, size):
        def attend(r, none):
            att[r] = attended(qkv, r)
            return none

        lax.fori_loop(low, low + size, attend, 0, unroll=size)

    def send_rows(low, size):
        def update(i, none):
            some = att[pl.ds(i * 4, 4)].reshape(4 * FEATS, WIDTH)
            out = jnp.dot(some, wout[...], preferred_element_type=F32)
            out = out + rows[pl.ds(i * 4, 4)].reshape(4 * FEATS, WIDTH).astype(F32)
            mix[pl.ds(i * 4 * FEATS, 4 * FEATS), :] = out
            return none

        lax.fori_loop(low // 4, (low + size) // 4, update, 0, unroll=2)

        def turn(f, none):
            send[f, low : low + size, :] = mix[
                pl.ds(low * FEATS + f, size, stride=FEATS), :
            ].astype(BF16)
            return none

        lax.fori_loop(0, FEATS, turn, 0, unroll=8)
        these = pl.ds(low, size)
        for k, to, to_row, tx in peers:
            at = (low // 8) * OWNERS + k
            copy = remote(
                send.at[pl.ds(to * OWNED, OWNED), these],
                q_out.at[owner, :, these],
                qs.at[at],
                qr.at[at],
                to_row,
                tx,
            )
            copy.start()
            moved.append(copy)
        q_out[owner, :, low : low + size, :] = send[
            pl.ds(owner * OWNED, OWNED), low : low + size, :
        ]

    attend_rows(0, 16)

    for copy in key_moved:
        copy.wait_recv()
    spot_here = z * CS + c
    for yy in range(YS):
        for f in range(OWNED):
            low = key_in[yy * XS, f].astype(F32) + key_in[yy * XS + 1, f].astype(F32)
            high = key_in[yy * XS + 2, f].astype(F32) + key_in[yy * XS + 3, f].astype(F32)
            kv_out[spot_here, f, yy * 16 : yy * 16 + 16, :] = jnp.concatenate(
                [low, high], axis=0
            ).astype(BF16)

    right, left = row_of(y, around(z, 1, ZS), c), row_of(y, around(z, -1, ZS), c)
    other = row_of(y, z, 1 - c)

    right_two, left_two = row_of(y, around(z, 2, ZS), c), row_of(y, around(z, -2, ZS), c)

    def part_of(d, features):
        return kv_out.at[around(z, d, ZS) * CS + c, pl.ds(*features)]

    def hop(d, features, sems, k, to):
        here_part = part_of(d, features)
        copy = remote(here_part, here_part, sems[0].at[k], sems[1].at[k], to, x)
        copy.start()
        sent.append(copy)

    def lands(d, features, sems, k):
        here_part = part_of(d, features)
        remote(here_part, here_part, sems[0].at[k], sems[1].at[k], right, x).wait_recv()

    every_feature, low_features, high_features = (0, OWNED), (0, 3), (3, OWNED - 3)

    def place_at(d, core):
        return kv_out.at[around(z, d, ZS) * CS + core]

    def over(d):
        whole = place_at(d, c)
        copy = remote(whole, whole, ps.at[d + 4], pr.at[d + 4], other, x)
        copy.start()
        sent.append(copy)

    hop(0, every_feature, (rs, rr), 0, right)
    hop(0, every_feature, (ls, lr), 0, left)
    hop(0, every_feature, (rs, rr), 1, right_two)
    hop(0, every_feature, (ls, lr), 1, left_two)
    over(0)

    def ring_step(k):
        if k == 0:
            lands(-1, every_feature, (rs, rr), 0)
            hop(-1, every_feature, (rs, rr), 2, right_two)
            lands(1, every_feature, (ls, lr), 0)
            hop(1, every_feature, (ls, lr), 2, left_two)
        if k == 1:
            lands(-2, every_feature, (rs, rr), 1)
            hop(-2, low_features, (rs, rr), 3, right_two)
            lands(2, every_feature, (ls, lr), 1)
            hop(2, high_features, (ls, lr), 3, left_two)
        if k == 2:
            lands(-3, every_feature, (rs, rr), 2)
            lands(3, every_feature, (ls, lr), 2)
        if k == 3:
            lands(-4, low_features, (rs, rr), 3)
            lands(-4, high_features, (ls, lr), 3)
        over(-1 - k)
        if k < 3:
            over(1 + k)

    def project_place(at):
        some = kv_out[at].reshape(OWNED * KEYS, WIDTH)
        got = jnp.dot(some, item_w[:, WIDTH:], preferred_element_type=F32)
        kvp[at] = got.astype(BF16).reshape(OWNED, KEYS, 2 * WIDTH)

    def mine(d):
        project_place(around(z, d, ZS) * CS + c)

    def others(d):
        came = place_at(d, 1 - c)
        remote(came, came, ps.at[d + 4], pr.at[d + 4], other, x).wait_recv()
        project_place(around(z, d, ZS) * CS + 1 - c)

    send_rows(0, 16)
    attend_rows(16, 8)
    send_rows(16, 8)
    ring_step(0)
    attend_rows(24, 8)
    send_rows(24, 8)
    ring_step(1)
    for d in (0, -1, 1):
        mine(d)
    others(0)
    ring_step(2)
    for copy in moved:
        copy.wait_recv()

    def project_q(i, none):
        some = q_out[i].reshape(OWNED * GROUP, WIDTH)
        got = jnp.dot(some, item_w[:, :WIDTH], preferred_element_type=F32)
        qp[i] = (got * SCALE).astype(BF16).reshape(OWNED, GROUP, WIDTH)
        return none

    lax.fori_loop(0, OWNERS, project_q, 0, unroll=4)
    mine(-2)
    mine(2)
    others(-1)
    others(1)
    ring_step(3)
    others(-2)
    others(2)
    mine(-3)
    mine(3)
    mine(-4)
    for d in (-3, 3, -4):
        others(d)

    for copy in stat_xy + [copy for _, copy in bulk] + stat_z + key_moved + moved + sent:
        copy.wait_send()


def attend_tile(key, value, stacked, mask, top, total, acc):
    scores = lax.dot_general(
        key, stacked, (((1,), (1,)), ((), ())), preferred_element_type=F32
    )
    scores = scores + mask
    new_top = jnp.maximum(top, jnp.max(scores, axis=0, keepdims=True))
    shares = jnp.exp2(scores - new_top)
    fade = jnp.exp2(top - new_top)
    total = total * fade + jnp.sum(shares, axis=0, keepdims=True)
    got = lax.dot_general(
        value, shares.astype(BF16), (((0,), (0,)), ((), ())), preferred_element_type=F32
    )
    parts = []
    for h in range(HEADS):
        rows = slice(h * HEAD_DIM, (h + 1) * HEAD_DIM)
        cols = slice(h * BLOCK, (h + 1) * BLOCK)
        parts.append(acc[rows] * fade[:, cols] + got[rows, cols])
    return new_top, total, jnp.concatenate(parts, axis=0)


def stack_heads(query):
    head = iota((BLOCK, WIDTH), 1) // HEAD_DIM
    return jnp.concatenate(
        [jnp.where(head == h, query, jnp.zeros_like(query)) for h in range(HEADS)], axis=0
    )


def list_kernel(
    qp, kvp, table_in, train_in,
    kv_first, bias_first, tops, totals, accs,
    table, train, in_sem, kv_more, bias_more, every, chosen,
):
    row, x, y, z, c = position()
    loads = [
        pltpu.make_async_copy(source, target, in_sem.at[i])
        for i, (source, target) in enumerate(
            ((table_in, table), (train_in, train))
        )
    ]
    for load in loads:
        load.start()
    tops[...] = jnp.full_like(tops, MASKED)
    totals[...] = jnp.zeros_like(totals)
    accs[...] = jnp.zeros_like(accs)
    for load in loads:
        load.wait()

    group = (iota((OWNERS, BLOCK), 1) // GROUP == iota((OWNERS, BLOCK), 0) // KEEP)
    spread = train[...].astype(F32)[:, None, :] * group.astype(F32)[None]
    counts = jnp.dot(
        spread.reshape(BLOCKS * OWNERS, BLOCK).astype(BF16),
        jnp.ones((BLOCK, WIDTH), BF16),
        preferred_element_type=F32,
    )
    number = (iota((BLOCKS * OWNERS, WIDTH), 0) % KEEP).astype(F32)
    every[...] = jnp.where(number < counts, 0.0, MASKED)
    nothing = jnp.zeros((16, 2 * WIDTH), BF16)
    masked = jnp.full((16, WIDTH), MASKED, F32)

    def one_block(yy, none):
        mine = table[row_of(yy, z, c)]
        n = jnp.int32(0)
        for j in range(BLOCKS):
            chosen[n] = j
            n = n + jnp.where(table[j] == mine, 1, 0)
        tiles = lax.div(n + 15, 16)

        def gather(i, none):
            j = chosen[i]
            at = pl.multiple_of(i * 16, 16)
            come = pl.multiple_of(lax.div(j, PLACES) * 16, 16)
            for f in range(OWNED):
                kv_first[yy, f, pl.ds(at, 16), :] = kvp[lax.rem(j, PLACES), f, pl.ds(come, 16), :]
            bias_first[yy, pl.ds(at, 16), :] = every[pl.ds(pl.multiple_of(j * 16, 16), 16), :]
            return none

        lax.fori_loop(0, jnp.minimum(n, 16), gather, 0)

        def tail(i, none):
            at = pl.multiple_of(i * 16, 16)
            for f in range(OWNED):
                kv_first[yy, f, pl.ds(at, 16), :] = nothing
            bias_first[yy, pl.ds(at, 16), :] = masked
            return none

        lax.fori_loop(jnp.minimum(n, 16), 16, tail, 0)

        @pl.when(tiles > 1)
        def _():
            def gather_more(i, none):
                j = chosen[i]
                at = pl.multiple_of((i - 16) * 16, 16)
                come = pl.multiple_of(lax.div(j, PLACES) * 16, 16)
                for f in range(OWNED):
                    kv_more[f, pl.ds(at, 16), :] = kvp[lax.rem(j, PLACES), f, pl.ds(come, 16), :]
                bias_more[pl.ds(at, 16), :] = every[pl.ds(pl.multiple_of(j * 16, 16), 16), :]
                return none

            lax.fori_loop(16, n, gather_more, 0)

            def tail_more(i, none):
                at = pl.multiple_of((i - 16) * 16, 16)
                for f in range(OWNED):
                    kv_more[f, pl.ds(at, 16), :] = nothing
                bias_more[pl.ds(at, 16), :] = masked
                return none

            lax.fori_loop(n, tiles * 16, tail_more, 0)

            def one_tile(kt, none):
                at = pl.multiple_of((kt - 1) * TILE, TILE)
                mask = jnp.concatenate([bias_more[pl.ds(at, TILE), :]] * HEADS, axis=1)
                for f in range(OWNED):
                    query = jnp.concatenate([qp[yy * XS + xx, f] for xx in range(XS)], axis=0)
                    tops[yy, f], totals[yy, f], accs[yy, f] = attend_tile(
                        kv_more[f, pl.ds(at, TILE), 0:WIDTH],
                        kv_more[f, pl.ds(at, TILE), WIDTH:],
                        stack_heads(query),
                        mask,
                        tops[yy, f],
                        totals[yy, f],
                        accs[yy, f],
                    )
                return none

            lax.fori_loop(1, tiles, one_tile, 0)

        return none

    lax.fori_loop(0, YS, one_block, 0)


def back_kernel(
    q_in, qp, kv_first, bias_first, tops, totals, accs, wout_in, out,
    wout, done, landed, wide, send_sems, recv_sems, own_sem,
):
    row, x, y, z, c = position()
    owner = y * XS + x
    load = pltpu.make_async_copy(wout_in, wout, own_sem.at[0])
    load.start()
    barrier = pltpu.get_barrier_semaphore()
    for dy in range(YS):
        for dx in range(XS):
            if dx or dy:
                peer = (row_of(around(y, dy, YS), z, c), around(x, dx, XS))
                pl.semaphore_signal(barrier, inc=1, device_id=peer, device_id_type=MESH)
    load.wait()
    sent = []

    def place(g):
        for f in range(OWNED):
            wide[pl.ds(g * OWNED + f, GROUP, stride=FEATS), :] = landed[g, f].astype(F32)

    def take(dy):
        for dx in (1, 3, 2, 0):
            if dx or dy:
                k = dy * XS + dx
                g = around(y, -dy, YS) * XS + around(x, -dx, XS)
                remote(
                    landed.at[g], landed.at[g], send_sems.at[k], recv_sems.at[k], row, x
                ).wait_recv()
                place(g)

    order = (2, 1, 3, 0)
    for turn, dy in enumerate(order):
        yy = around(y, dy, YS)
        mask = jnp.concatenate([bias_first[yy]] * HEADS, axis=1)
        for f in range(OWNED):
            query = jnp.concatenate([qp[yy * XS + xx, f] for xx in range(XS)], axis=0)
            _, total, acc = attend_tile(
                kv_first[yy, f, :, 0:WIDTH],
                kv_first[yy, f, :, WIDTH:],
                stack_heads(query),
                mask,
                tops[yy, f],
                totals[yy, f],
                accs[yy, f],
            )
            attended = jnp.concatenate(
                [
                    acc[h * HEAD_DIM : (h + 1) * HEAD_DIM]
                    * (1.0 / total[:, h * BLOCK : (h + 1) * BLOCK])
                    for h in range(HEADS)
                ],
                axis=0,
            ).astype(BF16)
            got = lax.dot_general(
                attended, wout[...], (((0,), (0,)), ((), ())), preferred_element_type=F32
            )
            for xx in range(XS):
                mixed = q_in[yy * XS + xx, f].astype(F32)
                done[yy * XS + xx, f] = (mixed + got[xx * GROUP : (xx + 1) * GROUP]).astype(BF16)
        if turn == 0:
            pl.semaphore_wait(barrier, OWNERS - 1)
        for dx in (2, 1, 3, 0):
            if dx or dy:
                k = dy * XS + dx
                tx = around(x, dx, XS)
                copy = remote(
                    done.at[yy * XS + tx],
                    landed.at[owner],
                    send_sems.at[k],
                    recv_sems.at[k],
                    row_of(yy, z, c),
                    tx,
                )
                copy.start()
                sent.append(copy)
        if turn >= 2:
            take(order[turn - 2])
    landed[owner] = done[owner]
    place(owner)
    take(order[2])
    take(order[3])

    def finish(i, none):
        some = wide[pl.ds(pl.multiple_of(i * 4 * FEATS, 64), 4 * FEATS), :]
        out[pl.ds(i * 4, 4)] = some.reshape(4, FEATS, WIDTH).astype(BF16)
        return none

    lax.fori_loop(0, GROUP // 4, finish, 0, unroll=2)
    for copy in sent:
        copy.wait_send()


def list_call(query, key, block_table, train):
    shape = jax.ShapeDtypeStruct
    state = shape((YS, OWNED, 1, HEADS * BLOCK), F32)
    return pl.pallas_call(
        list_kernel,
        name="list",
        out_shape=(
            shape((YS, OWNED, TILE, 2 * WIDTH), BF16),
            shape((YS, TILE, WIDTH), F32),
            state,
            state,
            shape((YS, OWNED, WIDTH, BLOCK), F32),
        ),
        in_specs=[VMEM, VMEM, HBM, HBM],
        out_specs=(VMEM,) * 5,
        scratch_shapes=[
            pltpu.SMEM((BLOCKS,), jnp.int32),
            pltpu.VMEM((BLOCKS, BLOCK), jnp.int32),
            pltpu.SemaphoreType.DMA((2,)),
            pltpu.VMEM((OWNED, PLACES * KEYS, 2 * WIDTH), BF16),
            pltpu.VMEM((PLACES * KEYS, WIDTH), F32),
            pltpu.VMEM((PLACES * KEYS, WIDTH), F32),
            pltpu.SMEM((BLOCKS + 8,), jnp.int32),
        ],
        compiler_params=pltpu.CompilerParams(vmem_limit_bytes=ITEM_VMEM),
    )(query, key, *stay(block_table, train))


def on_device(cells, block_table, row_live, row_train, feat_qkv, feat_out, item_qkv, item_out):
    train = row_train.reshape(BLOCKS, BLOCK)
    live = row_live.reshape(BLOCKS, BLOCK)
    by_feature = jnp.transpose(cells, (1, 0, 2))
    dma = pltpu.SemaphoreType.DMA
    moved = jax.ShapeDtypeStruct((OWNERS, OWNED, GROUP, WIDTH), BF16)
    mixed, query, key = pl.pallas_call(
        mix_kernel,
        name="mix",
        out_shape=(
            moved,
            moved,
            jax.ShapeDtypeStruct((PLACES, OWNED, KEYS, 2 * WIDTH), BF16),
        ),
        in_specs=[HBM] * 7,
        out_specs=(VMEM,) * 3,
        scratch_shapes=[
            pltpu.VMEM((PLACES, OWNED, KEYS, WIDTH), BF16),
            pltpu.VMEM((KEEP, FEATS, WIDTH), BF16),
            pltpu.VMEM((KEEP, FEATS, 3 * WIDTH), BF16),
            pltpu.VMEM((WIDTH, 3 * WIDTH), BF16),
            pltpu.SMEM((BLOCKS,), jnp.int32),
            pltpu.VMEM((BLOCKS, BLOCK), jnp.int32),
            pltpu.SMEM((BLOCKS * BLOCK,), jnp.int32),
            pltpu.VMEM((WIDTH, 3 * WIDTH), BF16),
            pltpu.VMEM((WIDTH, WIDTH), BF16),
            dma((6,)),
            pltpu.VMEM((SHARD, BLOCK, WIDTH), BF16),
            pltpu.VMEM((FEATS, GROUP, WIDTH), BF16),
            pltpu.VMEM((SHARD, WIDTH), F32),
            pltpu.VMEM((SHARD, WIDTH), F32),
            pltpu.VMEM((FEATS, WIDTH), F32),
            pltpu.VMEM((FEATS, WIDTH), F32),
            pltpu.VMEM((2, WIDTH), F32),
            pltpu.VMEM((YS * CS, XS, 2, WIDTH), F32),
            pltpu.VMEM((2, YS * CS, WIDTH), F32),
            pltpu.VMEM((ZS, 2, YS * CS, WIDTH), F32),
            pltpu.VMEM((BLOCKS, WIDTH), F32),
            pltpu.VMEM((GROUP * FEATS, WIDTH), F32),
            pltpu.VMEM((GROUP, FEATS, WIDTH), BF16),
            pltpu.VMEM((GROUP, FEATS, 3 * WIDTH), BF16),
            pltpu.VMEM((GROUP, FEATS, WIDTH), BF16),
            pltpu.VMEM((GROUP * FEATS, WIDTH), F32),
            pltpu.VMEM((FEATS, GROUP, WIDTH), BF16),
            pltpu.VMEM((FEATS * 8, WIDTH), F32),
            pltpu.VMEM((FEATS, 8, WIDTH), BF16),
            pltpu.VMEM((OWNERS, OWNED, 8, WIDTH), BF16),
            dma((2,)),
            dma((XS,)), dma((XS,)), dma((OWNERS * CS,)), dma((OWNERS * CS,)),
            dma((8,)), dma((8,)),
            dma((OWNERS,)), dma((OWNERS,)), dma((4 * OWNERS,)), dma((4 * OWNERS,)),
            dma((4,)), dma((4,)), dma((4,)), dma((4,)),
            dma((8,)), dma((8,)),
        ],
        compiler_params=pltpu.CompilerParams(
            collective_id=0, has_side_effects=True, vmem_limit_bytes=MIX_VMEM
        ),
    )(*stay(by_feature, block_table, live, row_train, feat_qkv, feat_out, item_qkv))
    listed = list_call(query, key, block_table, train)
    return pl.pallas_call(
        back_kernel,
        name="back",
        out_shape=jax.ShapeDtypeStruct((GROUP, FEATS, WIDTH), BF16),
        in_specs=[VMEM] * 7 + [HBM],
        out_specs=VMEM,
        scratch_shapes=[
            pltpu.VMEM((WIDTH, WIDTH), BF16),
            pltpu.VMEM((OWNERS, OWNED, GROUP, WIDTH), BF16),
            pltpu.VMEM((OWNERS, OWNED, GROUP, WIDTH), BF16),
            pltpu.VMEM((GROUP * FEATS, WIDTH), F32),
            dma((OWNERS,)), dma((OWNERS,)), dma((1,)),
        ],
        compiler_params=pltpu.CompilerParams(
            collective_id=1, has_side_effects=True, vmem_limit_bytes=BACK_VMEM
        ),
    )(mixed, query, *listed, *stay(item_out))


def solution(mesh):
    return jax.shard_map(
        on_device,
        mesh=mesh,
        in_specs=(P("rows", "feat", None), P(), P(), P(), P(), P(), P(), P()),
        out_specs=P(("rows", "feat"), None, None),
        check_vma=False,
    )
```

```python
import jax
import jax.numpy as jnp
from jax import lax
from jax.experimental import pallas as pl
from jax.experimental.pallas import tpu as pltpu
from jax.sharding import PartitionSpec as P

HEADS = 4
HEAD_DIM = 32
WIDTH = 128
KEEP = 4
XS, YS, ZS, CS = 4, 4, 8, 2
BLOCKS = YS * ZS * CS
BLOCK = 128
FEATS = 80
SHARD = 20
OWNED = 5
GROUP = 32
OWNERS = XS * YS
PLACES = ZS * CS
KEYS = YS * XS * KEEP
TILE = 256
EPSILON = 1e-05
MASKED = -1e30
SCALE = HEAD_DIM**-0.5 * 1.4426950408889634
MESH = pl.DeviceIdType.MESH
MIX_VMEM = 20 << 20
ITEM_VMEM = 20 << 20
BACK_VMEM = 12 << 20
F32 = jnp.float32
BF16 = jnp.bfloat16
VMEM = pl.BlockSpec(memory_space=pltpu.VMEM)
SMEM = pl.BlockSpec(memory_space=pltpu.SMEM)
ANY = pl.BlockSpec(memory_space=pl.ANY)
HBM = pl.BlockSpec(memory_space=pltpu.HBM)


def iota(shape, dim):
    return lax.broadcasted_iota(jnp.int32, shape, dim)


def row_of(y, z, c):
    return y * (ZS * CS) + z * CS + c


def around(at, step, size):
    return lax.rem(at + step + size, size)


def remote(source, target, send, recv, row, feat):
    return pltpu.make_async_remote_copy(
        src_ref=source,
        dst_ref=target,
        send_sem=send,
        recv_sem=recv,
        device_id=(row, feat),
        device_id_type=MESH,
    )


def stay(*arrays):
    return [pltpu.with_memory_space_constraint(a, pltpu.HBM) for a in arrays]


def position():
    row = lax.axis_index("rows")
    x = lax.axis_index("feat")
    y = lax.div(row, ZS * CS)
    z = lax.rem(lax.div(row, CS), ZS)
    c = lax.rem(row, CS)
    return row, x, y, z, c


def mix_kernel(
    cells, table_in, live_in, train_in, wqkv_in, wout_in, item_in, q_out, qp, kvp,
    kv_out, key_rows, key_qkv, item_w, table, live, train, wqkv, wout, in_sem, own, xbuf, part, level, mean_of, inv_of, st_src, sxy, sz_src, sz, counts, nrm, rows, qkv, att, mix, send,
    key_wide, key_send, key_in,
    own_sem, xs, xr, ss, sr, zs, zr, ks, kr, qs, qr, rs, rr, ls, lr, ps, pr,
):
    row, x, y, z, c = position()
    owner = y * XS + x

    fetch = pltpu.make_async_copy(cells, own, own_sem.at[0])
    fetch.start()
    loads = [
        pltpu.make_async_copy(source, target, in_sem.at[i])
        for i, (source, target) in enumerate(
            ((live_in, live), (table_in, table), (train_in, train), (wqkv_in, wqkv), (wout_in, wout),
             (item_in, item_w))
        )
    ]
    for load in loads:
        load.start()
    barrier = pltpu.get_barrier_semaphore()
    greet = []
    plane = [
        (dx, dy, dc) for dy in range(YS) for dc in range(CS) for dx in range(XS) if dx or dy or dc
    ]
    for dx, dy, dc in plane:
        greet.append((row_of(around(y, dy, YS), z, around(c, dc, CS)), around(x, dx, XS)))
    for dz in range(1, ZS):
        greet.append((row_of(y, around(z, dz, ZS), c), x))
    for peer in greet:
        pl.semaphore_signal(barrier, inc=1, device_id=peer, device_id_type=MESH)
    fetch.wait()
    for load in loads:
        load.wait()

    square = iota((BLOCK, WIDTH), 0) == iota((BLOCK, WIDTH), 1)
    flags = live[pl.ds(row, 1), :].astype(F32)
    weight = jnp.broadcast_to(
        jnp.sum(jnp.where(square, flags, 0.0), axis=1, keepdims=True), (BLOCK, WIDTH)
    )
    entries = jnp.broadcast_to(jnp.sum(flags, axis=1, keepdims=True) * WIDTH, (SHARD, WIDTH))

    def add_first(f, none):
        part[pl.ds(f, 1), :] = jnp.sum(own[f].astype(F32) * weight, axis=0, keepdims=True)
        return none

    lax.fori_loop(0, SHARD, add_first, 0, unroll=4)
    first = jnp.sum(part[...], axis=1, keepdims=True)
    level[...] = jnp.broadcast_to(first, (SHARD, WIDTH)) / entries

    def add_second(f, none):
        off = own[f].astype(F32) - level[pl.ds(f, 1), :]
        part[pl.ds(f, 1), :] = jnp.sum(off * off * weight, axis=0, keepdims=True)
        return none

    lax.fori_loop(0, SHARD, add_second, 0, unroll=4)
    second = jnp.sum(part[...], axis=1, keepdims=True)
    lane = iota((SHARD, WIDTH), 1)
    sub = iota((SHARD, WIDTH), 0)
    spot = lane == sub + GROUP * x

    def to_row(column):
        return jnp.sum(jnp.where(spot, column, 0.0), axis=0, keepdims=True)

    st_src[...] = jnp.concatenate(
        [to_row(first), to_row(second)], axis=0
    )
    counts[...] = WIDTH * jnp.dot(
        live[...].astype(F32).astype(BF16),
        jnp.ones((BLOCK, WIDTH), BF16),
        preferred_element_type=F32,
    )
    key_wide[...] = jnp.zeros_like(key_wide)
    pl.semaphore_wait(barrier, len(greet))

    here = y * CS + c
    stat_xy = []
    for dx, dy, dc in plane:
        k = (dy * CS + dc) * XS + dx
        to = row_of(around(y, dy, YS), z, around(c, dc, CS))
        copy = remote(st_src, sxy.at[here, x], ss.at[k], sr.at[k], to, around(x, dx, XS))
        copy.start()
        stat_xy.append(copy)
    bulk = []
    for d in (2, 1, 3):
        to = around(x, d, XS)
        copy = remote(
            cells.at[:, pl.ds(pl.multiple_of(to * GROUP, GROUP), GROUP)],
            xbuf.at[pl.ds(x * SHARD, SHARD)],
            xs.at[d],
            xr.at[d],
            row,
            to,
        )
        copy.start()
        bulk.append((d, copy))
    keep = pltpu.make_async_copy(
        own.at[:, pl.ds(pl.multiple_of(x * GROUP, GROUP), GROUP)],
        xbuf.at[pl.ds(x * SHARD, SHARD)],
        own_sem.at[1],
    )
    keep.start()
    sxy[here, x] = st_src[...]
    for dx, dy, dc in plane:
        k = (dy * CS + dc) * XS + dx
        came = sxy.at[around(y, -dy, YS) * CS + around(c, dc, CS), around(x, -dx, XS)]
        remote(came, came, ss.at[k], sr.at[k], row, x).wait_recv()
    merged = [
        sxy[i, 0] + sxy[i, 1] + sxy[i, 2] + sxy[i, 3] for i in range(YS * CS)
    ]
    for k in range(2):
        tile = jnp.concatenate([merged[i][k : k + 1] for i in range(YS * CS)], axis=0)
        sz_src[k] = tile
        sz[z, k] = tile
    stat_z = []
    for d in range(1, ZS):
        copy = remote(
            sz_src, sz.at[z], zs.at[d], zr.at[d], row_of(y, around(z, d, ZS), c), x
        )
        copy.start()
        stat_z.append(copy)
    spots = [jnp.int32(0)] * KEEP
    seen = jnp.int32(0)
    for r in range(GROUP):
        flag = train[row * BLOCK + x * GROUP + r]
        for j in range(KEEP):
            spots[j] = jnp.where((flag == 1) & (seen == j), r, spots[j])
        seen = seen + flag
    here_table = table[row]
    weights = [jnp.where(table[b] == here_table, 1.0, 0.0).astype(F32) for b in range(BLOCKS)]
    entries_all = jnp.zeros((1, WIDTH), F32)
    for b in range(BLOCKS):
        entries_all = entries_all + weights[b] * counts[b : b + 1, :]
    for d in range(1, ZS):
        came = around(z, -d, ZS)
        remote(sz_src, sz.at[came], zs.at[d], zr.at[d], row, x).wait_recv()

    places = [
        (zz, i, row_of(i // CS, zz, i % CS)) for zz in range(ZS) for i in range(YS * CS)
    ]
    acc = jnp.zeros((1, WIDTH), F32)
    for zz, i, b in places:
        acc = acc + weights[b] * sz[zz, 0, i : i + 1, :]
    mean_row = acc / entries_all
    spread = jnp.zeros((1, WIDTH), F32)
    for zz, i, b in places:
        entries_b = counts[b : b + 1, :]
        off = sz[zz, 0, i : i + 1, :] / entries_b - mean_row
        spread = spread + weights[b] * (sz[zz, 1, i : i + 1, :] + entries_b * (off * off))
    inv_row = lax.rsqrt(spread / entries_all + EPSILON)

    for d, _ in bulk:
        came = xbuf.at[pl.ds(around(x, -d, XS) * SHARD, SHARD)]
        remote(came, came, xs.at[d], xr.at[d], row, x).wait_recv()
    keep.wait()
    for s in range(XS):
        pick = lane == sub + GROUP * s
        for ref, values in ((mean_of, mean_row), (inv_of, inv_row)):
            column = jnp.sum(jnp.where(pick, values, 0.0), axis=1, keepdims=True)
            ref[SHARD * s : SHARD * (s + 1), :] = jnp.broadcast_to(column, (SHARD, WIDTH))

    def norm(f, none):
        value = (xbuf[f].astype(F32) - mean_of[pl.ds(f, 1), :]) * inv_of[pl.ds(f, 1), :]
        nrm[pl.ds(pl.multiple_of(f * GROUP, GROUP), GROUP), :] = value.astype(BF16).astype(F32)
        return none

    lax.fori_loop(0, FEATS, norm, 0, unroll=8)

    def by_row(r, none):
        rows[r] = nrm[pl.ds(r, FEATS, stride=GROUP), :].astype(BF16)
        return none

    lax.fori_loop(0, GROUP, by_row, 0, unroll=8)

    head = iota((FEATS, WIDTH), 1) // HEAD_DIM
    def attended(source, r):
        query = source[r, :, 0:WIDTH]
        key = source[r, :, WIDTH : 2 * WIDTH]
        value = source[r, :, 2 * WIDTH :]
        keys = jnp.concatenate(
            [jnp.where(head == h, key, jnp.zeros_like(key)) for h in range(HEADS)], axis=0
        )
        values = jnp.concatenate(
            [jnp.where(head == h, value, jnp.zeros_like(value)) for h in range(HEADS)], axis=0
        )
        scores = lax.dot_general(
            keys, query, (((1,), (1,)), ((), ())), preferred_element_type=F32
        )
        shares = []
        for h in range(HEADS):
            some = scores[h * FEATS : (h + 1) * FEATS]
            some = jnp.exp2(some - jnp.max(some, axis=0, keepdims=True))
            shares.append((some * (1.0 / jnp.sum(some, axis=0, keepdims=True))).astype(BF16))
        return lax.dot_general(
            jnp.concatenate(shares, axis=0),
            values,
            (((0,), (0,)), ((), ())),
            preferred_element_type=F32,
        ).astype(BF16)

    for j in range(KEEP):
        key_rows[j] = rows[spots[j]]
    some = key_rows[...].reshape(KEEP * FEATS, WIDTH)
    out = jnp.dot(some, wqkv[...], preferred_element_type=F32)
    key_qkv[:, :, 0:WIDTH] = (out[:, :WIDTH] * SCALE).astype(BF16).reshape(KEEP, FEATS, WIDTH)
    key_qkv[:, :, WIDTH:] = out[:, WIDTH:].astype(BF16).reshape(KEEP, FEATS, 2 * WIDTH)
    found = jnp.concatenate([attended(key_qkv, j) for j in range(KEEP)], axis=0)
    out = jnp.dot(found, wout[...], preferred_element_type=F32)
    out = out + key_rows[...].reshape(KEEP * FEATS, WIDTH).astype(F32)
    for j in range(KEEP):
        key_wide[pl.ds(KEEP * lax.rem(x, 2) + j, FEATS, stride=8), :] = out[
            j * FEATS : (j + 1) * FEATS
        ]
    key_send[...] = key_wide[...].reshape(FEATS, 8, WIDTH).astype(BF16)
    peers = []
    for dy in range(YS):
        for dx in range(XS):
            if dx or dy:
                ty, tx = around(y, dy, YS), around(x, dx, XS)
                peers.append((dy * XS + dx, ty * XS + tx, row_of(ty, z, c), tx))
    peers.sort(key=lambda peer: -min(peer[0] // XS, YS - peer[0] // XS) - min(peer[0] % XS, XS - peer[0] % XS))
    sent = []
    key_moved = []
    for k, to, to_row, tx in peers:
        copy = remote(
            key_send.at[pl.ds(to * OWNED, OWNED)], key_in.at[owner], ks.at[k], kr.at[k], to_row, tx
        )
        copy.start()
        key_moved.append(copy)
    key_in[owner] = key_send[pl.ds(owner * OWNED, OWNED)]

    def project(i, none):
        some = rows[pl.ds(i * 4, 4)].reshape(4 * FEATS, WIDTH)
        out = jnp.dot(some, wqkv[...], preferred_element_type=F32)
        qkv[pl.ds(i * 4, 4), :, 0:WIDTH] = (
            (out[:, :WIDTH] * SCALE).astype(BF16).reshape(4, FEATS, WIDTH)
        )
        qkv[pl.ds(i * 4, 4), :, WIDTH:] = (
            out[:, WIDTH:].astype(BF16).reshape(4, FEATS, 2 * WIDTH)
        )
        return none

    lax.fori_loop(0, GROUP // 4, project, 0, unroll=4)

    moved = []

    def attend_rows(low, size):
        def attend(r, none):
            att[r] = attended(qkv, r)
            return none

        lax.fori_loop(low, low + size, attend, 0, unroll=size)

    def send_rows(low, size):
        def update(i, none):
            some = att[pl.ds(i * 4, 4)].reshape(4 * FEATS, WIDTH)
            out = jnp.dot(some, wout[...], preferred_element_type=F32)
            out = out + rows[pl.ds(i * 4, 4)].reshape(4 * FEATS, WIDTH).astype(F32)
            mix[pl.ds(i * 4 * FEATS, 4 * FEATS), :] = out
            return none

        lax.fori_loop(low // 4, (low + size) // 4, update, 0, unroll=2)

        def turn(f, none):
            send[f, low : low + size, :] = mix[
                pl.ds(low * FEATS + f, size, stride=FEATS), :
            ].astype(BF16)
            return none

        lax.fori_loop(0, FEATS, turn, 0, unroll=8)
        these = pl.ds(low, size)
        for k, to, to_row, tx in peers:
            at = (low // 8) * OWNERS + k
            copy = remote(
                send.at[pl.ds(to * OWNED, OWNED), these],
                q_out.at[owner, :, these],
                qs.at[at],
                qr.at[at],
                to_row,
                tx,
            )
            copy.start()
            moved.append(copy)
        q_out[owner, :, low : low + size, :] = send[
            pl.ds(owner * OWNED, OWNED), low : low + size, :
        ]

    attend_rows(0, 16)

    for copy in key_moved:
        copy.wait_recv()
    spot_here = z * CS + c
    for yy in range(YS):
        for f in range(OWNED):
            low = key_in[yy * XS, f].astype(F32) + key_in[yy * XS + 1, f].astype(F32)
            high = key_in[yy * XS + 2, f].astype(F32) + key_in[yy * XS + 3, f].astype(F32)
            kv_out[spot_here, f, yy * 16 : yy * 16 + 16, :] = jnp.concatenate(
                [low, high], axis=0
            ).astype(BF16)

    right, left = row_of(y, around(z, 1, ZS), c), row_of(y, around(z, -1, ZS), c)
    other = row_of(y, z, 1 - c)

    right_two, left_two = row_of(y, around(z, 2, ZS), c), row_of(y, around(z, -2, ZS), c)

    def part_of(d, features):
        return kv_out.at[around(z, d, ZS) * CS + c, pl.ds(*features)]

    def hop(d, features, sems, k, to):
        here_part = part_of(d, features)
        copy = remote(here_part, here_part, sems[0].at[k], sems[1].at[k], to, x)
        copy.start()
        sent.append(copy)

    def lands(d, features, sems, k):
        here_part = part_of(d, features)
        remote(here_part, here_part, sems[0].at[k], sems[1].at[k], right, x).wait_recv()

    every_feature, low_features, high_features = (0, OWNED), (0, 3), (3, OWNED - 3)

    def place_at(d, core):
        return kv_out.at[around(z, d, ZS) * CS + core]

    def over(d):
        whole = place_at(d, c)
        copy = remote(whole, whole, ps.at[d + 4], pr.at[d + 4], other, x)
        copy.start()
        sent.append(copy)

    hop(0, every_feature, (rs, rr), 0, right)
    hop(0, every_feature, (ls, lr), 0, left)
    hop(0, every_feature, (rs, rr), 1, right_two)
    hop(0, every_feature, (ls, lr), 1, left_two)
    over(0)

    def ring_step(k):
        if k == 0:
            lands(-1, every_feature, (rs, rr), 0)
            hop(-1, every_feature, (rs, rr), 2, right_two)
            lands(1, every_feature, (ls, lr), 0)
            hop(1, every_feature, (ls, lr), 2, left_two)
        if k == 1:
            lands(-2, every_feature, (rs, rr), 1)
            hop(-2, low_features, (rs, rr), 3, right_two)
            lands(2, every_feature, (ls, lr), 1)
            hop(2, high_features, (ls, lr), 3, left_two)
        if k == 2:
            lands(-3, every_feature, (rs, rr), 2)
            lands(3, every_feature, (ls, lr), 2)
        if k == 3:
            lands(-4, low_features, (rs, rr), 3)
            lands(-4, high_features, (ls, lr), 3)
        over(-1 - k)
        if k < 3:
            over(1 + k)

    def project_place(at):
        some = kv_out[at].reshape(OWNED * KEYS, WIDTH)
        got = jnp.dot(some, item_w[:, WIDTH:], preferred_element_type=F32)
        kvp[at] = got.astype(BF16).reshape(OWNED, KEYS, 2 * WIDTH)

    def mine(d):
        project_place(around(z, d, ZS) * CS + c)

    def others(d):
        came = place_at(d, 1 - c)
        remote(came, came, ps.at[d + 4], pr.at[d + 4], other, x).wait_recv()
        project_place(around(z, d, ZS) * CS + 1 - c)

    send_rows(0, 16)
    attend_rows(16, 8)
    send_rows(16, 8)
    ring_step(0)
    attend_rows(24, 8)
    send_rows(24, 8)
    ring_step(1)
    for d in (0, -1, 1):
        mine(d)
    others(0)
    ring_step(2)
    for copy in moved:
        copy.wait_recv()

    def project_q(i, none):
        some = q_out[i].reshape(OWNED * GROUP, WIDTH)
        got = jnp.dot(some, item_w[:, :WIDTH], preferred_element_type=F32)
        qp[i] = (got * SCALE).astype(BF16).reshape(OWNED, GROUP, WIDTH)
        return none

    lax.fori_loop(0, OWNERS, project_q, 0, unroll=4)
    mine(-2)
    mine(2)
    others(-1)
    others(1)
    ring_step(3)
    others(-2)
    others(2)
    mine(-3)
    mine(3)
    mine(-4)
    for d in (-3, 3, -4):
        others(d)

    for copy in stat_xy + [copy for _, copy in bulk] + stat_z + key_moved + moved + sent:
        copy.wait_send()


def attend_tile(key, value, stacked, mask, top, total, acc):
    scores = lax.dot_general(
        key, stacked, (((1,), (1,)), ((), ())), preferred_element_type=F32
    )
    scores = scores + mask
    new_top = jnp.maximum(top, jnp.max(scores, axis=0, keepdims=True))
    shares = jnp.exp2(scores - new_top)
    fade = jnp.exp2(top - new_top)
    total = total * fade + jnp.sum(shares, axis=0, keepdims=True)
    got = lax.dot_general(
        value, shares.astype(BF16), (((0,), (0,)), ((), ())), preferred_element_type=F32
    )
    parts = []
    for h in range(HEADS):
        rows = slice(h * HEAD_DIM, (h + 1) * HEAD_DIM)
        cols = slice(h * BLOCK, (h + 1) * BLOCK)
        parts.append(acc[rows] * fade[:, cols] + got[rows, cols])
    return new_top, total, jnp.concatenate(parts, axis=0)


def stack_heads(query):
    head = iota((BLOCK, WIDTH), 1) // HEAD_DIM
    return jnp.concatenate(
        [jnp.where(head == h, query, jnp.zeros_like(query)) for h in range(HEADS)], axis=0
    )


def list_kernel(
    qp, kvp, table_in, train_in,
    kv_first, bias_first, tops, totals, accs,
    table, train, in_sem, kv_more, bias_more, every, chosen,
):
    row, x, y, z, c = position()
    loads = [
        pltpu.make_async_copy(source, target, in_sem.at[i])
        for i, (source, target) in enumerate(
            ((table_in, table), (train_in, train))
        )
    ]
    for load in loads:
        load.start()
    tops[...] = jnp.full_like(tops, MASKED)
    totals[...] = jnp.zeros_like(totals)
    accs[...] = jnp.zeros_like(accs)
    for load in loads:
        load.wait()

    group = (iota((OWNERS, BLOCK), 1) // GROUP == iota((OWNERS, BLOCK), 0) // KEEP)
    spread = train[...].astype(F32)[:, None, :] * group.astype(F32)[None]
    counts = jnp.dot(
        spread.reshape(BLOCKS * OWNERS, BLOCK).astype(BF16),
        jnp.ones((BLOCK, WIDTH), BF16),
        preferred_element_type=F32,
    )
    number = (iota((BLOCKS * OWNERS, WIDTH), 0) % KEEP).astype(F32)
    every[...] = jnp.where(number < counts, 0.0, MASKED)
    nothing = jnp.zeros((16, 2 * WIDTH), BF16)
    masked = jnp.full((16, WIDTH), MASKED, F32)

    def one_block(yy, none):
        mine = table[row_of(yy, z, c)]
        n = jnp.int32(0)
        for j in range(BLOCKS):
            chosen[n] = j
            n = n + jnp.where(table[j] == mine, 1, 0)
        tiles = lax.div(n + 15, 16)

        def gather(i, none):
            j = chosen[i]
            at = pl.multiple_of(i * 16, 16)
            come = pl.multiple_of(lax.div(j, PLACES) * 16, 16)
            for f in range(OWNED):
                kv_first[yy, f, pl.ds(at, 16), :] = kvp[lax.rem(j, PLACES), f, pl.ds(come, 16), :]
            bias_first[yy, pl.ds(at, 16), :] = every[pl.ds(pl.multiple_of(j * 16, 16), 16), :]
            return none

        lax.fori_loop(0, jnp.minimum(n, 16), gather, 0)

        def tail(i, none):
            at = pl.multiple_of(i * 16, 16)
            for f in range(OWNED):
                kv_first[yy, f, pl.ds(at, 16), :] = nothing
            bias_first[yy, pl.ds(at, 16), :] = masked
            return none

        lax.fori_loop(jnp.minimum(n, 16), 16, tail, 0)

        @pl.when(tiles > 1)
        def _():
            def gather_more(i, none):
                j = chosen[i]
                at = pl.multiple_of((i - 16) * 16, 16)
                come = pl.multiple_of(lax.div(j, PLACES) * 16, 16)
                for f in range(OWNED):
                    kv_more[f, pl.ds(at, 16), :] = kvp[lax.rem(j, PLACES), f, pl.ds(come, 16), :]
                bias_more[pl.ds(at, 16), :] = every[pl.ds(pl.multiple_of(j * 16, 16), 16), :]
                return none

            lax.fori_loop(16, n, gather_more, 0)

            def tail_more(i, none):
                at = pl.multiple_of((i - 16) * 16, 16)
                for f in range(OWNED):
                    kv_more[f, pl.ds(at, 16), :] = nothing
                bias_more[pl.ds(at, 16), :] = masked
                return none

            lax.fori_loop(n, tiles * 16, tail_more, 0)

            def one_tile(kt, none):
                at = pl.multiple_of((kt - 1) * TILE, TILE)
                mask = jnp.concatenate([bias_more[pl.ds(at, TILE), :]] * HEADS, axis=1)
                for f in range(OWNED):
                    query = jnp.concatenate([qp[yy * XS + xx, f] for xx in range(XS)], axis=0)
                    tops[yy, f], totals[yy, f], accs[yy, f] = attend_tile(
                        kv_more[f, pl.ds(at, TILE), 0:WIDTH],
                        kv_more[f, pl.ds(at, TILE), WIDTH:],
                        stack_heads(query),
                        mask,
                        tops[yy, f],
                        totals[yy, f],
                        accs[yy, f],
                    )
                return none

            lax.fori_loop(1, tiles, one_tile, 0)

        return none

    lax.fori_loop(0, YS, one_block, 0)


def back_kernel(
    q_in, qp, kv_first, bias_first, tops, totals, accs, wout_in, out,
    wout, done, landed, wide, send_sems, recv_sems, own_sem,
):
    row, x, y, z, c = position()
    owner = y * XS + x
    load = pltpu.make_async_copy(wout_in, wout, own_sem.at[0])
    load.start()
    barrier = pltpu.get_barrier_semaphore()
    for dy in range(YS):
        for dx in range(XS):
            if dx or dy:
                peer = (row_of(around(y, dy, YS), z, c), around(x, dx, XS))
                pl.semaphore_signal(barrier, inc=1, device_id=peer, device_id_type=MESH)
    load.wait()
    sent = []

    def place(g):
        for f in range(OWNED):
            wide[pl.ds(g * OWNED + f, GROUP, stride=FEATS), :] = landed[g, f].astype(F32)

    def take(dy):
        for dx in (1, 3, 2, 0):
            if dx or dy:
                k = dy * XS + dx
                g = around(y, -dy, YS) * XS + around(x, -dx, XS)
                remote(
                    landed.at[g], landed.at[g], send_sems.at[k], recv_sems.at[k], row, x
                ).wait_recv()
                place(g)

    order = (2, 1, 3, 0)
    for turn, dy in enumerate(order):
        yy = around(y, dy, YS)
        mask = jnp.concatenate([bias_first[yy]] * HEADS, axis=1)
        for f in range(OWNED):
            query = jnp.concatenate([qp[yy * XS + xx, f] for xx in range(XS)], axis=0)
            _, total, acc = attend_tile(
                kv_first[yy, f, :, 0:WIDTH],
                kv_first[yy, f, :, WIDTH:],
                stack_heads(query),
                mask,
                tops[yy, f],
                totals[yy, f],
                accs[yy, f],
            )
            attended = jnp.concatenate(
                [
                    acc[h * HEAD_DIM : (h + 1) * HEAD_DIM]
                    * (1.0 / total[:, h * BLOCK : (h + 1) * BLOCK])
                    for h in range(HEADS)
                ],
                axis=0,
            ).astype(BF16)
            got = lax.dot_general(
                attended, wout[...], (((0,), (0,)), ((), ())), preferred_element_type=F32
            )
            for xx in range(XS):
                mixed = q_in[yy * XS + xx, f].astype(F32)
                done[yy * XS + xx, f] = (mixed + got[xx * GROUP : (xx + 1) * GROUP]).astype(BF16)
        if turn == 0:
            pl.semaphore_wait(barrier, OWNERS - 1)
        for dx in (2, 1, 3, 0):
            if dx or dy:
                k = dy * XS + dx
                tx = around(x, dx, XS)
                copy = remote(
                    done.at[yy * XS + tx],
                    landed.at[owner],
                    send_sems.at[k],
                    recv_sems.at[k],
                    row_of(yy, z, c),
                    tx,
                )
                copy.start()
                sent.append(copy)
        if turn >= 2:
            take(order[turn - 2])
    landed[owner] = done[owner]
    place(owner)
    take(order[2])
    take(order[3])

    def finish(i, none):
        some = wide[pl.ds(pl.multiple_of(i * 4 * FEATS, 64), 4 * FEATS), :]
        out[pl.ds(i * 4, 4)] = some.reshape(4, FEATS, WIDTH).astype(BF16)
        return none

    lax.fori_loop(0, GROUP // 4, finish, 0, unroll=2)
    for copy in sent:
        copy.wait_send()


def list_call(query, key, block_table, train):
    shape = jax.ShapeDtypeStruct
    state = shape((YS, OWNED, 1, HEADS * BLOCK), F32)
    return pl.pallas_call(
        list_kernel,
        name="list",
        out_shape=(
            shape((YS, OWNED, TILE, 2 * WIDTH), BF16),
            shape((YS, TILE, WIDTH), F32),
            state,
            state,
            shape((YS, OWNED, WIDTH, BLOCK), F32),
        ),
        in_specs=[VMEM, VMEM, HBM, HBM],
        out_specs=(VMEM,) * 5,
        scratch_shapes=[
            pltpu.SMEM((BLOCKS,), jnp.int32),
            pltpu.VMEM((BLOCKS, BLOCK), jnp.int32),
            pltpu.SemaphoreType.DMA((2,)),
            pltpu.VMEM((OWNED, PLACES * KEYS, 2 * WIDTH), BF16),
            pltpu.VMEM((PLACES * KEYS, WIDTH), F32),
            pltpu.VMEM((PLACES * KEYS, WIDTH), F32),
            pltpu.SMEM((BLOCKS + 8,), jnp.int32),
        ],
        compiler_params=pltpu.CompilerParams(vmem_limit_bytes=ITEM_VMEM),
    )(query, key, *stay(block_table, train))


def on_device(cells, block_table, row_live, row_train, feat_qkv, feat_out, item_qkv, item_out):
    train = row_train.reshape(BLOCKS, BLOCK)
    live = row_live.reshape(BLOCKS, BLOCK)
    by_feature = jnp.transpose(cells, (1, 0, 2))
    dma = pltpu.SemaphoreType.DMA
    moved = jax.ShapeDtypeStruct((OWNERS, OWNED, GROUP, WIDTH), BF16)
    mixed, query, key = pl.pallas_call(
        mix_kernel,
        name="mix",
        out_shape=(
            moved,
            moved,
            jax.ShapeDtypeStruct((PLACES, OWNED, KEYS, 2 * WIDTH), BF16),
        ),
        in_specs=[HBM] * 7,
        out_specs=(VMEM,) * 3,
        scratch_shapes=[
            pltpu.VMEM((PLACES, OWNED, KEYS, WIDTH), BF16),
            pltpu.VMEM((KEEP, FEATS, WIDTH), BF16),
            pltpu.VMEM((KEEP, FEATS, 3 * WIDTH), BF16),
            pltpu.VMEM((WIDTH, 3 * WIDTH), BF16),
            pltpu.SMEM((BLOCKS,), jnp.int32),
            pltpu.VMEM((BLOCKS, BLOCK), jnp.int32),
            pltpu.SMEM((BLOCKS * BLOCK,), jnp.int32),
            pltpu.VMEM((WIDTH, 3 * WIDTH), BF16),
            pltpu.VMEM((WIDTH, WIDTH), BF16),
            dma((6,)),
            pltpu.VMEM((SHARD, BLOCK, WIDTH), BF16),
            pltpu.VMEM((FEATS, GROUP, WIDTH), BF16),
            pltpu.VMEM((SHARD, WIDTH), F32),
            pltpu.VMEM((SHARD, WIDTH), F32),
            pltpu.VMEM((FEATS, WIDTH), F32),
            pltpu.VMEM((FEATS, WIDTH), F32),
            pltpu.VMEM((2, WIDTH), F32),
            pltpu.VMEM((YS * CS, XS, 2, WIDTH), F32),
            pltpu.VMEM((2, YS * CS, WIDTH), F32),
            pltpu.VMEM((ZS, 2, YS * CS, WIDTH), F32),
            pltpu.VMEM((BLOCKS, WIDTH), F32),
            pltpu.VMEM((GROUP * FEATS, WIDTH), F32),
            pltpu.VMEM((GROUP, FEATS, WIDTH), BF16),
            pltpu.VMEM((GROUP, FEATS, 3 * WIDTH), BF16),
            pltpu.VMEM((GROUP, FEATS, WIDTH), BF16),
            pltpu.VMEM((GROUP * FEATS, WIDTH), F32),
            pltpu.VMEM((FEATS, GROUP, WIDTH), BF16),
            pltpu.VMEM((FEATS * 8, WIDTH), F32),
            pltpu.VMEM((FEATS, 8, WIDTH), BF16),
            pltpu.VMEM((OWNERS, OWNED, 8, WIDTH), BF16),
            dma((2,)),
            dma((XS,)), dma((XS,)), dma((OWNERS * CS,)), dma((OWNERS * CS,)),
            dma((8,)), dma((8,)),
            dma((OWNERS,)), dma((OWNERS,)), dma((4 * OWNERS,)), dma((4 * OWNERS,)),
            dma((4,)), dma((4,)), dma((4,)), dma((4,)),
            dma((8,)), dma((8,)),
        ],
        compiler_params=pltpu.CompilerParams(
            collective_id=0, has_side_effects=True, vmem_limit_bytes=MIX_VMEM
        ),
    )(*stay(by_feature, block_table, live, row_train, feat_qkv, feat_out, item_qkv))
    listed = list_call(query, key, block_table, train)
    return pl.pallas_call(
        back_kernel,
        name="back",
        out_shape=jax.ShapeDtypeStruct((GROUP, FEATS, WIDTH), BF16),
        in_specs=[VMEM] * 7 + [HBM],
        out_specs=VMEM,
        scratch_shapes=[
            pltpu.VMEM((WIDTH, WIDTH), BF16),
            pltpu.VMEM((OWNERS, OWNED, GROUP, WIDTH), BF16),
            pltpu.VMEM((OWNERS, OWNED, GROUP, WIDTH), BF16),
            pltpu.VMEM((GROUP * FEATS, WIDTH), F32),
            dma((OWNERS,)), dma((OWNERS,)), dma((1,)),
        ],
        compiler_params=pltpu.CompilerParams(
            collective_id=1, has_side_effects=True, vmem_limit_bytes=BACK_VMEM
        ),
    )(mixed, query, *listed, *stay(item_out))


def solution(mesh):
    return jax.shard_map(
        on_device,
        mesh=mesh,
        in_specs=(P("rows", "feat", None), P(), P(), P(), P(), P(), P(), P()),
        out_specs=P(("rows", "feat"), None, None),
        check_vma=False,
    )
```
